32 devices in a mesh: freq: 4 (over z), tm: 4 (over y, x), grp: 2 (over core).
Axes of the slice: x: 2, y: 2, z: 4, core: 2. Of those that a mesh axis runs over, the one named last changes fastest.
Arguments:
- inputs: bfloat16 [10, 1280, 768], P('grp', ('freq', 'tm')), may hold values from -6 to 6
- gain_one: float32 [768], replicated, may hold values from 0.5 to 1.5
- shift_one: float32 [768], replicated, may hold values from -1.8 to 1.8
- w_qkv: bfloat16 [768, 2304], replicated, may hold values from -0.21875 to 0.21875
- bias_query: float32 [768], replicated, may hold values from -1.8 to 1.8
- bias_value: float32 [768], replicated, may hold values from -0.18 to 0.18
- w_out: bfloat16 [768, 768], replicated, may hold values from -4 to 4
- bias_out: float32 [768], replicated, may hold values from -0.6 to 0.6
- gain_two: float32 [768], replicated, may hold values from 0.5 to 1.5
- shift_two: float32 [768], replicated, may hold values from -1.8 to 1.8
- w_up: bfloat16 [768, 3072], replicated, may hold values from -0.21875 to 0.21875
- bias_up: float32 [3072], replicated, may hold values from -1.8 to 1.8
- w_down: bfloat16 [3072, 768], replicated, may hold values from -0.109375 to 0.109375
- bias_down: float32 [768], replicated, may hold values from -0.6 to 0.6
- cotangent: bfloat16 [10, 1280, 768], P('grp', ('freq', 'tm')), may hold values from -6 to 6
Outputs:
- block_out: float32 [10, 1280, 768], P('grp', ('freq', 'tm'))
- grad_inputs: float32 [10, 1280, 768], P('grp', ('freq', 'tm'))
- grad_gain_one: float32 [768], P(('freq', 'tm', 'grp'))
- grad_shift_one: float32 [768], P(('freq', 'tm', 'grp'))
- grad_w_qkv: float32 [768, 2304], P(('freq', 'tm', 'grp'))
- grad_bias_query: float32 [768], P(('freq', 'tm', 'grp'))
- grad_bias_value: float32 [768], P(('freq', 'tm', 'grp'))
- grad_w_out: float32 [768, 768], P(('freq', 'tm', 'grp'))
- grad_bias_out: float32 [768], P(('freq', 'tm', 'grp'))
- grad_gain_two: float32 [768], P(('freq', 'tm', 'grp'))
- grad_shift_two: float32 [768], P(('freq', 'tm', 'grp'))
- grad_w_up: float32 [768, 3072], P(('freq', 'tm', 'grp'))
- grad_bias_up: float32 [3072], P(('freq', 'tm', 'grp'))
- grad_w_down: float32 [3072, 768], P(('freq', 'tm', 'grp'))
- grad_bias_down: float32 [768], P(('freq', 'tm', 'grp'))
The draws below stay inside these ranges and needn't reach their ends.
All inputs are finite; a program needn't handle non-finite values.
Results may differ from the reference program's by a relative error of at most 0.019.
Values may be sent and summed in bfloat16 or wider, within the bound.
No kernel may reach another device: no remote copies, remote signals or barrier semaphores. Data moves between devices by JAX's collectives and lax.ppermute only.
A program may use at most 256 MiB of HBM per device.

```python
import jax
import jax.numpy as jnp
from jax import lax

D = 768
HD = 64
FF = 3072
SEQ = 1280
NCLIP = 10


def raised(result, rng, source, target, shards_of, factor):
    owner, partner = [(jnp.arange(result.shape[position]) // (result.shape[position] // shards_of)).reshape([-1 if axis == position else 1 for axis in range(result.ndim)]) for position in (source, target)]
    chosen = jax.random.permutation(rng, shards_of)[partner]
    strong = (owner == chosen) | (owner == (partner + shards_of // 2) % shards_of)
    return jnp.where(strong, factor * result, result)


def steps_of(rng, dims, split, smallest, largest):
    def one(axis_at, shards_of):
        heights = jax.random.uniform(jax.random.fold_in(jax.random.fold_in(rng, 6), axis_at), (shards_of,), jnp.float32, smallest / len(split), largest / len(split))
        return jnp.repeat(jnp.exp(heights), dims[axis_at] // shards_of).reshape((-1,) + (1,) * (len(dims) - axis_at - 1))

    factor_of = one(*split[0])
    for cut in split[1:]:
        factor_of = factor_of * one(*cut)
    return factor_of


def normal_values(key, shape, deviation, limit, pieces=(), dtype=jnp.bfloat16):
    array = deviation * jax.random.normal(key, shape, jnp.float32)
    if pieces:
        array = array * steps_of(key, shape, pieces, -0.22, 0.18)
    return jnp.clip(array, -limit, limit).astype(dtype)


def gaussian_with(stream_key, shape, spread, bound, pieces, heavy, kind=jnp.bfloat16):
    entries = spread * jax.random.normal(stream_key, shape, jnp.float32)
    if pieces:
        entries = entries * steps_of(stream_key, shape, pieces, -0.22, 0.18)
    return jnp.clip(raised(entries, jax.random.fold_in(stream_key, 3), *heavy), -bound, bound).astype(kind)


def setup_inputs(seed: int = 0) -> dict:
    arg_keys = jax.random.split(jax.random.key(seed), 16)
    return {
        "inputs": normal_values(arg_keys[0], (NCLIP, SEQ, D), 1.0, 6.0, ((0, 2), (1, 16))),
        "gain_one": jnp.clip(1.0 + 0.1 * jax.random.normal(arg_keys[1], (D,), jnp.float32), 0.5, 1.5),
        "shift_one": normal_values(arg_keys[2], (D,), 0.3, 1.8, (), jnp.float32),
        "w_qkv": normal_values(arg_keys[3], (D, 3 * D), D ** -0.5, 0.21875),
        "bias_query": normal_values(arg_keys[4], (D,), 0.3, 1.8, (), jnp.float32),
        "bias_value": normal_values(arg_keys[5], (D,), 0.03, 0.18, (), jnp.float32),
        "w_out": normal_values(arg_keys[6], (D, D), 2 ** -0.5, 4.0),
        "bias_out": normal_values(arg_keys[7], (D,), 0.1, 0.6, (), jnp.float32),
        "gain_two": jnp.clip(1.0 + 0.1 * jax.random.normal(arg_keys[8], (D,), jnp.float32), 0.5, 1.5),
        "shift_two": normal_values(arg_keys[9], (D,), 0.3, 1.8, (), jnp.float32),
        "w_up": normal_values(arg_keys[10], (D, FF), D ** -0.5, 0.21875),
        "bias_up": normal_values(arg_keys[11], (FF,), 0.3, 1.8, (), jnp.float32),
        "w_down": normal_values(arg_keys[12], (FF, D), FF ** -0.5, 0.109375),
        "bias_down": normal_values(arg_keys[13], (D,), 0.1, 0.6, (), jnp.float32),
        "cotangent": gaussian_with(arg_keys[14], (NCLIP, SEQ, D), 1.0, 6.0, ((0, 2), (1, 16)), (0, 2, 2, 2.0)),
    }


@jax.custom_vjp
def low(v):
    return lax.optimization_barrier(v.astype(jnp.bfloat16)).astype(jnp.float32)

@jax.custom_vjp
def low_back(v):
    return v

def low_keep(v):
    return (low(v), None)

def low_pass(kept, grad):
    return (grad,)

def back_keep(v):
    return (v, None)

def back_low(kept, grad):
    return (low(grad),)
low.defvjp(low_keep, low_pass)
low_back.defvjp(back_keep, back_low)
NORM_EPS = 1e-06
PRECISE = lax.Precision.HIGHEST

def layer_norm(tensor, gain_vec, shift_vec):
    row_mean = lax.optimization_barrier(jnp.mean(tensor, axis=-1, keepdims=True))
    centered = tensor - row_mean
    variance = lax.optimization_barrier(jnp.mean(centered * centered, axis=-1, keepdims=True))
    return centered * lax.rsqrt(variance + NORM_EPS) * gain_vec + shift_vec

def one_clip(tokens, weights):
    gain_one, shift_one, w_qkv, bias_query, bias_value, w_out, bias_out, gain_two, shift_two, w_up, bias_up, w_down, bias_down = weights
    seq_len = tokens.shape[0]
    model_width = tokens.shape[1]
    head_count = model_width // HD
    normed_one = low(layer_norm(tokens, gain_one, shift_one))
    projected = jnp.dot(normed_one, w_qkv, precision=PRECISE)
    queries = low_back(low(projected[:, :model_width] + bias_query))
    keys_all = low_back(low(projected[:, model_width:2 * model_width]))
    values_all = low_back(low(projected[:, 2 * model_width:] + bias_value))
    scores = jnp.einsum('qhe,khe->hqk', queries.reshape(seq_len, head_count, HD), keys_all.reshape(seq_len, head_count, HD), precision=PRECISE) * HD ** (-0.5)
    scores = low_back(scores)
    probs = jnp.exp(scores - jax.nn.logsumexp(scores, axis=-1, keepdims=True))
    attended = jnp.einsum('hqk,khe->qhe', low(probs), values_all.reshape(seq_len, head_count, HD), precision=PRECISE).reshape(seq_len, model_width)
    attended = low_back(low(attended))
    resid_mid = tokens + low_back(jnp.dot(attended, w_out, precision=PRECISE) + bias_out)
    normed_two = low(layer_norm(resid_mid, gain_two, shift_two))
    hidden_pre = low_back(jnp.dot(normed_two, w_up, precision=PRECISE) + bias_up)
    activated = low(jax.nn.gelu(hidden_pre, approximate=False))
    return resid_mid + low_back(jnp.dot(activated, w_down, precision=PRECISE) + bias_down)

def reference(inputs, gain_one, shift_one, w_qkv, bias_query, bias_value, w_out, bias_out, gain_two, shift_two, w_up, bias_up, w_down, bias_down, cotangent):
    weights = tuple((tensor.astype(jnp.float32) for tensor in (gain_one, shift_one, w_qkv, bias_query, bias_value, w_out, bias_out, gain_two, shift_two, w_up, bias_up, w_down, bias_down)))
    clip_step = jax.checkpoint(one_clip)

    def forward(tokens_all, params):
        return lax.map(lambda tokens: clip_step(tokens, params), tokens_all)
    block_out, pull_back = jax.vjp(forward, inputs.astype(jnp.float32), weights)
    grad_inputs, grads = pull_back(cotangent.astype(jnp.float32))
    return (block_out, grad_inputs, grads[0], grads[1], grads[2], grads[3], grads[4], grads[5], grads[6], grads[7], grads[8], grads[9], grads[10], grads[11], grads[12])
```

```python
import functools

import jax
import jax.numpy as jnp
from jax import lax
from jax.experimental import pallas as pl
from jax.experimental.pallas import tpu as pltpu
from jax.sharding import PartitionSpec as P

HD = 64
NORM_EPS = 1e-06
BF = jnp.bfloat16
F32 = jnp.float32
ALL = ("freq", "tm", "grp")
VMEM_LIMIT = 60 * 1024 * 1024


def nn(a, b):
    return lax.dot_general(a, b, (((1,), (0,)), ((), ())), preferred_element_type=F32)


def nt_dot(a, b):
    return lax.dot_general(a, b, (((1,), (1,)), ((), ())), preferred_element_type=F32)


def tn_dot(a, b):
    return lax.dot_general(a, b, (((0,), (0,)), ((), ())), preferred_element_type=F32)


def normalize(x):
    mean = jnp.mean(x, axis=-1, keepdims=True)
    centered = x - mean
    var = jnp.mean(centered * centered, axis=-1, keepdims=True)
    rstd = lax.rsqrt(var + NORM_EPS)
    return centered * rstd, rstd


def norm_back(e, n, rstd, gain):
    eg = e * gain
    return rstd * (
        eg - jnp.mean(eg, axis=-1, keepdims=True) - n * jnp.mean(eg * n, axis=-1, keepdims=True)
    )


def colsum(x):
    return jnp.sum(x, axis=0, keepdims=True)


def low_lanes(rows):
    return lax.broadcasted_iota(jnp.int32, (rows, 2 * HD), 1) < HD


def swap_halves(x):
    return pltpu.roll(x, HD, 1)


def slot_of(head, nf, nt):
    per = -(-(12) // nf)
    return (head // per) * nt + head % per


def params(count=1):
    return pltpu.CompilerParams(
        dimension_semantics=("arbitrary",) * count, vmem_limit_bytes=VMEM_LIMIT
    )


def full(shape):
    return pl.BlockSpec(shape, lambda *_: (0,) * len(shape))


def cost(flops, nbytes):
    return pl.CostEstimate(flops=int(flops), bytes_accessed=int(nbytes), transcendentals=0)


def ln_kernel(x_ref, g_ref, s_ref, n_ref):
    n, _ = normalize(x_ref[...].astype(F32))
    n_ref[...] = (n * g_ref[...] + s_ref[...]).astype(BF)


def ln_call(x, gain, shift):
    return pl.pallas_call(
        ln_kernel,
        out_shape=jax.ShapeDtypeStruct(x.shape, BF),
        compiler_params=pltpu.CompilerParams(vmem_limit_bytes=VMEM_LIMIT),
        cost_estimate=cost(x.size * 10, x.size * 4),
        name="ln_one",
    )(x, gain, shift)


def q5_kernel(nf, nt, x_ref, g_ref, s_ref, w_ref, bq_ref, bv_ref, n_ref, pack_ref):
    rows, width = x_ref.shape
    half = rows // 2
    hat, _ = normalize(x_ref[...].astype(F32))
    n = (hat * g_ref[...] + s_ref[...]).astype(BF)
    n_ref[...] = n
    low = low_lanes(half)
    pack_ref[...] = jnp.zeros_like(pack_ref)
    for part in range(3):
        proj = nn(n, w_ref[:, part * width : (part + 1) * width])
        if part == 0:
            proj = (proj + bq_ref[...]) * (HD**-0.5)
        if part == 2:
            proj = proj + bv_ref[...]
        for pair in range(width // (2 * HD)):
            blk = proj[:, pair * 2 * HD : (pair + 1) * 2 * HD]
            top, bot = blk[:half], blk[half:]
            even = jnp.where(low, top, swap_halves(bot))
            odd = jnp.where(low, swap_halves(top), bot)
            lanes = slice(part * 2 * HD, (part + 1) * 2 * HD)
            pack_ref[slot_of(2 * pair, nf, nt), :, lanes] = even.astype(BF)
            pack_ref[slot_of(2 * pair + 1, nf, nt), :, lanes] = odd.astype(BF)


def q5_call(nf, nt, x, gain, shift, w, bq, bv):
    rows, width = x.shape
    return pl.pallas_call(
        functools.partial(q5_kernel, nf, nt),
        out_shape=(
            jax.ShapeDtypeStruct((rows, width), BF),
            jax.ShapeDtypeStruct((nf * nt, rows // 2, 6 * HD), BF),
        ),
        compiler_params=pltpu.CompilerParams(vmem_limit_bytes=VMEM_LIMIT),
        cost_estimate=cost(2 * rows * w.size, w.size * 2),
        name="q_shared",
    )(x, gain, shift, w, bq, bv)


def spread(x):
    rows = x.shape[0]
    low = low_lanes(rows)
    zero = jnp.zeros_like(x)
    return jnp.concatenate([jnp.where(low, x, zero), jnp.where(low, swap_halves(x), zero)], axis=0)


def unspread(x):
    half = x.shape[0] // 2
    return x[:half] + swap_halves(x[half:])


def softmax_block(q, k, v):
    s = nt_dot(q, k)
    m = jnp.max(s, axis=-1, keepdims=True)
    e = jnp.exp(s - m)
    total = jnp.sum(e, axis=-1, keepdims=True)
    e = e.astype(BF)
    rinv = 1.0 / total
    return e, nn(e, v) * rinv, rinv


def attn5_fwd_kernel(steps, x_ref, o_ref, r_ref, ob_ref, e_ref, qf, kf, vf, of, rf):
    for part, dst in enumerate((qf, kf, vf)):
        blk = x_ref[:, part * 2 * HD : (part + 1) * 2 * HD].astype(F32)
        dst[...] = spread(blk).astype(BF)
    rows = qf.shape[0] // steps
    low = low_lanes(rows)

    def body(i, carry):
        at = pl.ds(pl.multiple_of(i * rows, rows), rows)
        e, o, rinv = softmax_block(qf[at, :], kf[...], vf[...])
        e_ref[at, :] = e
        of[at, :] = o
        rf[at, :] = jnp.where(low, jnp.broadcast_to(rinv, (rows, 2 * HD)), 0.0)
        return carry

    lax.fori_loop(0, steps, body, 0)
    packed = unspread(of[...])
    o_ref[...] = packed
    ob_ref[...] = packed.astype(BF)
    r_ref[...] = unspread(rf[...])


def attn5_fwd_call(x):
    rows = x.shape[0]
    toks = 2 * rows
    return pl.pallas_call(
        functools.partial(attn5_fwd_kernel, 4),
        out_shape=(
            jax.ShapeDtypeStruct((rows, 2 * HD), F32),
            jax.ShapeDtypeStruct((rows, 2 * HD), F32),
            jax.ShapeDtypeStruct((rows, 2 * HD), BF),
            jax.ShapeDtypeStruct((toks, toks), BF),
        ),
        scratch_shapes=[pltpu.VMEM((toks, 2 * HD), BF)] * 3 + [pltpu.VMEM((toks, 2 * HD), F32)] * 2,
        compiler_params=pltpu.CompilerParams(vmem_limit_bytes=VMEM_LIMIT),
        cost_estimate=cost(4 * 4 * toks * toks * 2 * HD, toks * toks * 2),
        name="attn_shared_fwd",
    )(x)


def attn5_bwd_kernel(
    steps, x_ref, ga_ref, o_ref, r_ref, e_ref, out_ref, qf, kf, vf, gf, inn, dq, dk, dv
):
    for part, dst in enumerate((qf, kf, vf)):
        blk = x_ref[:, part * 2 * HD : (part + 1) * 2 * HD].astype(F32)
        dst[...] = spread(blk).astype(BF)
    g = ga_ref[...].astype(F32) * r_ref[...]
    gs = spread(g)
    gf[...] = gs.astype(BF)
    inn[...] = jnp.sum(gs * spread(o_ref[...]), axis=-1, keepdims=True)
    rows = qf.shape[0] // steps
    dk[...] = jnp.zeros_like(dk)
    dv[...] = jnp.zeros_like(dv)

    def body(i, carry):
        at = pl.ds(pl.multiple_of(i * rows, rows), rows)
        e = e_ref[at, :]
        gb = gf[at, :]
        dp = nt_dot(gb, vf[...])
        ds = (e.astype(F32) * (dp - inn[at, :])).astype(BF)
        dq[at, :] = nn(ds, kf[...]) * (HD**-0.5)
        dk[...] += tn_dot(ds, qf[at, :])
        dv[...] += tn_dot(e, gb)
        return carry

    lax.fori_loop(0, steps, body, 0)
    for part, src in enumerate((dq, dk, dv)):
        out_ref[:, part * 2 * HD : (part + 1) * 2 * HD] = unspread(src[...]).astype(BF)


def attn5_bwd_call(x, ga, o, r, e):
    rows = x.shape[0]
    toks = 2 * rows
    return pl.pallas_call(
        functools.partial(attn5_bwd_kernel, 4),
        out_shape=jax.ShapeDtypeStruct((rows, 6 * HD), BF),
        scratch_shapes=[pltpu.VMEM((toks, 2 * HD), BF)] * 4
        + [pltpu.VMEM((toks, 1), F32)]
        + [pltpu.VMEM((toks, 2 * HD), F32)] * 3,
        compiler_params=pltpu.CompilerParams(vmem_limit_bytes=VMEM_LIMIT),
        cost_estimate=cost(8 * 4 * toks * toks * 2 * HD, toks * toks * 2),
        name="attn_shared_bwd",
    )(x, ga, o, r, e)


def attn_fwd_kernel(nt, *refs):
    ns = refs[:nt]
    wq, wk, wv, bq, bv = refs[nt : nt + 5]
    att_ref, o_ref, r_ref, q_ref, k_ref, v_ref, e_ref = refs[nt + 5 :]
    rows = ns[0].shape[0]
    for c in range(nt):
        at = slice(c * rows, (c + 1) * rows)
        x = ns[c][...]
        k_ref[at, :] = nn(x, wk[...]).astype(BF)
        v_ref[at, :] = (nn(x, wv[...]) + bv[...]).astype(BF)
    q_ref[...] = ((nn(ns[0][...], wq[...]) + bq[...]) * (HD**-0.5)).astype(BF)
    low = low_lanes(rows)
    for pair in range(q_ref.shape[1] // (2 * HD)):
        lanes = slice(pair * 2 * HD, (pair + 1) * 2 * HD)
        q, k, v = q_ref[:, lanes], k_ref[:, lanes], v_ref[:, lanes]
        zero = jnp.zeros_like(q)
        e0, o0, r0 = softmax_block(jnp.where(low, q, zero), k, v)
        e_ref[2 * pair] = e0
        e1, o1, r1 = softmax_block(jnp.where(low, zero, q), k, v)
        e_ref[2 * pair + 1] = e1
        o = jnp.where(low, o0, o1)
        o_ref[:, lanes] = o
        att_ref[:, lanes] = o.astype(BF)
        r_ref[:, lanes] = jnp.where(
            low, jnp.broadcast_to(r0, (rows, 2 * HD)), jnp.broadcast_to(r1, (rows, 2 * HD))
        )


def attn_fwd_call(ns, w, bq, bv):
    nt = len(ns)
    rows, width = ns[0].shape
    toks = nt * rows
    blk = 4 * HD
    steps = width // blk
    wspec = [pl.BlockSpec((width, blk), lambda j, p=p: (0, p * steps + j)) for p in range(3)]
    bspec = pl.BlockSpec((1, blk), lambda j: (0, j))
    row = lambda n: pl.BlockSpec((n, blk), lambda j: (0, j))
    return pl.pallas_call(
        functools.partial(attn_fwd_kernel, nt),
        grid=(steps,),
        in_specs=[full((rows, width))] * nt + wspec + [bspec, bspec],
        out_specs=[row(rows)] * 4
        + [row(toks)] * 2
        + [pl.BlockSpec((4, rows, toks), lambda j: (j, 0, 0))],
        out_shape=(
            jax.ShapeDtypeStruct((rows, width), BF),
            jax.ShapeDtypeStruct((rows, width), F32),
            jax.ShapeDtypeStruct((rows, width), F32),
            jax.ShapeDtypeStruct((rows, width), BF),
            jax.ShapeDtypeStruct((toks, width), BF),
            jax.ShapeDtypeStruct((toks, width), BF),
            jax.ShapeDtypeStruct((width // HD, rows, toks), BF),
        ),
        compiler_params=params(),
        cost_estimate=cost(4 * toks * width * width + 16 * rows * toks * width, 20 << 20),
        name="attn_fwd",
    )(*ns, w, w, w, bq, bv)


def attn_bwd_kernel(nt, *refs):
    ns = refs[:nt]
    wq, wk, wv, ga_ref, q_ref, k_ref, v_ref, o_ref, r_ref, e_ref = refs[nt : nt + 10]
    dw_ref, gbq_ref, gbv_ref = refs[nt + 10 : nt + 13]
    dxs = refs[nt + 13 : nt + 13 + nt]
    gq, gk, gv, dx = refs[nt + 13 + nt :]
    step = pl.program_id(0)
    rows = ns[0].shape[0]
    low = low_lanes(rows)
    for pair in range(q_ref.shape[1] // (2 * HD)):
        lanes = slice(pair * 2 * HD, (pair + 1) * 2 * HD)
        q, k, v = q_ref[:, lanes], k_ref[:, lanes], v_ref[:, lanes]
        g = ga_ref[:, lanes].astype(F32) * r_ref[:, lanes]
        go = g * o_ref[:, lanes]
        g = g.astype(BF)
        zero = jnp.zeros_like(q)
        halves = []
        for side in range(2):
            mine = low if side == 0 else jnp.logical_not(low)
            qh = jnp.where(mine, q, zero)
            gh = jnp.where(mine, g, zero)
            inner = jnp.sum(jnp.where(mine, go, 0.0), axis=-1, keepdims=True)
            e = e_ref[2 * pair + side]
            dp = nt_dot(gh, v)
            ds = (e.astype(F32) * (dp - inner)).astype(BF)
            halves.append((nn(ds, k), tn_dot(ds, qh), tn_dot(e, gh)))
        gq[:, lanes] = (jnp.where(low, halves[0][0], halves[1][0]) * (HD**-0.5)).astype(BF)
        gk[:, lanes] = (halves[0][1] + halves[1][1]).astype(BF)
        gv[:, lanes] = (halves[0][2] + halves[1][2]).astype(BF)

    @pl.when(step == 0)
    def _():
        dx[...] = jnp.zeros_like(dx)

    gbq_ref[...] = colsum(gq[...].astype(F32))
    gbv_ref[...] = colsum(gv[...].astype(F32))
    dw_ref[0] = tn_dot(ns[0][...], gq[...]).astype(BF)
    dx[0:rows, :] += nt_dot(gq[...], wq[...])
    dwk = jnp.zeros(dw_ref.shape[1:], F32)
    dwv = jnp.zeros(dw_ref.shape[1:], F32)
    for c in range(nt):
        at = slice(c * rows, (c + 1) * rows)
        dx[at, :] += nt_dot(gk[at, :], wk[...]) + nt_dot(gv[at, :], wv[...])
        dwk += tn_dot(ns[c][...], gk[at, :])
        dwv += tn_dot(ns[c][...], gv[at, :])
    dw_ref[1] = dwk.astype(BF)
    dw_ref[2] = dwv.astype(BF)

    @pl.when(step == pl.num_programs(0) - 1)
    def _():
        for c in range(nt):
            dxs[c][...] = dx[c * rows : (c + 1) * rows, :].astype(dxs[c].dtype)


def attn_bwd_call(ns, w, ga, q, k, v, o, r, e):
    nt = len(ns)
    rows, width = ns[0].shape
    toks = nt * rows
    blk = 4 * HD
    steps = width // blk
    wspec = [pl.BlockSpec((width, blk), lambda j, p=p: (0, p * steps + j)) for p in range(3)]
    row = lambda n: pl.BlockSpec((n, blk), lambda j: (0, j))
    return pl.pallas_call(
        functools.partial(attn_bwd_kernel, nt),
        grid=(steps,),
        in_specs=[full((rows, width))] * nt
        + wspec
        + [row(rows), row(rows), row(toks), row(toks), row(rows), row(rows)]
        + [pl.BlockSpec((4, rows, toks), lambda j: (j, 0, 0))],
        out_specs=[pl.BlockSpec((3, width, blk), lambda j: (0, 0, j)), row(1), row(1)]
        + [full((rows, width))] * nt,
        out_shape=[
            jax.ShapeDtypeStruct((3, width, width), BF),
            jax.ShapeDtypeStruct((1, width), F32),
            jax.ShapeDtypeStruct((1, width), F32),
            jax.ShapeDtypeStruct((rows, width), F32),
        ]
        + [jax.ShapeDtypeStruct((rows, width), BF)] * (nt - 1),
        scratch_shapes=[
            pltpu.VMEM((rows, blk), BF),
            pltpu.VMEM((toks, blk), BF),
            pltpu.VMEM((toks, blk), BF),
            pltpu.VMEM((toks, width), F32),
        ],
        compiler_params=params(),
        cost_estimate=cost(8 * toks * width * width + 32 * rows * toks * width, 24 << 20),
        name="attn_bwd",
    )(*ns, w, w, w, ga, q, k, v, o, r, e)


def mid_kernel(nf, nt, *refs):
    (
        att_ref,
        att5_ref,
        xm_ref,
        x5_ref,
        cm_ref,
        c5_ref,
        wo_ref,
        bo_ref,
        g2_ref,
        s2_ref,
        bd_ref,
        wu_ref,
        bu_ref,
        wd_ref,
        out_ref,
        out5_ref,
        gm_ref,
        ga_ref,
        ga5_ref,
        dwo_ref,
        dwu_ref,
        dwd_ref,
        vec_ref,
        gbu_ref,
        att,
        cot,
        mid,
        hat,
        rst,
        two,
        acc,
        gn2,
    ) = refs
    step = pl.program_id(0)
    rm = xm_ref.shape[0]
    r5, width = x5_ref.shape
    half = r5 // 2
    low = low_lanes(half)
    pairs = width // (2 * HD)

    @pl.when(step == 0)
    def _():
        att[0:rm, :] = att_ref[...]
        for pair in range(pairs):
            lanes = slice(pair * 2 * HD, (pair + 1) * 2 * HD)
            even = att5_ref[slot_of(2 * pair, nf, nt)].astype(F32)
            odd = att5_ref[slot_of(2 * pair + 1, nf, nt)].astype(F32)
            top = jnp.where(low, even, swap_halves(odd))
            bot = jnp.where(low, swap_halves(even), odd)
            att[rm : rm + r5, lanes] = jnp.concatenate([top, bot], axis=0).astype(BF)
        cot[0:rm, :] = cm_ref[...]
        cot[rm : rm + r5, :] = c5_ref[...]
        mid[...] = nn(att[...], wo_ref[...]) + bo_ref[...]
        mid[0:rm, :] += xm_ref[...].astype(F32)
        mid[rm : rm + r5, :] += x5_ref[...].astype(F32)
        n, rstd = normalize(mid[...])
        hat[...] = n
        rst[...] = rstd
        two[...] = (n * g2_ref[...] + s2_ref[...]).astype(BF)
        acc[...] = mid[...] + bd_ref[...]
        gn2[...] = jnp.zeros_like(gn2)

    pre = nn(two[...], wu_ref[...]) + bu_ref[...]
    cdf = 0.5 * (1.0 + lax.erf(pre * (0.5**0.5)))
    slope = cdf + pre * (jnp.exp(-0.5 * pre * pre) * 0.3989422804014327)
    act = (pre * cdf).astype(BF)
    acc[...] += nn(act, wd_ref[...])
    dwd_ref[...] = tn_dot(act, cot[...]).astype(BF)
    gpre = (nt_dot(cot[...], wd_ref[...]) * slope).astype(BF)
    gbu_ref[...] = colsum(gpre.astype(F32))
    dwu_ref[...] = tn_dot(two[...], gpre).astype(BF)
    gn2[...] += nt_dot(gpre, wu_ref[...])

    @pl.when(step == pl.num_programs(0) - 1)
    def _():
        out_ref[...] = acc[0:rm, :].astype(BF)
        out5_ref[...] = acc[rm : rm + r5, :]
        e = gn2[...]
        n = hat[...]
        c = cot[...].astype(F32)
        gmid = c + norm_back(e, n, rst[...], g2_ref[...])
        gm_ref[...] = gmid
        branch = gmid.astype(BF)
        vec_ref[0:1, :] = colsum(branch.astype(F32))
        vec_ref[1:2, :] = colsum(e * n)
        vec_ref[2:3, :] = colsum(e)
        vec_ref[3:4, :] = colsum(c)
        dwo_ref[...] = tn_dot(att[...], branch).astype(BF)
        gatt = nt_dot(branch, wo_ref[...])
        ga_ref[...] = gatt[0:rm].astype(BF)
        ga5_ref[...] = jnp.zeros_like(ga5_ref)
        for pair in range(pairs):
            lanes = slice(pair * 2 * HD, (pair + 1) * 2 * HD)
            top, bot = gatt[rm : rm + half, lanes], gatt[rm + half : rm + r5, lanes]
            even = jnp.where(low, top, swap_halves(bot))
            odd = jnp.where(low, swap_halves(top), bot)
            ga5_ref[slot_of(2 * pair, nf, nt)] = even.astype(BF)
            ga5_ref[slot_of(2 * pair + 1, nf, nt)] = odd.astype(BF)


def mid_call(nf, nt, att, att5, xm, x5, cm, c5, wo, bo, g2, s2, bd, wu, bu, wd):
    rm, width = xm.shape
    r5 = x5.shape[0]
    rows = rm + r5
    ff = wu.shape[1]
    blk = 768
    vec = full((1, width))
    return pl.pallas_call(
        functools.partial(mid_kernel, nf, nt),
        grid=(ff // blk,),
        in_specs=[
            full(att.shape),
            full(att5.shape),
            full(xm.shape),
            full(x5.shape),
            full(cm.shape),
            full(c5.shape),
            full(wo.shape),
            vec,
            vec,
            vec,
            vec,
            pl.BlockSpec((width, blk), lambda j: (0, j)),
            pl.BlockSpec((1, blk), lambda j: (0, j)),
            pl.BlockSpec((blk, width), lambda j: (j, 0)),
        ],
        out_specs=[
            full((rm, width)),
            full((r5, width)),
            full((rows, width)),
            full((rm, width)),
            full(att5.shape),
            full((width, width)),
            pl.BlockSpec((width, blk), lambda j: (0, j)),
            pl.BlockSpec((blk, width), lambda j: (j, 0)),
            full((4, width)),
            pl.BlockSpec((1, blk), lambda j: (0, j)),
        ],
        out_shape=[
            jax.ShapeDtypeStruct((rm, width), BF),
            jax.ShapeDtypeStruct((r5, width), F32),
            jax.ShapeDtypeStruct((rows, width), F32),
            jax.ShapeDtypeStruct((rm, width), BF),
            jax.ShapeDtypeStruct(att5.shape, BF),
            jax.ShapeDtypeStruct((width, width), BF),
            jax.ShapeDtypeStruct((width, ff), BF),
            jax.ShapeDtypeStruct((ff, width), BF),
            jax.ShapeDtypeStruct((4, width), F32),
            jax.ShapeDtypeStruct((1, ff), F32),
        ],
        scratch_shapes=[
            pltpu.VMEM((rows, width), BF),
            pltpu.VMEM((rows, width), BF),
            pltpu.VMEM((rows, width), F32),
            pltpu.VMEM((rows, width), F32),
            pltpu.VMEM((rows, 1), F32),
            pltpu.VMEM((rows, width), BF),
            pltpu.VMEM((rows, width), F32),
            pltpu.VMEM((rows, width), F32),
        ],
        compiler_params=params(),
        cost_estimate=cost(12 * rows * width * ff + 6 * rows * width * width, 24 << 20),
        name="mid",
    )(att, att5, xm, x5, cm, c5, wo, bo, g2, s2, bd, wu, bu, wd)


def tail5_kernel(nf, nt, *refs):
    (g_ref, n5_ref, x5_ref, gm_ref, w_ref, dw_ref, g1_ref, dwo_ref, gb_ref, gin_ref, vec_ref, g5, dx) = refs
    step = pl.program_id(0)
    r5, width = x5_ref.shape
    half = r5 // 2
    low = low_lanes(half)
    for pair in range(width // (2 * HD)):
        lanes = slice(pair * 2 * HD, (pair + 1) * 2 * HD)
        even = g_ref[slot_of(2 * pair, nf, nt)].astype(F32)
        odd = g_ref[slot_of(2 * pair + 1, nf, nt)].astype(F32)
        top = jnp.where(low, even, swap_halves(odd))
        bot = jnp.where(low, swap_halves(even), odd)
        g5[:, lanes] = jnp.concatenate([top, bot], axis=0).astype(BF)
    g = g5[...]
    gb_ref[0] = colsum(g.astype(F32))
    dwo_ref[...] = (dw_ref[0].astype(F32) + tn_dot(n5_ref[...], g)).astype(BF)

    @pl.when(step == 0)
    def _():
        dx[...] = jnp.zeros_like(dx)

    dx[...] += nt_dot(g, w_ref[...])

    @pl.when(step == pl.num_programs(0) - 1)
    def _():
        n, rstd = normalize(x5_ref[...].astype(F32))
        e = dx[...]
        gin_ref[...] = gm_ref[...] + norm_back(e, n, rstd, g1_ref[...])
        vec_ref[0:1, :] = colsum(e * n)
        vec_ref[1:2, :] = colsum(e)


def tail5_call(nf, nt, g, n5, x5, gm, w, dw, g1):
    r5, width = x5.shape
    at = gm.shape[0] // r5 - 1
    return pl.pallas_call(
        functools.partial(tail5_kernel, nf, nt),
        grid=(3,),
        in_specs=[
            pl.BlockSpec((g.shape[0], r5 // 2, 2 * HD), lambda j: (0, 0, j)),
            full(n5.shape),
            full(x5.shape),
            pl.BlockSpec((r5, width), lambda j: (at, 0)),
            pl.BlockSpec((width, width), lambda j: (0, j)),
            pl.BlockSpec((1, width, width), lambda j: (j, 0, 0)),
            full((1, width)),
        ],
        out_specs=[
            pl.BlockSpec((width, width), lambda j: (0, j)),
            pl.BlockSpec((1, 1, width), lambda j: (j, 0, 0)),
            full((r5, width)),
            full((2, width)),
        ],
        out_shape=[
            jax.ShapeDtypeStruct((width, 3 * width), BF),
            jax.ShapeDtypeStruct((3, 1, width), F32),
            jax.ShapeDtypeStruct((r5, width), F32),
            jax.ShapeDtypeStruct((2, width), F32),
        ],
        scratch_shapes=[pltpu.VMEM((r5, width), BF), pltpu.VMEM((r5, width), F32)],
        compiler_params=params(),
        cost_estimate=cost(4 * r5 * width * width * 3, 12 << 20),
        name="tail_shared",
    )(g, n5, x5, gm, w, dw, g1)


def tail_kernel(nt, *refs):
    dxs = refs[:nt]
    x_ref, gm_ref, g1_ref, gin_ref, vec_ref = refs[nt:]
    e = dxs[0][...]
    for c in range(1, nt):
        e = e + dxs[c][...].astype(F32)
    n, rstd = normalize(x_ref[...].astype(F32))
    gin_ref[...] = (gm_ref[...] + norm_back(e, n, rstd, g1_ref[...])).astype(BF)
    vec_ref[0:1, :] = colsum(e * n)
    vec_ref[1:2, :] = colsum(e)


def tail_call(dxs, x, gm, g1):
    rows, width = x.shape
    nt = len(dxs)
    return pl.pallas_call(
        functools.partial(tail_kernel, nt),
        grid=(1,),
        in_specs=[full((rows, width))] * (nt + 2) + [full((1, width))],
        out_specs=[full((rows, width)), full((2, width))],
        out_shape=[
            jax.ShapeDtypeStruct((rows, width), BF),
            jax.ShapeDtypeStruct((2, width), F32),
        ],
        compiler_params=params(),
        cost_estimate=cost(30 * rows * width, 6 << 20),
        name="tail",
    )(*dxs, x, gm, g1)


def over(axes, x):
    return lax.all_to_all(x, axes, 0, 0)


def partners(nt, k):
    if nt & (nt - 1):
        return [(i, (i + k) % nt) for i in range(nt)], [(i, (i - k) % nt) for i in range(nt)]
    pairs = [(i, i ^ k) for i in range(nt)]
    return pairs, pairs


def local(
    nf,
    nt,
    ng,
    inputs,
    gain_one,
    shift_one,
    w_qkv,
    bias_query,
    bias_value,
    w_out,
    bias_out,
    gain_two,
    shift_two,
    w_up,
    bias_up,
    w_down,
    bias_down,
    cotangent,
):
    clips, r, width = inputs.shape
    ff = w_up.shape[1]
    g1, s1 = gain_one[None], shift_one[None]
    bq, bv = bias_query[None], bias_value[None]
    rm = nf * r
    x5, c5 = inputs[nf], cotangent[nf]
    xm = over("freq", inputs[:nf]).reshape(rm, width)
    n5, pack5 = q5_call(nf, nt, x5, g1, s1, w_qkv, bq, bv)
    got5 = over(("freq", "tm"), pack5).reshape(-1, 6 * HD)
    nm = ln_call(xm, g1, s1)
    ns = [nm] + [lax.ppermute(nm, "tm", partners(nt, k)[0]) for k in range(1, nt)]
    cm = over("freq", cotangent[:nf]).reshape(rm, width)
    o5, r5, ob5, e5 = attn5_fwd_call(got5)
    att5 = over(("freq", "tm"), ob5.reshape(nf * nt, r // 2, 2 * HD))
    att, o, rr, q, k, v, e = attn_fwd_call(ns, w_qkv, bq, bv)
    out_m, out5, gm, ga, ga5, dwo, dwu, dwd, vec, gbu = mid_call(
        nf,
        nt,
        att,
        att5,
        xm,
        x5,
        cm,
        c5,
        w_out,
        bias_out[None],
        gain_two[None],
        shift_two[None],
        bias_down[None],
        w_up,
        bias_up[None],
        w_down,
    )
    got_ga5 = over(("freq", "tm"), ga5).reshape(-1, 2 * HD)
    g5 = over(
        ("freq", "tm"),
        attn5_bwd_call(got5, got_ga5, o5, r5, e5).reshape(nf * nt, r // 2, 6 * HD),
    )
    dw_main, gbq, gbv, *dxs = attn_bwd_call(ns, w_qkv, ga, q, k, v, o, rr, e)
    dxs = [dxs[0]] + [lax.ppermute(dxs[k], "tm", partners(nt, k)[1]) for k in range(1, nt)]
    gin_m, vec_m = tail_call(dxs, xm, gm, g1)
    dwqkv, gb5, gin5, vec5 = tail5_call(nf, nt, g5, n5, x5, gm, w_qkv, dw_main, g1)

    block_out = over("freq", out_m.reshape(nf, r, width)).astype(F32)
    block_out = jnp.concatenate([block_out, out5[None]], axis=0)
    grad_in = over("freq", gin_m.reshape(nf, r, width)).astype(F32)
    grad_in = jnp.concatenate([grad_in, gin5[None]], axis=0)

    def scatter(x):
        return lax.psum_scatter(x, ALL, scatter_dimension=0, tiled=True).astype(F32)

    dev = nf * nt * ng
    vec1 = vec_m + vec5
    small = jnp.concatenate([vec1, vec, gbq + gb5[0], gbv + gb5[2]], axis=0)
    small = small.reshape(8, dev, width // dev).transpose(1, 0, 2).reshape(dev, -1)
    small = jnp.concatenate([small, gbu.reshape(dev, ff // dev)], axis=1)
    small = jnp.sum(over(ALL, small), axis=0)
    per = width // dev
    piece = lambda i: small[i * per : (i + 1) * per]
    return (
        block_out,
        grad_in,
        piece(0),
        piece(1),
        scatter(dwqkv),
        piece(6),
        piece(7),
        scatter(dwo),
        piece(2),
        piece(3),
        piece(4),
        scatter(dwu),
        small[8 * per :],
        scatter(dwd),
        piece(5),
    )


def solution(mesh):
    tokens = P("grp", ("freq", "tm"), None)
    vec = P(ALL)
    mat = P(ALL, None)
    return jax.shard_map(
        functools.partial(local, mesh.shape["freq"], mesh.shape["tm"], mesh.shape["grp"]),
        mesh=mesh,
        in_specs=(tokens,) + (P(),) * 13 + (tokens,),
        out_specs=(
            tokens,
            tokens,
            vec,
            vec,
            mat,
            vec,
            vec,
            mat,
            vec,
            vec,
            vec,
            mat,
            vec,
            mat,
            vec,
        ),
        check_vma=False,
    )
```

```python
import functools

import jax
import jax.numpy as jnp
from jax import lax
from jax.experimental import pallas as pl
from jax.experimental.pallas import tpu as pltpu
from jax.sharding import PartitionSpec as P

HD = 64
NORM_EPS = 1e-06
BF = jnp.bfloat16
F32 = jnp.float32
ALL = ("freq", "tm", "grp")
VMEM_LIMIT = 60 * 1024 * 1024


def nn(a, b):
    return lax.dot_general(a, b, (((1,), (0,)), ((), ())), preferred_element_type=F32)


def nt_dot(a, b):
    return lax.dot_general(a, b, (((1,), (1,)), ((), ())), preferred_element_type=F32)


def tn_dot(a, b):
    return lax.dot_general(a, b, (((0,), (0,)), ((), ())), preferred_element_type=F32)


def normalize(x):
    mean = jnp.mean(x, axis=-1, keepdims=True)
    centered = x - mean
    var = jnp.mean(centered * centered, axis=-1, keepdims=True)
    rstd = lax.rsqrt(var + NORM_EPS)
    return centered * rstd, rstd


def norm_back(e, n, rstd, gain):
    eg = e * gain
    return rstd * (
        eg - jnp.mean(eg, axis=-1, keepdims=True) - n * jnp.mean(eg * n, axis=-1, keepdims=True)
    )


def colsum(x):
    return jnp.sum(x, axis=0, keepdims=True)


def low_lanes(rows):
    return lax.broadcasted_iota(jnp.int32, (rows, 2 * HD), 1) < HD


def swap_halves(x):
    return pltpu.roll(x, HD, 1)


def slot_of(head, nf, nt):
    per = -(-(12) // nf)
    return (head // per) * nt + head % per


def params(count=1):
    return pltpu.CompilerParams(
        dimension_semantics=("arbitrary",) * count, vmem_limit_bytes=VMEM_LIMIT
    )


def full(shape):
    return pl.BlockSpec(shape, lambda *_: (0,) * len(shape))


def cost(flops, nbytes):
    return pl.CostEstimate(flops=int(flops), bytes_accessed=int(nbytes), transcendentals=0)


def pick_kernel(nf, me_ref, x_ref, c_ref, *outs):
    for k in range(nf):
        outs[k][...] = x_ref[me_ref[0] ^ k]
        outs[nf + k][...] = c_ref[me_ref[0] ^ k]


def pick_call(nf, me, x, c):
    _, rows, width = x.shape
    return pl.pallas_call(
        functools.partial(pick_kernel, nf),
        grid_spec=pltpu.PrefetchScalarGridSpec(
            num_scalar_prefetch=1,
            grid=(1,),
            in_specs=[full(x.shape)] * 2,
            out_specs=[full((rows, width))] * (2 * nf),
        ),
        out_shape=[jax.ShapeDtypeStruct((rows, width), BF)] * (2 * nf),
        compiler_params=params(),
        cost_estimate=cost(0, 4 * x.size),
        name="pick",
    )(me, x, c)


def ln_kernel(nf, *refs):
    g_ref, s_ref, n_ref = refs[nf:]
    for k in range(nf):
        rows = refs[k].shape[0]
        n, _ = normalize(refs[k][...].astype(F32))
        n_ref[k * rows : (k + 1) * rows, :] = (n * g_ref[...] + s_ref[...]).astype(BF)


def ln_call(xs, gain, shift):
    rows, width = xs[0].shape
    return pl.pallas_call(
        functools.partial(ln_kernel, len(xs)),
        out_shape=jax.ShapeDtypeStruct((len(xs) * rows, width), BF),
        compiler_params=pltpu.CompilerParams(vmem_limit_bytes=VMEM_LIMIT),
        cost_estimate=cost(len(xs) * rows * width * 10, len(xs) * rows * width * 4),
        name="ln_one",
    )(*xs, gain, shift)


def q5_kernel(nf, nt, x_ref, g_ref, s_ref, w_ref, bq_ref, bv_ref, n_ref, pack_ref):
    rows, width = x_ref.shape
    half = rows // 2
    hat, _ = normalize(x_ref[...].astype(F32))
    n = (hat * g_ref[...] + s_ref[...]).astype(BF)
    n_ref[...] = n
    low = low_lanes(half)
    pack_ref[...] = jnp.zeros_like(pack_ref)
    for part in range(3):
        proj = nn(n, w_ref[:, part * width : (part + 1) * width])
        if part == 0:
            proj = (proj + bq_ref[...]) * (HD**-0.5)
        if part == 2:
            proj = proj + bv_ref[...]
        for pair in range(width // (2 * HD)):
            blk = proj[:, pair * 2 * HD : (pair + 1) * 2 * HD]
            top, bot = blk[:half], blk[half:]
            even = jnp.where(low, top, swap_halves(bot))
            odd = jnp.where(low, swap_halves(top), bot)
            lanes = slice(part * 2 * HD, (part + 1) * 2 * HD)
            pack_ref[slot_of(2 * pair, nf, nt), :, lanes] = even.astype(BF)
            pack_ref[slot_of(2 * pair + 1, nf, nt), :, lanes] = odd.astype(BF)


def q5_call(nf, nt, x, gain, shift, w, bq, bv):
    rows, width = x.shape
    return pl.pallas_call(
        functools.partial(q5_kernel, nf, nt),
        out_shape=(
            jax.ShapeDtypeStruct((rows, width), BF),
            jax.ShapeDtypeStruct((nf * nt, rows // 2, 6 * HD), BF),
        ),
        compiler_params=pltpu.CompilerParams(vmem_limit_bytes=VMEM_LIMIT),
        cost_estimate=cost(2 * rows * w.size, w.size * 2),
        name="q_shared",
    )(x, gain, shift, w, bq, bv)


def spread(x):
    rows = x.shape[0]
    low = low_lanes(rows)
    zero = jnp.zeros_like(x)
    return jnp.concatenate([jnp.where(low, x, zero), jnp.where(low, swap_halves(x), zero)], axis=0)


def unspread(x):
    half = x.shape[0] // 2
    return x[:half] + swap_halves(x[half:])


def softmax_block(q, k, v):
    s = nt_dot(q, k)
    m = jnp.max(s, axis=-1, keepdims=True)
    e = jnp.exp(s - m)
    total = jnp.sum(e, axis=-1, keepdims=True)
    e = e.astype(BF)
    rinv = 1.0 / total
    return e, nn(e, v) * rinv, rinv


def attn5_fwd_kernel(steps, x_ref, o_ref, r_ref, ob_ref, e_ref, qf, kf, vf, of, rf):
    for part, dst in enumerate((qf, kf, vf)):
        blk = x_ref[:, part * 2 * HD : (part + 1) * 2 * HD].astype(F32)
        dst[...] = spread(blk).astype(BF)
    rows = qf.shape[0] // steps
    low = low_lanes(rows)

    def body(i, carry):
        at = pl.ds(pl.multiple_of(i * rows, rows), rows)
        e, o, rinv = softmax_block(qf[at, :], kf[...], vf[...])
        e_ref[at, :] = e
        of[at, :] = o
        rf[at, :] = jnp.where(low, jnp.broadcast_to(rinv, (rows, 2 * HD)), 0.0)
        return carry

    lax.fori_loop(0, steps, body, 0)
    packed = unspread(of[...])
    o_ref[...] = packed
    ob_ref[...] = packed.astype(BF)
    r_ref[...] = unspread(rf[...])


def attn5_fwd_call(x):
    rows = x.shape[0]
    toks = 2 * rows
    return pl.pallas_call(
        functools.partial(attn5_fwd_kernel, 4),
        out_shape=(
            jax.ShapeDtypeStruct((rows, 2 * HD), F32),
            jax.ShapeDtypeStruct((rows, 2 * HD), F32),
            jax.ShapeDtypeStruct((rows, 2 * HD), BF),
            jax.ShapeDtypeStruct((toks, toks), BF),
        ),
        scratch_shapes=[pltpu.VMEM((toks, 2 * HD), BF)] * 3 + [pltpu.VMEM((toks, 2 * HD), F32)] * 2,
        compiler_params=pltpu.CompilerParams(vmem_limit_bytes=VMEM_LIMIT),
        cost_estimate=cost(4 * 4 * toks * toks * 2 * HD, toks * toks * 2),
        name="attn_shared_fwd",
    )(x)


def attn5_bwd_kernel(
    steps, x_ref, ga_ref, o_ref, r_ref, e_ref, out_ref, qf, kf, vf, gf, inn, dq, dk, dv
):
    for part, dst in enumerate((qf, kf, vf)):
        blk = x_ref[:, part * 2 * HD : (part + 1) * 2 * HD].astype(F32)
        dst[...] = spread(blk).astype(BF)
    g = ga_ref[...].astype(F32) * r_ref[...]
    gs = spread(g)
    gf[...] = gs.astype(BF)
    inn[...] = jnp.sum(gs * spread(o_ref[...]), axis=-1, keepdims=True)
    rows = qf.shape[0] // steps
    dk[...] = jnp.zeros_like(dk)
    dv[...] = jnp.zeros_like(dv)

    def body(i, carry):
        at = pl.ds(pl.multiple_of(i * rows, rows), rows)
        e = e_ref[at, :]
        gb = gf[at, :]
        dp = nt_dot(gb, vf[...])
        ds = (e.astype(F32) * (dp - inn[at, :])).astype(BF)
        dq[at, :] = nn(ds, kf[...]) * (HD**-0.5)
        dk[...] += tn_dot(ds, qf[at, :])
        dv[...] += tn_dot(e, gb)
        return carry

    lax.fori_loop(0, steps, body, 0)
    for part, src in enumerate((dq, dk, dv)):
        out_ref[:, part * 2 * HD : (part + 1) * 2 * HD] = unspread(src[...]).astype(BF)


def attn5_bwd_call(x, ga, o, r, e):
    rows = x.shape[0]
    toks = 2 * rows
    return pl.pallas_call(
        functools.partial(attn5_bwd_kernel, 4),
        out_shape=jax.ShapeDtypeStruct((rows, 6 * HD), BF),
        scratch_shapes=[pltpu.VMEM((toks, 2 * HD), BF)] * 4
        + [pltpu.VMEM((toks, 1), F32)]
        + [pltpu.VMEM((toks, 2 * HD), F32)] * 3,
        compiler_params=pltpu.CompilerParams(vmem_limit_bytes=VMEM_LIMIT),
        cost_estimate=cost(8 * 4 * toks * toks * 2 * HD, toks * toks * 2),
        name="attn_shared_bwd",
    )(x, ga, o, r, e)


def attn_fwd_kernel(nt, *refs):
    ns = refs[:nt]
    wq, wk, wv, bq, bv = refs[nt : nt + 5]
    att_ref, o_ref, r_ref, q_ref, k_ref, v_ref, e_ref = refs[nt + 5 :]
    rows = ns[0].shape[0]
    for c in range(nt):
        at = slice(c * rows, (c + 1) * rows)
        x = ns[c][...]
        k_ref[at, :] = nn(x, wk[...]).astype(BF)
        v_ref[at, :] = (nn(x, wv[...]) + bv[...]).astype(BF)
    q_ref[...] = ((nn(ns[0][...], wq[...]) + bq[...]) * (HD**-0.5)).astype(BF)
    low = low_lanes(rows)

    def body(pair, carry):
        lanes = pl.ds(pl.multiple_of(pair * 2 * HD, 2 * HD), 2 * HD)
        q, k, v = q_ref[:, lanes], k_ref[:, lanes], v_ref[:, lanes]
        zero = jnp.zeros_like(q)
        e0, o0, r0 = softmax_block(jnp.where(low, q, zero), k, v)
        e_ref[2 * pair] = e0
        e1, o1, r1 = softmax_block(jnp.where(low, zero, q), k, v)
        e_ref[2 * pair + 1] = e1
        o = jnp.where(low, o0, o1)
        o_ref[:, lanes] = o
        att_ref[:, lanes] = o.astype(BF)
        r_ref[:, lanes] = jnp.where(
            low, jnp.broadcast_to(r0, (rows, 2 * HD)), jnp.broadcast_to(r1, (rows, 2 * HD))
        )
        return carry

    lax.fori_loop(0, q_ref.shape[1] // (2 * HD), body, 0)


def attn_fwd_call(ns, w, bq, bv):
    nt = len(ns)
    rows, width = ns[0].shape
    toks = nt * rows
    blk = 4 * HD
    steps = width // blk
    wspec = [pl.BlockSpec((width, blk), lambda j, p=p: (0, p * steps + j)) for p in range(3)]
    bspec = pl.BlockSpec((1, blk), lambda j: (0, j))
    row = lambda n: pl.BlockSpec((n, blk), lambda j: (0, j))
    return pl.pallas_call(
        functools.partial(attn_fwd_kernel, nt),
        grid=(steps,),
        in_specs=[full((rows, width))] * nt + wspec + [bspec, bspec],
        out_specs=[row(rows)] * 4
        + [row(toks)] * 2
        + [pl.BlockSpec((4, rows, toks), lambda j: (j, 0, 0))],
        out_shape=(
            jax.ShapeDtypeStruct((rows, width), BF),
            jax.ShapeDtypeStruct((rows, width), F32),
            jax.ShapeDtypeStruct((rows, width), F32),
            jax.ShapeDtypeStruct((rows, width), BF),
            jax.ShapeDtypeStruct((toks, width), BF),
            jax.ShapeDtypeStruct((toks, width), BF),
            jax.ShapeDtypeStruct((width // HD, rows, toks), BF),
        ),
        compiler_params=params(),
        cost_estimate=cost(4 * toks * width * width + 16 * rows * toks * width, 20 << 20),
        name="attn_fwd",
    )(*ns, w, w, w, bq, bv)


def attn_bwd_kernel(ga_ref, q_ref, k_ref, v_ref, o_ref, r_ref, e_ref, gq_ref, gk_ref, gv_ref):
    rows = q_ref.shape[0]
    low = low_lanes(rows)
    q, k, v = q_ref[...], k_ref[...], v_ref[...]
    g = ga_ref[...].astype(F32) * r_ref[...]
    go = g * o_ref[...]
    g = g.astype(BF)
    zero = jnp.zeros_like(q)
    halves = []
    for side in range(2):
        mine = low if side == 0 else jnp.logical_not(low)
        qh = jnp.where(mine, q, zero)
        gh = jnp.where(mine, g, zero)
        inner = jnp.sum(jnp.where(mine, go, 0.0), axis=-1, keepdims=True)
        e = e_ref[side]
        dp = nt_dot(gh, v)
        ds = (e.astype(F32) * (dp - inner)).astype(BF)
        halves.append((nn(ds, k), tn_dot(ds, qh), tn_dot(e, gh)))
    gq_ref[...] = (jnp.where(low, halves[0][0], halves[1][0]) * (HD**-0.5)).astype(BF)
    gk_ref[...] = (halves[0][1] + halves[1][1]).astype(BF)
    gv_ref[...] = (halves[0][2] + halves[1][2]).astype(BF)


def attn_bwd_call(first, steps, ga, q, k, v, o, r, e):
    rows, width = q.shape
    toks = k.shape[0]
    blk = 2 * HD
    row = lambda n: pl.BlockSpec((n, blk), lambda j: (0, j + first))
    out = lambda n: pl.BlockSpec((n, blk), lambda j: (0, j))
    return pl.pallas_call(
        attn_bwd_kernel,
        grid=(steps,),
        in_specs=[row(rows), row(rows), row(toks), row(toks), row(rows), row(rows)]
        + [pl.BlockSpec((2, rows, toks), lambda j: (j + first, 0, 0))],
        out_specs=[out(rows), out(toks), out(toks)],
        out_shape=[jax.ShapeDtypeStruct((n, steps * blk), BF) for n in (rows, toks, toks)],
        compiler_params=params(),
        cost_estimate=cost(32 * rows * toks * blk * steps, steps * (4 << 20)),
        name="attn_bwd",
    )(ga, q, k, v, o, r, e)


def dx_kernel(count, widths, *refs):
    gqs, gks, gvs = refs[:count], refs[count : 2 * count], refs[2 * count : 3 * count]
    w_ref, own, dx, uy, d2, u1, total = refs[3 * count :]
    rows, width = own.shape
    half = rows // 2
    step = pl.program_id(0)
    col = 0
    for i, blk in enumerate(widths):
        part = nt_dot(gks[i][...], w_ref[:, width + col : width + col + blk])
        part += nt_dot(gvs[i][...], w_ref[:, 2 * width + col : 2 * width + col + blk])
        if i == 0:
            total[...] = part
        else:
            total[...] += part
        col += blk

    @pl.when(step == 0)
    def _():
        col = 0
        for i, blk in enumerate(widths):
            total[...] += nt_dot(gqs[i][...], w_ref[:, col : col + blk])
            col += blk
        own[...] = total[...]

    def put(c, top, bot):
        @pl.when(step == c)
        def _():
            top[0][top[1]] = total[:half].astype(BF)
            bot[0][bot[1]] = total[half:].astype(BF)

    put(1, (dx, 0), (u1, Ellipsis))
    put(2, (d2, Ellipsis), (uy, 0))
    put(3, (dx, 1), (uy, 1))


def dx_call(gqs, gks, gvs, w):
    rows, width = gqs[0].shape[0], w.shape[0]
    widths = [g.shape[1] for g in gqs]
    shape = jax.ShapeDtypeStruct
    chunk = [pl.BlockSpec((rows, b), lambda j: (j, 0)) for b in widths]
    return pl.pallas_call(
        functools.partial(dx_kernel, len(gqs), widths),
        grid=(4,),
        in_specs=[full(x.shape) for x in gqs] + chunk + chunk + [full(w.shape)],
        out_specs=[full((rows, width))]
        + [full((2, rows // 2, width))] * 2
        + [full((rows // 2, width))] * 2,
        out_shape=[shape((rows, width), F32)]
        + [shape((2, rows // 2, width), BF)] * 2
        + [shape((rows // 2, width), BF)] * 2,
        scratch_shapes=[pltpu.VMEM((rows, width), F32)],
        compiler_params=params(),
        cost_estimate=cost(16 * rows * width * width, 12 << 20),
        name="dx",
    )(*gqs, *gks, *gvs, w)


def put_pieces(me_ref, src, keep_ref, send_ref, index):
    nt, nf = keep_ref.shape[0], keep_ref.shape[1]
    for k in range(nt):
        for f in range(nf):
            at = (f * nt + (me_ref[1] ^ k)) * 2
            keep_ref[(k, f) + index] = src[at + me_ref[2]]
            send_ref[(k, f) + index] = src[at + 1 - me_ref[2]]


def mid_kernel(nf, nt, fast, me_ref, *refs):
    refs = list(refs)
    if fast:
        *refs, down, up, side, sems = refs
    xms, cms, refs = refs[:nf], refs[nf : 2 * nf], refs[2 * nf :]
    att_ref, att5_ref, x5_ref, c5_ref, wo_ref, bo_ref, g2_ref, s2_ref, bd_ref = refs[:9]
    wu_ref, bu_ref, wd_ref, outs_ref, out5_ref, gm_ref, ga_ref, ga5_ref = refs[9:17]
    *grads, vec_ref, gbu_ref, att, cot, mid, hat, rst, two, acc, gn2 = refs[17:]
    step = pl.program_id(0)
    r5, width = x5_ref.shape
    rm = nf * r5
    half = r5 // 2
    low = low_lanes(half)
    pairs = width // (2 * HD)

    @pl.when(step == 0)
    def _():
        att[0:rm, :] = att_ref[...]
        for pair in range(pairs):
            lanes = slice(pair * 2 * HD, (pair + 1) * 2 * HD)
            even = att5_ref[slot_of(2 * pair, nf, nt)].astype(F32)
            odd = att5_ref[slot_of(2 * pair + 1, nf, nt)].astype(F32)
            top = jnp.where(low, even, swap_halves(odd))
            bot = jnp.where(low, swap_halves(even), odd)
            att[rm : rm + r5, lanes] = jnp.concatenate([top, bot], axis=0).astype(BF)
        for k in range(nf):
            cot[k * r5 : (k + 1) * r5, :] = cms[k][...]
        cot[rm : rm + r5, :] = c5_ref[...]
        mid[...] = nn(att[...], wo_ref[...]) + bo_ref[...]
        for k in range(nf):
            mid[k * r5 : (k + 1) * r5, :] += xms[k][...].astype(F32)
        mid[rm : rm + r5, :] += x5_ref[...].astype(F32)
        n, rstd = normalize(mid[...])
        hat[...] = n
        rst[...] = rstd
        two[...] = (n * g2_ref[...] + s2_ref[...]).astype(BF)
        acc[...] = mid[...] + bd_ref[...]
        gn2[...] = jnp.zeros_like(gn2)

    pre = nn(two[...], wu_ref[...]) + bu_ref[...]
    cdf = 0.5 * (1.0 + lax.erf(pre * (0.5**0.5)))
    slope = cdf + pre * (jnp.exp(-0.5 * pre * pre) * 0.3989422804014327)
    act = (pre * cdf).astype(BF)
    acc[...] += nn(act, wd_ref[...])
    dwd = tn_dot(act, cot[...]).astype(BF)
    if fast:
        pd, pu = down.shape[2], up.shape[2]
        owners = down.shape[1]

        def copies(j):
            to_down = grads[0].at[pl.ds(j * owners, owners), pl.ds(0, pd), :]
            to_up = grads[0].at[:, pl.ds(pd + j * pu, pu), :]
            return (
                pltpu.make_async_copy(down.at[j], to_down, sems.at[0, j]),
                pltpu.make_async_copy(up.at[j], to_up, sems.at[1, j]),
            )

        down[step] = dwd.reshape(down.shape[1:])
    else:
        grads[0][...] = dwd
    gpre = (nt_dot(cot[...], wd_ref[...]) * slope).astype(BF)
    gbu_ref[...] = colsum(gpre.astype(F32))
    dwu = tn_dot(two[...], gpre)
    if fast:
        up[step] = dwu.reshape(up.shape[1:]).astype(BF)
        for copy in copies(step):
            copy.start()
    else:
        grads[1][...] = dwu.astype(BF)
    gn2[...] += nt_dot(gpre, wu_ref[...])

    @pl.when(step == pl.num_programs(0) - 1)
    def _():
        for k in range(nf):
            outs_ref[me_ref[0] ^ k] = acc[k * r5 : (k + 1) * r5, :].astype(BF)
        out5_ref[...] = acc[rm : rm + r5, :]
        e = gn2[...]
        n = hat[...]
        c = cot[...].astype(F32)
        gmid = c + norm_back(e, n, rst[...], g2_ref[...])
        gm_ref[...] = gmid
        branch = gmid.astype(BF)
        vec_ref[0:1, :] = colsum(branch.astype(F32))
        vec_ref[1:2, :] = colsum(e * n)
        vec_ref[2:3, :] = colsum(e)
        vec_ref[3:4, :] = colsum(c)
        dwo = tn_dot(att[...], branch)
        if fast:
            side[...] = dwo.reshape(side.shape).astype(BF)
            put_pieces(me_ref, side, grads[1], grads[2], ())
        else:
            grads[2][...] = dwo.astype(BF)
        gatt = nt_dot(branch, wo_ref[...])
        ga_ref[...] = gatt[0:rm].astype(BF)
        ga5_ref[...] = jnp.zeros_like(ga5_ref)
        for pair in range(pairs):
            lanes = slice(pair * 2 * HD, (pair + 1) * 2 * HD)
            top, bot = gatt[rm : rm + half, lanes], gatt[rm + half : rm + r5, lanes]
            even = jnp.where(low, top, swap_halves(bot))
            odd = jnp.where(low, swap_halves(top), bot)
            ga5_ref[slot_of(2 * pair, nf, nt)] = even.astype(BF)
            ga5_ref[slot_of(2 * pair + 1, nf, nt)] = odd.astype(BF)
        if fast:
            for j in range(nf):
                for copy in copies(j):
                    copy.wait()


def mid_call(nf, nt, fast, me, xms, cms, att, att5, x5, c5, wo, bo, g2, s2, bd, wu, bu, wd):
    r5, width = x5.shape
    rm = nf * r5
    rows = rm + r5
    ff = wu.shape[1]
    blk = ff // nf
    shape = jax.ShapeDtypeStruct
    if fast:
        dev = nf * nt * 2
        pd, pu = ff // dev, width // dev
        oshape = (nt, nf, pu, width)
        gspecs = [pl.BlockSpec(memory_space=pl.ANY)] + [full(oshape)] * 2
        gshapes = [shape((dev, pd + nf * pu, width), BF)] + [shape(oshape, BF)] * 2
        extra = [
            pltpu.VMEM((nf, nt * 2, pd, width), BF),
            pltpu.VMEM((nf, dev, pu, width), BF),
            pltpu.VMEM((dev, pu, width), BF),
            pltpu.SemaphoreType.DMA((2, nf)),
        ]
    else:
        gspecs = [
            pl.BlockSpec((blk, width), lambda j, *_: (j, 0)),
            pl.BlockSpec((width, blk), lambda j, *_: (0, j)),
            full((width, width)),
        ]
        gshapes = [shape((ff, width), BF), shape((width, ff), BF), shape((width, width), BF)]
        extra = []
    ins = [*xms, *cms, att, att5, x5, c5, wo, bo, g2, s2, bd]
    return pl.pallas_call(
        functools.partial(mid_kernel, nf, nt, fast),
        grid_spec=pltpu.PrefetchScalarGridSpec(
            num_scalar_prefetch=1,
            grid=(nf,),
            in_specs=[full(x.shape) for x in ins]
            + [
                pl.BlockSpec((width, blk), lambda j, *_: (0, j)),
                pl.BlockSpec((1, blk), lambda j, *_: (0, j)),
                pl.BlockSpec((blk, width), lambda j, *_: (j, 0)),
            ],
            out_specs=[
                full((nf, r5, width)),
                full((r5, width)),
                full((rows, width)),
                full((rm, width)),
                full(att5.shape),
            ]
            + gspecs
            + [full((4, width)), pl.BlockSpec((1, blk), lambda j, *_: (0, j))],
            scratch_shapes=[
                pltpu.VMEM((rows, width), BF),
                pltpu.VMEM((rows, width), BF),
                pltpu.VMEM((rows, width), F32),
                pltpu.VMEM((rows, width), F32),
                pltpu.VMEM((rows, 1), F32),
                pltpu.VMEM((rows, width), BF),
                pltpu.VMEM((rows, width), F32),
                pltpu.VMEM((rows, width), F32),
            ]
            + extra,
        ),
        out_shape=[
            shape((nf, r5, width), BF),
            shape((r5, width), F32),
            shape((rows, width), F32),
            shape((rm, width), BF),
            shape(att5.shape, BF),
        ]
        + gshapes
        + [shape((4, width), F32), shape((1, ff), F32)],
        compiler_params=params(),
        cost_estimate=cost(12 * rows * width * ff + 6 * rows * width * width, 24 << 20),
        name="mid",
    )(me, *ins, wu, bu, wd)


def tail5_kernel(nf, nt, fast, widths, *refs):
    if fast:
        me_ref, *refs = refs
        *refs, side = refs
    count = len(widths)
    gqs, gks, gvs = refs[:count], refs[count : 2 * count], refs[2 * count : 3 * count]
    ns, refs = refs[3 * count : 3 * count + nt], refs[3 * count + nt :]
    g_ref, n5_ref, x5_ref, gm_ref, w_ref, g1_ref = refs[:6]
    (*dwo, gb_ref, gin_ref, vec_ref, g5, dx, dw, xt) = refs[6:]
    step = pl.program_id(0)
    r5, width = x5_ref.shape
    half = r5 // 2
    low = low_lanes(half)
    for pair in range(width // (2 * HD)):
        lanes = slice(pair * 2 * HD, (pair + 1) * 2 * HD)
        even = g_ref[slot_of(2 * pair, nf, nt)].astype(F32)
        odd = g_ref[slot_of(2 * pair + 1, nf, nt)].astype(F32)
        top = jnp.where(low, even, swap_halves(odd))
        bot = jnp.where(low, swap_halves(even), odd)
        g5[:, lanes] = jnp.concatenate([top, bot], axis=0).astype(BF)
    g = g5[...]
    gb5 = colsum(g.astype(F32))
    rows = ns[0].shape[0]

    def add(mains, chunks):
        col = 0
        for main, blk in zip(mains, widths):
            lanes = slice(col, col + blk)
            gb_ref[0, :, lanes] = gb5[:, lanes] + colsum(main[...].astype(F32))
            dw[:, lanes] = nn(xt[:, 0 : chunks * rows], main[...]) + tn_dot(n5_ref[...], g[:, lanes])
            col += blk

    @pl.when(step == 0)
    def _():
        dx[...] = jnp.zeros_like(dx)
        for c in range(nt):
            xt[:, c * rows : (c + 1) * rows] = ns[c][...].T
        add(gqs, 1)

    @pl.when(step == 1)
    def _():
        add(gks, nt)

    @pl.when(step == 2)
    def _():
        add(gvs, nt)

    if fast:
        side[...] = dw[...].reshape(side.shape).astype(BF)
        put_pieces(me_ref, side, dwo[0], dwo[1], (0,))
    else:
        dwo[0][...] = dw[...].astype(BF)

    dx[...] += nt_dot(g, w_ref[...])

    @pl.when(step == pl.num_programs(0) - 1)
    def _():
        n, rstd = normalize(x5_ref[...].astype(F32))
        e = dx[...]
        gin_ref[...] = gm_ref[...] + norm_back(e, n, rstd, g1_ref[...])
        vec_ref[0:1, :] = colsum(e * n)
        vec_ref[1:2, :] = colsum(e)


def tail5_call(nf, nt, fast, me, gqs, gks, gvs, ns, g, n5, x5, gm, w, g1):
    r5, width = x5.shape
    at = gm.shape[0] // r5 - 1
    bshape = jax.ShapeDtypeStruct
    if fast:
        pu = width // (nf * nt * 2)
        wspecs = [pl.BlockSpec((nt, nf, 1, pu, width), lambda j, *_: (0, 0, j, 0, 0))] * 2
        wshapes = [bshape((nt, nf, 3, pu, width), BF)] * 2
        extra = [pltpu.VMEM((nf * nt * 2, pu, width), BF)]
    else:
        wspecs = [pl.BlockSpec((width, width), lambda j, *_: (0, j))]
        wshapes = [bshape((width, 3 * width), BF)]
        extra = []
    return pl.pallas_call(
        functools.partial(tail5_kernel, nf, nt, fast, [x.shape[1] for x in gqs]),
        grid_spec=pltpu.PrefetchScalarGridSpec(
            num_scalar_prefetch=int(fast),
            grid=(3,),
            in_specs=[full(x.shape) for x in (*gqs, *gks, *gvs, *ns)]
            + [
                pl.BlockSpec((g.shape[0], r5 // 2, 2 * HD), lambda j, *_: (0, 0, j)),
                full(n5.shape),
                full(x5.shape),
                pl.BlockSpec((r5, width), lambda j, *_: (at, 0)),
                pl.BlockSpec((width, width), lambda j, *_: (0, j)),
                full((1, width)),
            ],
            out_specs=wspecs
            + [
                pl.BlockSpec((1, 1, width), lambda j, *_: (j, 0, 0)),
                full((r5, width)),
                full((2, width)),
            ],
            scratch_shapes=[
                pltpu.VMEM((r5, width), BF),
                pltpu.VMEM((r5, width), F32),
                pltpu.VMEM((width, width), F32),
                pltpu.VMEM((width, nt * ns[0].shape[0]), BF),
            ]
            + extra,
        ),
        out_shape=wshapes
        + [
            bshape((3, 1, width), F32),
            bshape((r5, width), F32),
            bshape((2, width), F32),
        ],
        compiler_params=params(),
        cost_estimate=cost(4 * r5 * width * width * 3 + 4 * width * width * 1280, 16 << 20),
        name="tail_shared",
    )(*([me] if fast else []), *gqs, *gks, *gvs, *ns, g, n5, x5, gm, w, g1)


def tail_kernel(nf, me_ref, own, gx, gy, rd, ru, *refs):
    xs, (gm_ref, g1_ref, gin_ref, vec_ref) = refs[:nf], refs[nf:]
    rows = xs[0].shape[0]
    half = rd.shape[0]
    gain_sum = shift_sum = 0.0
    for k in range(nf):
        at = slice(k * rows, (k + 1) * rows)
        lower = k * rows < half
        one, two = (gx, rd) if lower else (gy, ru)
        part = slice(k * rows, (k + 1) * rows) if lower else slice(k * rows - half, (k + 1) * rows - half)
        e = own[at, :] + one[0, part, :].astype(F32) + two[part, :].astype(F32)
        n, rstd = normalize(xs[k][...].astype(F32))
        gin_ref[me_ref[0] ^ k] = (gm_ref[at, :] + norm_back(e, n, rstd, g1_ref[...])).astype(BF)
        gain_sum += colsum(e * n)
        shift_sum += colsum(e)
    vec_ref[0:1, :] = gain_sum
    vec_ref[1:2, :] = shift_sum


def tail_call(me, own, gx, gy, rd, ru, xs, gm, g1):
    rows, width = xs[0].shape
    nf = len(xs)
    half = nf * rows // 2
    return pl.pallas_call(
        functools.partial(tail_kernel, nf),
        grid_spec=pltpu.PrefetchScalarGridSpec(
            num_scalar_prefetch=1,
            grid=(1,),
            in_specs=[full((nf * rows, width))]
            + [full((1, half, width))] * 2
            + [full((half, width))] * 2
            + [full((rows, width))] * nf
            + [full((nf * rows, width)), full((1, width))],
            out_specs=[full((nf, rows, width)), full((2, width))],
        ),
        out_shape=[
            jax.ShapeDtypeStruct((nf, rows, width), BF),
            jax.ShapeDtypeStruct((2, width), F32),
        ],
        compiler_params=params(),
        cost_estimate=cost(30 * nf * rows * width, 6 << 20),
        name="tail",
    )(me, own, gx, gy, rd, ru, *xs, gm, g1)


def pair_sum_kernel(nd, nu, *refs):
    ins, (dx, d0, d2, uy, u0, u1) = refs[: 2 * (nd + nu)], refs[2 * (nd + nu) :]
    outs = ((d0, (dx, 0), d2, (dx, 1)), (u0, u1, (uy, 0), (uy, 1)))
    for side, pairs in enumerate((ins[: 2 * nd], ins[2 * nd :])):
        at = 0
        for keep, got in zip(pairs[0::2], pairs[1::2]):
            rows = keep.shape[2]
            for k in range(4):
                total = (keep[k, 0].astype(F32) + got[k, 0].astype(F32)).astype(BF)
                out = outs[side][k]
                if isinstance(out, tuple):
                    out[0][out[1], 0, at : at + rows, :] = total
                else:
                    out[0, at : at + rows, :] = total
            at += rows


def pair_sum(ds, us, steps):
    width = ds[0][0].shape[3]
    specs, args = [], []
    for keep, got, first in ds + us:
        spec = pl.BlockSpec((4, 1) + keep.shape[2:], lambda j, f=first: (0, j + f, 0, 0))
        specs += [spec, spec]
        args += [keep, got]
    ospecs, oshapes = [], []
    for side in (ds, us):
        rows = sum(x[0].shape[2] for x in side)
        one = pl.BlockSpec((1, rows, width), lambda j: (j, 0, 0))
        two = pl.BlockSpec((2, 1, rows, width), lambda j: (0, j, 0, 0))
        ospecs += [two, one, one]
        oshapes += [
            jax.ShapeDtypeStruct((2, steps, rows, width), BF),
            jax.ShapeDtypeStruct((steps, rows, width), BF),
            jax.ShapeDtypeStruct((steps, rows, width), BF),
        ]
    return pl.pallas_call(
        functools.partial(pair_sum_kernel, len(ds), len(us)),
        grid=(steps,),
        in_specs=specs,
        out_specs=ospecs,
        out_shape=oshapes,
        compiler_params=params(),
        cost_estimate=cost(1 << 20, 8 << 20),
        name="pair_sum",
    )(*args)


def relay_sum_kernel(d2, gx, u1, gy, sd, su):
    sd[...] = (d2[...].astype(F32) + gx[0].astype(F32)).astype(BF)
    su[...] = (u1[...].astype(F32) + gy[0].astype(F32)).astype(BF)


def relay_sum(d2, gx, u1, gy):
    second = lambda x: pl.BlockSpec((1,) + x.shape[1:], lambda *_: (1,) + (0,) * (x.ndim - 1))
    return pl.pallas_call(
        relay_sum_kernel,
        grid=(1,),
        in_specs=[full(d2.shape), second(gx), full(u1.shape), second(gy)],
        out_specs=[full(d2.shape), full(u1.shape)],
        out_shape=[jax.ShapeDtypeStruct(d2.shape, BF), jax.ShapeDtypeStruct(u1.shape, BF)],
        compiler_params=params(),
        cost_estimate=cost(d2.size, 6 * d2.size),
        name="relay_sum",
    )(d2, gx, u1, gy)


def along(axis, k, x):
    return lax.ppermute(x, axis, [(i, i ^ k) for i in range(4)])


def relay_start(dx, uy):
    return along("tm", 1, dx), along("tm", 2, uy)


def relay_end(gx, gy, d2, u1):
    sd, su = relay_sum(d2, gx, u1, gy)
    return along("tm", 2, sd), along("tm", 1, su)


def tm_sum_kernel(nf, groups, me_ref, *refs):
    count = len(groups)
    outs, total = refs[3 * count : 3 * count + nf], refs[-1]
    for i, (first, blocks, at) in enumerate(groups):
        own, gx, rd = refs[3 * i : 3 * i + 3]
        rows = own.shape[1]
        for f in range(blocks):
            part = own[f].astype(F32) + gx[0, f].astype(F32) + rd[f].astype(F32)
            total[first + f, at : at + rows, :] = part.astype(BF)
    for k in range(nf):
        outs[k][...] = total[me_ref[0] ^ k]


def tm_sum(nf, me, groups):
    specs, args, where, rows = [], [], [], 0
    for own, gx, rd, first, at in groups:
        specs += [full(own.shape), full((1,) + own.shape), full(own.shape)]
        args += [own, gx, rd]
        where.append((first, own.shape[0], at))
        rows = max(rows, at + own.shape[1])
    width = groups[0][0].shape[2]
    return pl.pallas_call(
        functools.partial(tm_sum_kernel, nf, where),
        grid_spec=pltpu.PrefetchScalarGridSpec(
            num_scalar_prefetch=1,
            grid=(1,),
            in_specs=specs,
            out_specs=[full((rows, width))] * nf,
            scratch_shapes=[pltpu.VMEM((nf, rows, width), BF)],
        ),
        out_shape=[jax.ShapeDtypeStruct((rows, width), BF)] * nf,
        compiler_params=params(),
        cost_estimate=cost(1 << 20, 5 << 20),
        name="tm_sum",
    )(me, *args)


def last_sum_kernel(nf, places, *refs):
    parts, outs = refs[:nf], refs[nf:]
    for at, rows, out, col in places:
        lanes = parts[0].shape[1]
        total = parts[0][at : at + rows, :].astype(F32)
        for part in parts[1:]:
            total = total + part[at : at + rows, :].astype(F32)
        outs[out][:, col : col + lanes] = total


def last_sum(parts, places, shapes):
    nf = len(parts)
    return pl.pallas_call(
        functools.partial(last_sum_kernel, nf, places),
        out_shape=[jax.ShapeDtypeStruct(x, F32) for x in shapes],
        compiler_params=pltpu.CompilerParams(vmem_limit_bytes=VMEM_LIMIT),
        cost_estimate=cost(nf * parts[0].size, 2 * nf * parts[0].size),
        name="last_sum",
    )(*parts)


def swap_cores(x):
    return lax.ppermute(x, "grp", [(0, 1), (1, 0)])


def exchange(axis, parts):
    pairs = lambda k: [(i, i ^ k) for i in range(len(parts))]
    return [parts[0]] + [lax.ppermute(parts[k], axis, pairs(k)) for k in range(1, len(parts))]


def tie(x, *deps):
    flat, tree = jax.tree.flatten(x)
    tied = lax.optimization_barrier((flat, deps))[0]
    return jax.tree.unflatten(tree, tied)


def over(axes, x):
    return lax.all_to_all(x, axes, 0, 0)


def local(
    nf,
    nt,
    ng,
    inputs,
    gain_one,
    shift_one,
    w_qkv,
    bias_query,
    bias_value,
    w_out,
    bias_out,
    gain_two,
    shift_two,
    w_up,
    bias_up,
    w_down,
    bias_down,
    cotangent,
):
    _, r, width = inputs.shape
    ff = w_up.shape[1]
    dev = nf * nt * ng
    per = width // dev
    fast = ng == 2 and per % 8 == 0 and ff // nf == width
    me = jnp.stack([lax.axis_index(a) for a in ALL]).astype(jnp.int32)
    g1, s1 = gain_one[None], shift_one[None]
    bq, bv = bias_query[None], bias_value[None]
    both = ("freq", "tm")
    x5, c5 = inputs[nf], cotangent[nf]

    picked = pick_call(nf, me, inputs, cotangent)
    xs = exchange("freq", picked[:nf])
    n5, pack5 = q5_call(nf, nt, x5, g1, s1, w_qkv, bq, bv)
    nm = ln_call(tie(xs, pack5), g1, s1)
    ns = exchange("tm", [nm] * nt)
    got5 = over(both, tie(pack5, nm)).reshape(-1, 6 * HD)
    cs = exchange("freq", tie(picked[nf:], got5))
    o5, r5, ob5, e5 = attn5_fwd_call(got5)
    att5 = over(both, ob5.reshape(nf * nt, r // 2, 2 * HD))
    att, o, rr, q, k, v, e = attn_fwd_call(tie(ns, ob5), w_qkv, bq, bv)
    bout, g2, s2, bdown, bup = (x[None] for x in (bias_out, gain_two, shift_two, bias_down, bias_up))
    outs, out5, gm, ga, ga5, *dws, vec, gbu = mid_call(
        nf, nt, fast, me, xs, cs, att, att5, x5, c5, w_out, bout, g2, s2, bdown, w_up, bup, w_down
    )
    pieces = lambda x: x.reshape(nt, nf, -1, width)
    half, pd = nf // 2, ff // dev
    if fast:
        dff = lax.psum_scatter(dws[0].reshape(-1, width), ALL, scatter_dimension=0, tiled=True)
        keep_o, got_o = pieces(dws[1]), pieces(swap_cores(dws[2]))
    got_ga5 = over(both, ga5).reshape(-1, 2 * HD)
    block0 = attn_bwd_call(0, 3, ga, q, k, v, o, rr, e)
    order = block0[0]
    g5 = attn5_bwd_call(got5, tie(got_ga5, order), o5, r5, e5).reshape(nf * nt, r // 2, 6 * HD)
    order = g5
    g5 = over(both, g5)
    block1 = attn_bwd_call(3, 3, tie(ga, order), q, k, v, o, rr, e)
    gqs, gks, gvs = zip(block0, block1)
    own, dxm, uym, d2m, u1m = dx_call(gqs, gks, gvs, w_qkv)
    gxm, gym = relay_start(dxm, uym)
    order = own
    outs = over("freq", tie(outs, order))
    *dwqkv, gb, gin5, vec5 = tail5_call(
        nf, nt, fast, me, tie(gqs, order), gks, gvs, ns, g5, n5, x5, gm, w_qkv, g1
    )
    order = gb
    if fast:
        keep, got = pieces(dwqkv[0]), pieces(swap_cores(dwqkv[1]))
    sdm, sum_ = relay_sum(*tie((d2m, gxm, u1m, gym), order))
    rdm, rum = along("tm", 2, sdm), along("tm", 1, sum_)
    gin, vec_m = tail_call(me, own, gxm, gym, rdm, rum, xs, gm, g1)
    order = vec_m
    gin = over("freq", gin)
    if fast:
        dxq, d0q, d2q, uyq, u0q, u1q = pair_sum(
            [(keep, tie(got, order), 0), (keep_o, got_o, 0)],
            [(keep, got, half), (keep_o, got_o, half)],
            half,
        )
        gxq, gyq = relay_start(dxq, uyq)
        sdq, suq = relay_sum(d2q, gxq, u1q, gyq)
        rdq, ruq = along("tm", 2, sdq), along("tm", 1, suq)
        sums_q = exchange(
            "freq", tm_sum(nf, me, [(d0q, gxq, rdq, 0, 0), (u0q, gyq, ruq, half, 0)])
        )
        places = [(i * per, per, 0, i * width) for i in range(3)] + [(3 * per, per, 1, 0)]
        dwqkv, dwo = last_sum(sums_q, places, [(per, 3 * width), (per, width)])
        dwd = dff[:pd].astype(F32)
        dwu = dff[pd:].astype(F32).reshape(nf, per, width).transpose(1, 0, 2).reshape(per, ff)
    else:
        dwd, dwu, dwo, dwqkv = (
            lax.psum_scatter(x, ALL, scatter_dimension=0, tiled=True).astype(F32)
            for x in dws + dwqkv
        )
    block_out = jnp.concatenate([outs.astype(F32), out5[None]], axis=0)
    grad_in = jnp.concatenate([gin.astype(F32), gin5[None]], axis=0)
    vec1 = vec_m + vec5
    small = jnp.concatenate([vec1, vec, gb[0], gb[2]], axis=0)
    small = small.reshape(8, dev, width // dev).transpose(1, 0, 2).reshape(dev, -1)
    small = jnp.concatenate([small, gbu.reshape(dev, ff // dev)], axis=1)
    small = jnp.sum(over(ALL, small), axis=0)
    piece = lambda i: small[i * per : (i + 1) * per]
    return (
        block_out,
        grad_in,
        piece(0),
        piece(1),
        dwqkv,
        piece(6),
        piece(7),
        dwo,
        piece(2),
        piece(3),
        piece(4),
        dwu,
        small[8 * per :],
        dwd,
        piece(5),
    )


def solution(mesh):
    tokens = P("grp", ("freq", "tm"), None)
    vec = P(ALL)
    mat = P(ALL, None)
    return jax.shard_map(
        functools.partial(local, mesh.shape["freq"], mesh.shape["tm"], mesh.shape["grp"]),
        mesh=mesh,
        in_specs=(tokens,) + (P(),) * 13 + (tokens,),
        out_specs=(
            tokens,
            tokens,
            vec,
            vec,
            mat,
            vec,
            vec,
            mat,
            vec,
            vec,
            vec,
            mat,
            vec,
            mat,
            vec,
        ),
        check_vma=False,
    )
```

```python
import functools

import jax
import jax.numpy as jnp
from jax import lax
from jax.experimental import pallas as pl
from jax.experimental.pallas import tpu as pltpu
from jax.sharding import PartitionSpec as P

HD = 64
NORM_EPS = 1e-06
BF = jnp.bfloat16
F32 = jnp.float32
ALL = ("freq", "tm", "grp")
VMEM_LIMIT = 60 * 1024 * 1024
GAIN1, SHIFT1, BIAS_Q, BIAS_V, BIAS_OUT, GAIN2, SHIFT2, BIAS_DOWN, BIAS_UP = range(9)


def row_of(ref, i):
    return ref[i : i + 1, :]


def nn(a, b):
    return lax.dot_general(a, b, (((1,), (0,)), ((), ())), preferred_element_type=F32)


def nt_dot(a, b):
    return lax.dot_general(a, b, (((1,), (1,)), ((), ())), preferred_element_type=F32)


def tn_dot(a, b):
    return lax.dot_general(a, b, (((0,), (0,)), ((), ())), preferred_element_type=F32)


def normalize(x):
    mean = jnp.mean(x, axis=-1, keepdims=True)
    centered = x - mean
    var = jnp.mean(centered * centered, axis=-1, keepdims=True)
    rstd = lax.rsqrt(var + NORM_EPS)
    return centered * rstd, rstd


def norm_back(e, n, rstd, gain):
    eg = e * gain
    return rstd * (
        eg - jnp.mean(eg, axis=-1, keepdims=True) - n * jnp.mean(eg * n, axis=-1, keepdims=True)
    )


def colsum(x):
    return jnp.sum(x, axis=0, keepdims=True)


def low_lanes(rows):
    return lax.broadcasted_iota(jnp.int32, (rows, 2 * HD), 1) < HD


def swap_halves(x):
    return pltpu.roll(x, HD, 1)


def slot_of(head, nf, nt):
    per = -(-(12) // nf)
    return (head // per) * nt + head % per


def params(count=1):
    return pltpu.CompilerParams(
        dimension_semantics=("arbitrary",) * count, vmem_limit_bytes=VMEM_LIMIT
    )


def full(shape):
    return pl.BlockSpec(shape, lambda *_: (0,) * len(shape))


def clip_at(x, i):
    return pl.BlockSpec((None,) + x.shape[1:], lambda *_: (i, 0, 0))


def cost(flops, nbytes, weight=1):
    return pl.CostEstimate(
        flops=int(weight * flops), bytes_accessed=int(weight * nbytes), transcendentals=0
    )


def pick_kernel(nf, count, me_ref, x_ref, *refs):
    vecs, outs = refs[:count], refs[count:]
    for k in range(nf):
        outs[k][...] = x_ref[me_ref[0] ^ k]
    if count:
        width = x_ref.shape[2]
        for i in range(count - 1):
            outs[nf][i : i + 1, :] = vecs[i][...].reshape(1, width)
        last = vecs[count - 1]
        for i in range(last.shape[0] // width):
            at = count - 1 + i
            outs[nf][at : at + 1, :] = last[i * width : (i + 1) * width].reshape(1, width)


def pick_call(nf, me, x, vecs=()):
    _, rows, width = x.shape
    count = 8 + -(-sum(v.shape[0] for v in vecs) // width) // 8 * 8
    more = [(count, width)] if vecs else []
    return pl.pallas_call(
        functools.partial(pick_kernel, nf, len(vecs)),
        grid_spec=pltpu.PrefetchScalarGridSpec(
            num_scalar_prefetch=1,
            grid=(1,),
            in_specs=[full(x.shape)] + [full(v.shape) for v in vecs],
            out_specs=[full((rows, width))] * nf + [full(y) for y in more],
        ),
        out_shape=[jax.ShapeDtypeStruct((rows, width), BF)] * nf
        + [jax.ShapeDtypeStruct(y, F32) for y in more],
        compiler_params=params(),
        cost_estimate=cost(0, 4 * x.size),
        name="pick",
    )(me, x, *vecs)


def assemble_kernel(nf, me_ref, *refs):
    for k in range(nf):
        refs[-1][me_ref[0] ^ k] = refs[k][...].astype(F32)
    refs[-1][nf] = refs[nf][...]


def assemble_call(nf, me, parts, five):
    rows, width = five.shape
    return pl.pallas_call(
        functools.partial(assemble_kernel, nf),
        grid_spec=pltpu.PrefetchScalarGridSpec(
            num_scalar_prefetch=1,
            grid=(1,),
            in_specs=[full((rows, width))] * (nf + 1),
            out_specs=full((nf + 1, rows, width)),
        ),
        out_shape=jax.ShapeDtypeStruct((nf + 1, rows, width), F32),
        compiler_params=params(),
        cost_estimate=cost(0, 8 * (nf + 1) * five.size),
        name="assemble",
    )(me, *parts, five)


def ln_kernel(nf, *refs):
    vec_ref, n_ref = refs[nf:]
    for k in range(nf):
        rows = refs[k].shape[0]
        n, _ = normalize(refs[k][...].astype(F32))
        n = n * row_of(vec_ref, GAIN1) + row_of(vec_ref, SHIFT1)
        n_ref[k * rows : (k + 1) * rows, :] = n.astype(BF)


def ln_call(xs, vecs):
    rows, width = xs[0].shape
    return pl.pallas_call(
        functools.partial(ln_kernel, len(xs)),
        grid=(1,),
        in_specs=[full((rows, width))] * len(xs) + [full(vecs.shape)],
        out_specs=full((len(xs) * rows, width)),
        out_shape=jax.ShapeDtypeStruct((len(xs) * rows, width), BF),
        compiler_params=pltpu.CompilerParams(vmem_limit_bytes=VMEM_LIMIT),
        cost_estimate=cost(len(xs) * rows * width * 10, len(xs) * rows * width * 4, 100),
        name="ln_one",
    )(*xs, vecs)


def q5_kernel(nf, nt, x_ref, vec_ref, w_ref, n_ref, pack_ref):
    rows, width = x_ref.shape
    half = rows // 2
    hat, _ = normalize(x_ref[...].astype(F32))
    n = (hat * row_of(vec_ref, GAIN1) + row_of(vec_ref, SHIFT1)).astype(BF)
    n_ref[...] = n
    low = low_lanes(half)
    pack_ref[...] = jnp.zeros_like(pack_ref)
    for part in range(3):
        proj = nn(n, w_ref[:, part * width : (part + 1) * width])
        if part == 0:
            proj = (proj + row_of(vec_ref, BIAS_Q)) * (HD**-0.5)
        if part == 2:
            proj = proj + row_of(vec_ref, BIAS_V)
        for pair in range(width // (2 * HD)):
            blk = proj[:, pair * 2 * HD : (pair + 1) * 2 * HD]
            top, bot = blk[:half], blk[half:]
            even = jnp.where(low, top, swap_halves(bot))
            odd = jnp.where(low, swap_halves(top), bot)
            lanes = slice(part * 2 * HD, (part + 1) * 2 * HD)
            pack_ref[slot_of(2 * pair, nf, nt), :, lanes] = even.astype(BF)
            pack_ref[slot_of(2 * pair + 1, nf, nt), :, lanes] = odd.astype(BF)


def q5_call(nf, nt, x, vecs, w):
    _, rows, width = x.shape
    return pl.pallas_call(
        functools.partial(q5_kernel, nf, nt),
        grid=(1,),
        in_specs=[clip_at(x, nf), full(vecs.shape), full(w.shape)],
        out_specs=[full((rows, width)), full((nf * nt, rows // 2, 6 * HD))],
        out_shape=(
            jax.ShapeDtypeStruct((rows, width), BF),
            jax.ShapeDtypeStruct((nf * nt, rows // 2, 6 * HD), BF),
        ),
        compiler_params=pltpu.CompilerParams(vmem_limit_bytes=VMEM_LIMIT),
        cost_estimate=cost(2 * rows * w.size, w.size * 2),
        name="q_shared",
    )(x, vecs, w)


def spread(x):
    rows = x.shape[0]
    low = low_lanes(rows)
    zero = jnp.zeros_like(x)
    return jnp.concatenate([jnp.where(low, x, zero), jnp.where(low, swap_halves(x), zero)], axis=0)


def unspread(x):
    half = x.shape[0] // 2
    return x[:half] + swap_halves(x[half:])


def stack_heads(x):
    low = low_lanes(x.shape[0])
    zero = jnp.zeros_like(x)
    return jnp.concatenate([jnp.where(low, x, zero), jnp.where(low, zero, x)], axis=0)


def softmax_block(q, k, v):
    s = nt_dot(q, k)
    m = jnp.max(s, axis=-1, keepdims=True)
    e = jnp.exp(s - m)
    total = jnp.sum(e, axis=-1, keepdims=True)
    e = e.astype(BF)
    rinv = 1.0 / total
    return e, nn(e, v) * rinv, rinv


def attn5_fwd_kernel(x_ref, o_ref, r_ref, ob_ref, e_ref, qf, kf, vf, of, rf):
    step = pl.program_id(0)

    @pl.when(step == 0)
    def _():
        for part, dst in enumerate((qf, kf, vf)):
            blk = x_ref[:, part * 2 * HD : (part + 1) * 2 * HD].astype(F32)
            dst[...] = spread(blk).astype(BF)

    rows = e_ref.shape[0]
    at = pl.ds(pl.multiple_of(step * rows, rows), rows)
    e, o, rinv = softmax_block(qf[at, :], kf[...], vf[...])
    e_ref[...] = e
    of[at, :] = o
    rf[at, :] = jnp.where(low_lanes(rows), jnp.broadcast_to(rinv, (rows, 2 * HD)), 0.0)

    @pl.when(step == pl.num_programs(0) - 1)
    def _():
        packed = unspread(of[...])
        o_ref[...] = packed
        ob_ref[...] = packed.astype(BF)
        r_ref[...] = unspread(rf[...])


def attn5_fwd_call(x):
    rows = x.shape[0]
    toks = 2 * rows
    shape = jax.ShapeDtypeStruct
    return pl.pallas_call(
        attn5_fwd_kernel,
        grid=(4,),
        in_specs=[full(x.shape)],
        out_specs=[full((rows, 2 * HD))] * 3 + [pl.BlockSpec((toks // 4, toks), lambda j: (j, 0))],
        out_shape=(
            shape((rows, 2 * HD), F32),
            shape((rows, 2 * HD), F32),
            shape((rows, 2 * HD), BF),
            shape((toks, toks), BF),
        ),
        scratch_shapes=[pltpu.VMEM((toks, 2 * HD), BF)] * 3 + [pltpu.VMEM((toks, 2 * HD), F32)] * 2,
        compiler_params=params(),
        cost_estimate=cost(4 * 4 * toks * toks * 2 * HD, toks * toks * 2),
        name="attn_shared_fwd",
    )(x)


def attn5_bwd_kernel(x_ref, ga_ref, o_ref, r_ref, e_ref, out_ref, qf, kf, vf, gf, inn, dq, dk, dv):
    step = pl.program_id(0)

    @pl.when(step == 0)
    def _():
        for part, dst in enumerate((qf, kf, vf)):
            blk = x_ref[:, part * 2 * HD : (part + 1) * 2 * HD].astype(F32)
            dst[...] = spread(blk).astype(BF)
        g = ga_ref[...].astype(F32) * r_ref[...]
        gs = spread(g)
        gf[...] = gs.astype(BF)
        inn[...] = jnp.sum(gs * spread(o_ref[...]), axis=-1, keepdims=True)
        dk[...] = jnp.zeros_like(dk)
        dv[...] = jnp.zeros_like(dv)

    rows = e_ref.shape[0]
    at = pl.ds(pl.multiple_of(step * rows, rows), rows)
    e = e_ref[...]
    gb = gf[at, :]
    dp = nt_dot(gb, vf[...])
    ds = (e.astype(F32) * (dp - inn[at, :])).astype(BF)
    dq[at, :] = nn(ds, kf[...]) * (HD**-0.5)
    dk[...] += tn_dot(ds, qf[at, :])
    dv[...] += tn_dot(e, gb)

    @pl.when(step == pl.num_programs(0) - 1)
    def _():
        for part, src in enumerate((dq, dk, dv)):
            out_ref[:, part * 2 * HD : (part + 1) * 2 * HD] = unspread(src[...]).astype(BF)


def attn5_bwd_call(x, ga, o, r, e):
    rows = x.shape[0]
    toks = 2 * rows
    return pl.pallas_call(
        attn5_bwd_kernel,
        grid=(4,),
        in_specs=[full(y.shape) for y in (x, ga, o, r)]
        + [pl.BlockSpec((toks // 4, toks), lambda j: (j, 0))],
        out_specs=full((rows, 6 * HD)),
        out_shape=jax.ShapeDtypeStruct((rows, 6 * HD), BF),
        scratch_shapes=[pltpu.VMEM((toks, 2 * HD), BF)] * 4
        + [pltpu.VMEM((toks, 1), F32)]
        + [pltpu.VMEM((toks, 2 * HD), F32)] * 3,
        compiler_params=params(),
        cost_estimate=cost(8 * 4 * toks * toks * 2 * HD, toks * toks * 2),
        name="attn_shared_bwd",
    )(x, ga, o, r, e)


def kv_kernel(count, first_v, *refs):
    xs, (w_ref, vec_ref, kv_ref) = refs[:count], refs[count:]
    rows = xs[0].shape[0]
    shift = jnp.where(pl.program_id(0) >= first_v, row_of(vec_ref, BIAS_V), 0.0)
    for c in range(count):
        part = nn(xs[c][...], w_ref[...]) + shift
        kv_ref[c * rows : (c + 1) * rows, :] = part.astype(BF)


def kv_call(xs, w, vecs, weight):
    rows, width = xs[0].shape
    blk = width // 2
    steps = width // blk
    return pl.pallas_call(
        functools.partial(kv_kernel, len(xs), steps),
        grid=(2 * steps,),
        in_specs=[full((rows, width))] * len(xs)
        + [
            pl.BlockSpec((width, blk), lambda j: (0, steps + j)),
            pl.BlockSpec((8, blk), lambda j: (0, j % steps)),
        ],
        out_specs=pl.BlockSpec((len(xs) * rows, blk), lambda j: (0, j)),
        out_shape=jax.ShapeDtypeStruct((len(xs) * rows, 2 * width), BF),
        compiler_params=params(),
        cost_estimate=cost(4 * len(xs) * rows * width * width, 6 << 20, weight),
        name="kv",
    )(*xs, w, vecs)


def attn_fwd_kernel(x_ref, wq_ref, vec_ref, k0, k1, v0, v1, att_ref, o_ref, r_ref, q_ref, e_ref, kc, vc):
    rows = x_ref.shape[0]
    kc[0:rows, :] = k0[...]
    kc[rows:, :] = k1[...]
    vc[0:rows, :] = v0[...]
    vc[rows:, :] = v1[...]
    q = ((nn(x_ref[...], wq_ref[...]) + row_of(vec_ref, BIAS_Q)) * (HD**-0.5)).astype(BF)
    q_ref[...] = q
    low = low_lanes(rows)
    zero = jnp.zeros_like(q)
    k, v = kc[...], vc[...]
    e0, o0, r0 = softmax_block(jnp.where(low, q, zero), k, v)
    e_ref[0] = e0
    e1, o1, r1 = softmax_block(jnp.where(low, zero, q), k, v)
    e_ref[1] = e1
    o = jnp.where(low, o0, o1)
    o_ref[...] = o
    att_ref[...] = o.astype(BF)
    r_ref[...] = jnp.where(
        low, jnp.broadcast_to(r0, (rows, 2 * HD)), jnp.broadcast_to(r1, (rows, 2 * HD))
    )


def kv_specs(kv0, kv1, pairs):
    one = lambda x, at: pl.BlockSpec((x.shape[0], 2 * HD), lambda j, at=at: (0, j + at))
    return [one(kv0, 0), one(kv1, 0), one(kv0, pairs), one(kv1, pairs)]


def attn_fwd_call(x, w, vecs, kv0, kv1):
    rows, width = x.shape
    toks = rows + kv1.shape[0]
    blk = 2 * HD
    pairs = width // blk
    row = pl.BlockSpec((rows, blk), lambda j: (0, j))
    shape = jax.ShapeDtypeStruct
    return pl.pallas_call(
        attn_fwd_kernel,
        grid=(pairs,),
        in_specs=[full(x.shape), pl.BlockSpec((width, blk), lambda j: (0, j))]
        + [pl.BlockSpec((8, blk), lambda j: (0, j))]
        + kv_specs(kv0, kv1, pairs),
        out_specs=[row] * 4 + [pl.BlockSpec((2, rows, toks), lambda j: (j, 0, 0))],
        out_shape=(
            shape((rows, width), BF),
            shape((rows, width), F32),
            shape((rows, width), F32),
            shape((rows, width), BF),
            shape((width // HD, rows, toks), BF),
        ),
        scratch_shapes=[pltpu.VMEM((toks, blk), BF)] * 2,
        compiler_params=params(),
        cost_estimate=cost(16 * rows * toks * width, 20 << 20, 0.01),
        name="attn_fwd",
    )(x, w, vecs, kv0, kv1, kv0, kv1)


def attn_bwd_kernel(ga_ref, q_ref, k0, k1, v0, v1, o_ref, r_ref, e_ref, gq_ref, gkv_ref, kc, vc):
    rows = q_ref.shape[0]
    kc[0:rows, :] = k0[...]
    kc[rows:, :] = k1[...]
    vc[0:rows, :] = v0[...]
    vc[rows:, :] = v1[...]
    low = low_lanes(rows)
    stack = stack_heads
    g = ga_ref[...].astype(F32) * r_ref[...]
    inner = jnp.sum(stack(g * o_ref[...]), axis=-1, keepdims=True)
    gs, qs = stack(g.astype(BF)), stack(q_ref[...])
    e = e_ref[...].reshape(2 * rows, e_ref.shape[2])
    dp = nt_dot(gs, vc[...])
    ds = (e.astype(F32) * (dp - inner)).astype(BF)
    dq = nn(ds, kc[...])
    gq_ref[...] = (jnp.where(low, dq[:rows], dq[rows:]) * (HD**-0.5)).astype(BF)
    gkv_ref[0] = tn_dot(ds, qs).astype(BF)
    gkv_ref[1] = tn_dot(e, gs).astype(BF)


def attn_bwd_call(ga, q, kv0, kv1, o, r, e):
    rows, width = q.shape
    toks = e.shape[2]
    blk = 2 * HD
    steps = width // blk
    row = pl.BlockSpec((rows, blk), lambda j: (0, j))
    return pl.pallas_call(
        attn_bwd_kernel,
        grid=(steps,),
        in_specs=[row, row]
        + kv_specs(kv0, kv1, steps)
        + [row, row, pl.BlockSpec((2, rows, toks), lambda j: (j, 0, 0))],
        out_specs=[row, pl.BlockSpec((2, toks, blk), lambda j: (0, 0, j))],
        out_shape=[
            jax.ShapeDtypeStruct((rows, steps * blk), BF),
            jax.ShapeDtypeStruct((2, toks, steps * blk), BF),
        ],
        scratch_shapes=[pltpu.VMEM((toks, blk), BF)] * 2,
        compiler_params=params(),
        cost_estimate=cost(32 * rows * toks * blk * steps, steps * (4 << 20)),
        name="attn_bwd",
    )(ga, q, kv0, kv1, kv0, kv1, o, r, e)


def put_pieces(me_ref, src, keep_ref, send_ref, index):
    nt, nf = keep_ref.shape[0], keep_ref.shape[1]
    for k in range(nt):
        for f in range(nf):
            at = (f * nt + (me_ref[1] ^ k)) * 2
            keep_ref[(k, f) + index] = src[at + me_ref[2]]
            send_ref[(k, f) + index] = src[at + 1 - me_ref[2]]


def spread_over(n, vec, lanes):
    size = vec.shape[1]
    scale = -(-(1 << 21) // n)
    assert all((i * scale) >> 21 == i // n for i in range(size))
    dev = size // n
    col = lax.broadcasted_iota(jnp.int32, (dev, size), 1)
    mine = ((col * scale) >> 21) == lax.broadcasted_iota(jnp.int32, (dev, size), 0)
    left = jnp.where(mine, jnp.broadcast_to(vec, (dev, size)), 0.0).astype(BF)
    row = lax.broadcasted_iota(jnp.int32, (size, lanes), 0)
    place = row - ((row * scale) >> 21) * n
    hit = place == lax.broadcasted_iota(jnp.int32, (size, lanes), 1)
    return nn(left, jnp.where(hit, 1.0, 0.0).astype(BF))


def dx_kernel(gq_ref, gkv_ref, n0, n1, n2, n3, w_ref, own, *refs):
    *others, vec_ref, total, n_all = refs
    width = w_ref.shape[0]
    step = pl.program_id(0)
    e = nt_dot(gkv_ref[0], w_ref[:, width : 2 * width])
    total[...] = e + nt_dot(gkv_ref[1], w_ref[:, 2 * width :])

    @pl.when(step == 0)
    def _():
        total[...] += nt_dot(gq_ref[...], w_ref[:, 0:width])
        own[...] = total[...]
        vec_ref[...] = jnp.zeros_like(vec_ref)

    for c, n in enumerate((n0, n1, n2, n3)):

        @pl.when(step == c)
        def _():
            n_all[...] = n[...]

    vec_ref[0:1, :] += colsum(total[...] * n_all[...].astype(F32))
    vec_ref[1:2, :] += colsum(total[...])
    for c, out in enumerate(others):

        @pl.when(step == c + 1)
        def _():
            out[...] = total[...].astype(BF)


def dx_call(gq, gkv, ns, w):
    rows, width = gq.shape
    shape = jax.ShapeDtypeStruct
    return pl.pallas_call(
        dx_kernel,
        grid=(4,),
        in_specs=[full(gq.shape), pl.BlockSpec((2, rows, width), lambda j: (0, j, 0))]
        + [full((rows, width))] * 4
        + [full(w.shape)],
        out_specs=[full((rows, width))] * 4 + [full((2, width))],
        out_shape=[shape((rows, width), F32)]
        + [shape((rows, width), BF)] * 3
        + [shape((2, width), F32)],
        scratch_shapes=[pltpu.VMEM((rows, width), F32), pltpu.VMEM((rows, width), BF)],
        compiler_params=params(),
        cost_estimate=cost(16 * rows * width * width, 12 << 20),
        name="dx",
    )(gq, gkv, *ns, w)


def mid_kernel(nf, nt, fast, me_ref, *refs):
    refs = list(refs)
    if fast:
        *refs, down, up, side, sems = refs
    xms, cms, refs = refs[:nf], refs[nf : 2 * nf], refs[2 * nf :]
    att_ref, att5_ref, x5_ref, c5_ref, wo_ref, vec_in = refs[:6]
    wu_ref, wd_ref, outs_ref, out5_ref, gm_ref, ga_ref, ga5_ref = refs[6:13]
    *grads, vec_ref, gbu_ref, att, cot, mid, hat, rst, two, acc, gn2 = refs[13:]
    step = pl.program_id(0)
    r5, width = x5_ref.shape
    rm = nf * r5
    half = r5 // 2
    low = low_lanes(half)
    pairs = width // (2 * HD)

    @pl.when(step == 0)
    def _():
        att[0:rm, :] = att_ref[...]
        for pair in range(pairs):
            lanes = slice(pair * 2 * HD, (pair + 1) * 2 * HD)
            even = att5_ref[slot_of(2 * pair, nf, nt)].astype(F32)
            odd = att5_ref[slot_of(2 * pair + 1, nf, nt)].astype(F32)
            top = jnp.where(low, even, swap_halves(odd))
            bot = jnp.where(low, swap_halves(even), odd)
            att[rm : rm + r5, lanes] = jnp.concatenate([top, bot], axis=0).astype(BF)
        for k in range(nf):
            cot[k * r5 : (k + 1) * r5, :] = cms[k][...]
        cot[rm : rm + r5, :] = c5_ref[...]
        mid[...] = nn(att[...], wo_ref[...]) + row_of(vec_in, BIAS_OUT)
        for k in range(nf):
            mid[k * r5 : (k + 1) * r5, :] += xms[k][...].astype(F32)
        mid[rm : rm + r5, :] += x5_ref[...].astype(F32)
        n, rstd = normalize(mid[...])
        hat[...] = n
        rst[...] = rstd
        two[...] = (n * row_of(vec_in, GAIN2) + row_of(vec_in, SHIFT2)).astype(BF)
        acc[...] = mid[...] + row_of(vec_in, BIAS_DOWN)
        gn2[...] = jnp.zeros_like(gn2)

    pre = nn(two[...], wu_ref[...]) + vec_in[pl.ds(BIAS_UP + step, 1), :]
    cdf = 0.5 * (1.0 + lax.erf(pre * (0.5**0.5)))
    slope = cdf + pre * (jnp.exp(-0.5 * pre * pre) * 0.3989422804014327)
    act = (pre * cdf).astype(BF)
    acc[...] += nn(act, wd_ref[...])
    dwd = tn_dot(act, cot[...]).astype(BF)
    if fast:
        pd, pu = down.shape[2], up.shape[2]
        owners = down.shape[1]

        def copies(j):
            to_down = grads[0].at[:, j, pl.ds(0, pd), :]
            return [pltpu.make_async_copy(down.at[j], to_down, sems.at[0, j])] + [
                pltpu.make_async_copy(
                    up.at[j, pl.ds(f * owners, owners)],
                    grads[0].at[:, f, pl.ds(pd + j * pu, pu), :],
                    sems.at[1 + f, j],
                )
                for f in range(nf)
            ]

        down[step] = dwd.reshape(down.shape[1:])
    else:
        grads[0][...] = dwd
    gpre = (nt_dot(cot[...], wd_ref[...]) * slope).astype(BF)
    gbu_ref[...] = colsum(gpre.astype(F32))
    dwu = tn_dot(two[...], gpre)
    if fast:
        up[step] = dwu.reshape(up.shape[1:]).astype(BF)
        for copy in copies(step):
            copy.start()
    else:
        grads[1][...] = dwu.astype(BF)
    gn2[...] += nt_dot(gpre, wu_ref[...])

    @pl.when(step == pl.num_programs(0) - 1)
    def _():
        for k in range(nf):
            outs_ref[me_ref[0] ^ k] = acc[k * r5 : (k + 1) * r5, :].astype(BF)
        out5_ref[...] = acc[rm : rm + r5, :]
        e = gn2[...]
        n = hat[...]
        c = cot[...].astype(F32)
        gmid = c + norm_back(e, n, rst[...], row_of(vec_in, GAIN2))
        gm_ref[...] = gmid
        branch = gmid.astype(BF)
        vec_ref[0:1, :] = colsum(branch.astype(F32))
        vec_ref[1:2, :] = colsum(e * n)
        vec_ref[2:3, :] = colsum(e)
        vec_ref[3:4, :] = colsum(c)
        dwo = tn_dot(att[...], branch)
        if fast:
            side[...] = dwo.reshape(side.shape).astype(BF)
            put_pieces(me_ref, side, grads[1], grads[2], ())
        else:
            grads[2][...] = dwo.astype(BF)
        gatt = nt_dot(branch, wo_ref[...])
        ga_ref[...] = gatt[0:rm].astype(BF)
        ga5_ref[...] = jnp.zeros_like(ga5_ref)
        for pair in range(pairs):
            lanes = slice(pair * 2 * HD, (pair + 1) * 2 * HD)
            top, bot = gatt[rm : rm + half, lanes], gatt[rm + half : rm + r5, lanes]
            even = jnp.where(low, top, swap_halves(bot))
            odd = jnp.where(low, swap_halves(top), bot)
            ga5_ref[slot_of(2 * pair, nf, nt)] = even.astype(BF)
            ga5_ref[slot_of(2 * pair + 1, nf, nt)] = odd.astype(BF)
        if fast:
            for j in range(nf):
                for copy in copies(j):
                    copy.wait()


def mid_call(nf, nt, fast, me, xms, cms, att, att5, x5, c5, wo, vecs, wu, wd):
    _, r5, width = x5.shape
    rm = nf * r5
    rows = rm + r5
    ff = wu.shape[1]
    blk = ff // nf
    shape = jax.ShapeDtypeStruct
    if fast:
        dev = nf * nt * 2
        pd, pu = ff // dev, width // dev
        oshape = (nt, nf, pu, width)
        gspecs = [pl.BlockSpec(memory_space=pl.ANY)] + [full(oshape)] * 2
        gshapes = [shape((nt * 2, nf, pd + nf * pu, width), BF)] + [shape(oshape, BF)] * 2
        extra = [
            pltpu.VMEM((nf, nt * 2, pd, width), BF),
            pltpu.VMEM((nf, dev, pu, width), BF),
            pltpu.VMEM((dev, pu, width), BF),
            pltpu.SemaphoreType.DMA((1 + nf, nf)),
        ]
    else:
        gspecs = [
            pl.BlockSpec((blk, width), lambda j, *_: (j, 0)),
            pl.BlockSpec((width, blk), lambda j, *_: (0, j)),
            full((width, width)),
        ]
        gshapes = [shape((ff, width), BF), shape((width, ff), BF), shape((width, width), BF)]
        extra = []
    ins = [*xms, *cms, att, att5, x5, c5, wo, vecs]
    return pl.pallas_call(
        functools.partial(mid_kernel, nf, nt, fast),
        grid_spec=pltpu.PrefetchScalarGridSpec(
            num_scalar_prefetch=1,
            grid=(nf,),
            in_specs=[clip_at(x, nf) if x.ndim == 3 and x.shape[0] == nf + 1 else full(x.shape) for x in ins]
            + [
                pl.BlockSpec((width, blk), lambda j, *_: (0, j)),
                pl.BlockSpec((blk, width), lambda j, *_: (j, 0)),
            ],
            out_specs=[
                full((nf, r5, width)),
                full((r5, width)),
                full((rows, width)),
                full((rm, width)),
                full(att5.shape),
            ]
            + gspecs
            + [full((4, width)), pl.BlockSpec((1, blk), lambda j, *_: (0, j))],
            scratch_shapes=[
                pltpu.VMEM((rows, width), BF),
                pltpu.VMEM((rows, width), BF),
                pltpu.VMEM((rows, width), F32),
                pltpu.VMEM((rows, width), F32),
                pltpu.VMEM((rows, 1), F32),
                pltpu.VMEM((rows, width), BF),
                pltpu.VMEM((rows, width), F32),
                pltpu.VMEM((rows, width), F32),
            ]
            + extra,
        ),
        out_shape=[
            shape((nf, r5, width), BF),
            shape((r5, width), F32),
            shape((rows, width), F32),
            shape((rm, width), BF),
            shape(att5.shape, BF),
        ]
        + gshapes
        + [shape((4, width), F32), shape((1, ff), F32)],
        compiler_params=params(),
        cost_estimate=cost(12 * rows * width * ff + 6 * rows * width * width, 24 << 20),
        name="mid",
    )(me, *ins, wu, wd)


def tail5_kernel(nf, nt, fast, *refs):
    refs = list(refs)
    if fast:
        me_ref = refs.pop(0)
        *refs, side, small = refs
    (gq_ref, gkv_ref), ns, refs = refs[:2], refs[2 : 2 + nt], refs[2 + nt :]
    g_ref, n5_ref, x5_ref, gm_ref, w_ref, in_ref, vm_ref, v2_ref, gbu_ref = refs[:9]
    (*dwo, gin_ref, vec_ref, dx, x_all, g_all, sums) = refs[9:]
    step = pl.program_id(0)
    r5, width = x5_ref.shape
    half = r5 // 2
    low = low_lanes(half)
    rows = ns[0].shape[0]

    @pl.when(step == 0)
    def _():
        x_all[0:r5, :] = n5_ref[...]
        for c in range(nt):
            x_all[r5 + c * rows : r5 + (c + 1) * rows, :] = ns[c][...]
        dx[...] = jnp.zeros_like(dx)

    for pair in range(width // (2 * HD)):
        lanes = slice(pair * 2 * HD, (pair + 1) * 2 * HD)
        even = g_ref[slot_of(2 * pair, nf, nt)].astype(F32)
        odd = g_ref[slot_of(2 * pair + 1, nf, nt)].astype(F32)
        top = jnp.where(low, even, swap_halves(odd))
        bot = jnp.where(low, swap_halves(even), odd)
        g_all[0:r5, lanes] = jnp.concatenate([top, bot], axis=0).astype(BF)
    dx[...] += nt_dot(g_all[0:r5, :], w_ref[...])

    def finish(end):
        g = g_all[0:end, :]
        sums[pl.ds(step, 1), :] = colsum(g.astype(F32))
        dw = tn_dot(x_all[0:end, :], g)
        if fast:
            side[...] = dw.reshape(side.shape).astype(BF)
        else:
            dwo[0][...] = dw.astype(BF)

    @pl.when(step < 2)
    def _():
        g_all[r5:, :] = gkv_ref[0]
        finish(r5 + nt * rows)

    @pl.when(step == 2)
    def _():
        g_all[r5 : r5 + rows, :] = gq_ref[...]
        finish(r5 + rows)
        n, rstd = normalize(x5_ref[...].astype(F32))
        e = dx[...]
        gin_ref[...] = gm_ref[...] + norm_back(e, n, rstd, row_of(in_ref, GAIN1))
        main = vm_ref[0:1, :] - row_of(in_ref, SHIFT1) * vm_ref[1:2, :]
        vec_ref[0:1, :] = main / row_of(in_ref, GAIN1) + colsum(e * n)
        vec_ref[1:2, :] = vm_ref[1:2, :] + colsum(e)
        vec_ref[2:6, :] = v2_ref[...]
        vec_ref[6:7, :] = sums[2:3, :]
        vec_ref[7:8, :] = sums[1:2, :]
        if fast:
            per = width // small.shape[0]
            lanes = width // 4
            total = 0.0
            for i in range(8):
                part = spread_over(per, vec_ref[i : i + 1, :], 2 * HD)
                part = jnp.concatenate([part, jnp.zeros((part.shape[0], lanes - 2 * HD), F32)], 1)
                total += pltpu.roll(part, i * per, 1) if i else part
            wide = spread_over(gbu_ref.shape[1] // small.shape[0], gbu_ref[...], 2 * HD)
            rest = width - lanes - 2 * HD
            line = jnp.concatenate([total, wide, jnp.zeros((wide.shape[0], rest), F32)], 1)
            small[...] = jnp.broadcast_to(line[:, None, :], small.shape).astype(BF)
            keep, send = (x.at[:, :, side.shape[1] :, :] for x in dwo[0:2])
            put_pieces(me_ref, small, keep, send, ())

    if fast:
        for i in range(3):

            @pl.when(step == (i + 2) % 3)
            def _():
                keep, send = (x.at[:, :, 0 : side.shape[1], :] for x in dwo[2 * i : 2 * i + 2])
                put_pieces(me_ref, side, keep, send, ())


def tail5_call(nf, nt, fast, me, gq, gkv, ns, g, n5, x5, gm, w, vecs, vm, v2, gbu):
    _, r5, width = x5.shape
    at = gm.shape[0] // r5 - 1
    toks = gkv.shape[1]
    part = lambda j: (j + 1) % 3
    bshape = jax.ShapeDtypeStruct
    if fast:
        pu = width // (nf * nt * 2)
        heights = (pu + 8,) * 2 + (pu,) * 4
        wspecs = [full((nt, nf, n, width)) for n in heights]
        wshapes = [bshape((nt, nf, n, width), BF) for n in heights]
        extra = [pltpu.VMEM((nf * nt * 2, n, width), BF) for n in (pu, 8)]
    else:
        wspecs = [pl.BlockSpec((width, width), lambda j, *_: (0, part(j)))]
        wshapes = [bshape((width, 3 * width), BF)]
        extra = []
    return pl.pallas_call(
        functools.partial(tail5_kernel, nf, nt, fast),
        grid_spec=pltpu.PrefetchScalarGridSpec(
            num_scalar_prefetch=int(fast),
            grid=(3,),
            in_specs=[full(gq.shape)]
            + [pl.BlockSpec((1, toks, width), lambda j, *_: (jnp.minimum(j, 1), 0, 0))]
            + [full(x.shape) for x in ns]
            + [
                pl.BlockSpec((g.shape[0], r5 // 2, 2 * HD), lambda j, *_: (0, 0, part(j))),
                full(n5.shape),
                clip_at(x5, nf),
                pl.BlockSpec((r5, width), lambda j, *_: (at, 0)),
                pl.BlockSpec((width, width), lambda j, *_: (0, part(j))),
            ]
            + [full(x.shape) for x in (vecs, vm, v2, gbu)],
            out_specs=wspecs + [full((r5, width)), full((8, width))],
            scratch_shapes=[
                pltpu.VMEM((r5, width), F32),
                pltpu.VMEM((r5 + toks, width), BF),
                pltpu.VMEM((r5 + toks, width), BF),
                pltpu.VMEM((8, width), F32),
            ]
            + extra,
        ),
        out_shape=wshapes + [bshape((r5, width), F32), bshape((8, width), F32)],
        compiler_params=params(),
        cost_estimate=cost(4 * r5 * width * width * 3 + 4 * width * width * toks, 16 << 20),
        name="tail_shared",
    )(*([me] if fast else []), gq, gkv, *ns, g, n5, x5, gm, w, vecs, vm, v2, gbu)


def tail_kernel(nf, nt, *refs):
    dxs, xs, refs = refs[:nt], refs[nt : nt + nf], refs[nt + nf :]
    gm_ref, vec_ref, *gins = refs
    rows = xs[0].shape[0]
    for k in range(nf):
        at = slice(k * rows, (k + 1) * rows)
        e = dxs[0][at, :]
        for c in range(1, nt):
            e = e + dxs[c][at, :].astype(F32)
        n, rstd = normalize(xs[k][...].astype(F32))
        gins[k][...] = (gm_ref[at, :] + norm_back(e, n, rstd, row_of(vec_ref, GAIN1))).astype(BF)


def tail_call(dxs, xs, gm, vecs):
    rows, width = xs[0].shape
    nf, nt = len(xs), len(dxs)
    return pl.pallas_call(
        functools.partial(tail_kernel, nf, nt),
        grid=(1,),
        in_specs=[full((nf * rows, width))] * nt
        + [full((rows, width))] * nf
        + [full((nf * rows, width)), full(vecs.shape)],
        out_specs=[full((rows, width))] * nf,
        out_shape=[jax.ShapeDtypeStruct((rows, width), BF)] * nf,
        compiler_params=params(),
        cost_estimate=cost(30 * nf * rows * width, 6 << 20, 1000),
        name="tail",
    )(*dxs, *xs, gm, vecs)


def pair_sum_kernel(count, *refs):
    ins, (dx, d0, d2, uy, u0, u1) = refs[: 4 * count], refs[4 * count :]
    outs = ((d0, dx.at[0], d2, dx.at[1]), (u0, u1, uy.at[0], uy.at[1]))
    for side in range(2):
        pairs = ins[2 * count * side : 2 * count * (side + 1)]
        at = 0
        for keep, got in zip(pairs[0::2], pairs[1::2]):
            rows = keep.shape[2]
            for k in range(4):
                total = (keep[k, 0].astype(F32) + got[k, 0].astype(F32)).astype(BF)
                outs[side][k][0, at : at + rows, :] = total
            at += rows


def pair_sum(trios):
    _, blocks, _, width = trios[0][0].shape
    steps = blocks // 2
    rows = sum(x[0].shape[2] for x in trios)
    specs, args = [], []
    for first in (0, steps):
        for keep, got in trios:
            spec = pl.BlockSpec((4, 1) + keep.shape[2:], lambda j, f=first: (0, j + f, 0, 0))
            specs += [spec, spec]
            args += [keep, got]
    two = pl.BlockSpec((2, 1, rows, width), lambda j: (0, j, 0, 0))
    one = pl.BlockSpec((1, rows, width), lambda j: (j, 0, 0))
    shape = jax.ShapeDtypeStruct
    return pl.pallas_call(
        functools.partial(pair_sum_kernel, len(trios)),
        grid=(steps,),
        in_specs=specs,
        out_specs=[two, one, one] * 2,
        out_shape=[
            shape((2, steps, rows, width), BF),
            shape((steps, rows, width), BF),
            shape((steps, rows, width), BF),
        ]
        * 2,
        compiler_params=params(),
        cost_estimate=cost(1 << 20, 8 << 20),
        name="pair_sum",
    )(*args)


def relay_sum_kernel(d2, gx, u1, gy, sd, su):
    sd[...] = (d2[...].astype(F32) + gx[0].astype(F32)).astype(BF)
    su[...] = (u1[...].astype(F32) + gy[0].astype(F32)).astype(BF)


def relay_sum(d2, gx, u1, gy):
    second = lambda x: pl.BlockSpec((1,) + x.shape[1:], lambda *_: (1,) + (0,) * (x.ndim - 1))
    return pl.pallas_call(
        relay_sum_kernel,
        grid=(1,),
        in_specs=[full(d2.shape), second(gx), full(u1.shape), second(gy)],
        out_specs=[full(d2.shape), full(u1.shape)],
        out_shape=[jax.ShapeDtypeStruct(d2.shape, BF), jax.ShapeDtypeStruct(u1.shape, BF)],
        compiler_params=params(),
        cost_estimate=cost(d2.size, 6 * d2.size, 1),
        name="relay_sum",
    )(d2, gx, u1, gy)


def along(axis, k, x):
    return lax.ppermute(x, axis, [(i, i ^ k) for i in range(4)])


def relay_start(dx, uy):
    return along("tm", 1, dx), along("tm", 2, uy)


def relay_end(gx, gy, d2, u1):
    sd, su = relay_sum(d2, gx, u1, gy)
    return along("tm", 2, sd), along("tm", 1, su)


def tm_sum_kernel(nf, lead, me_ref, *refs):
    d0, gx, rd, u0, gy, ru = refs[:6]
    outs, total = refs[6 : 6 + nf], refs[-1]
    half = d0.shape[0]
    for first, own, one, two in ((0, d0, gx, rd), (half, u0, gy, ru)):
        for f in range(half):
            part = own[f].astype(F32) + one[0, f, lead:, :].astype(F32) + two[f, lead:, :].astype(F32)
            total[first + f] = part.astype(BF)
    for k in range(nf):
        outs[k][...] = total[me_ref[0] ^ k]


def tm_sum(nf, me, d0, gx, rd, u0, gy, ru):
    _, rows, width = d0.shape
    first = full((1,) + gx.shape[1:])
    return pl.pallas_call(
        functools.partial(tm_sum_kernel, nf, gx.shape[2] - rows),
        grid_spec=pltpu.PrefetchScalarGridSpec(
            num_scalar_prefetch=1,
            grid=(1,),
            in_specs=[full(d0.shape), first, full(rd.shape)] * 2,
            out_specs=[full((rows, width))] * nf,
            scratch_shapes=[pltpu.VMEM((nf, rows, width), BF)],
        ),
        out_shape=[jax.ShapeDtypeStruct((rows, width), BF)] * nf,
        compiler_params=params(),
        cost_estimate=cost(1 << 20, 5 << 20),
        name="tm_sum",
    )(me, d0, gx, rd, u0, gy, ru)


def last_sum_kernel(nf, places, first_vec, per, *refs):
    parts, outs = refs[:nf], refs[nf:]
    if len(parts[0].shape) == 3:
        parts = [parts[0].at[i] for i in range(parts[0].shape[0])]
    for at, rows, out, col in places:
        lanes = parts[0].shape[1]
        total = parts[0][at : at + rows, :].astype(F32)
        for part in parts[1:]:
            total = total + part[at : at + rows, :].astype(F32)
        if out is None:
            for i in range(8):
                outs[first_vec + i][...] = (pltpu.roll(total, lanes - i * per, 1) if i else total)[0, 0:per]
            outs[first_vec + 8][...] = total[0, lanes // 4 : lanes // 4 + outs[first_vec + 8].shape[0]]
        else:
            outs[out][:, col : col + lanes] = total


def last_sum(parts, places, shapes, first_vec=None, per=None):
    nf = len(parts)
    return pl.pallas_call(
        functools.partial(last_sum_kernel, nf, places, first_vec, per),
        out_shape=[jax.ShapeDtypeStruct(x, F32) for x in shapes],
        compiler_params=pltpu.CompilerParams(vmem_limit_bytes=VMEM_LIMIT),
        cost_estimate=cost(nf * parts[0].size, 2 * nf * parts[0].size, 1),
        name="last_sum",
    )(*parts)


def swap_cores(x):
    return lax.ppermute(x, "grp", [(0, 1), (1, 0)])


def exchange(axis, parts):
    pairs = lambda k: [(i, i ^ k) for i in range(len(parts))]
    return [parts[0]] + [lax.ppermute(parts[k], axis, pairs(k)) for k in range(1, len(parts))]


def tie(x, *deps):
    flat, tree = jax.tree.flatten(x)
    tied = lax.optimization_barrier((flat, deps))[0]
    return jax.tree.unflatten(tree, tied)


def over(axes, x):
    return lax.all_to_all(x, axes, 0, 0)


def local(
    nf,
    nt,
    ng,
    inputs,
    gain_one,
    shift_one,
    w_qkv,
    bias_query,
    bias_value,
    w_out,
    bias_out,
    gain_two,
    shift_two,
    w_up,
    bias_up,
    w_down,
    bias_down,
    cotangent,
):
    _, r, width = inputs.shape
    ff = w_up.shape[1]
    dev = nf * nt * ng
    per = width // dev
    fast = ng == 2 and per % 8 == 0 and ff // nf == width
    me = jnp.stack([lax.axis_index(a) for a in ALL]).astype(jnp.int32)
    both = ("freq", "tm")
    *picked, vecs = pick_call(
        nf,
        me,
        inputs,
        (gain_one, shift_one, bias_query, bias_value, bias_out, gain_two, shift_two, bias_down, bias_up),
    )
    xs = exchange("freq", picked)
    n5, pack5 = q5_call(nf, nt, tie(inputs, picked[0]), vecs, w_qkv)
    got5 = over(both, pack5).reshape(-1, 6 * HD)
    nm = ln_call(tie(xs, pack5), vecs)
    ns = exchange("tm", [nm] * nt)
    kv0 = kv_call([nm], w_qkv, vecs, 100)
    o5, r5, ob5, e5 = attn5_fwd_call(tie(got5, kv0))
    att5 = over(both, ob5.reshape(nf * nt, r // 2, 2 * HD))
    cs = exchange("freq", tie(pick_call(nf, me, tie(cotangent, pack5)), nm))
    kv1 = kv_call(tie(ns[1:], ob5), w_qkv, vecs, 0.01)
    att, o, rr, q, e = attn_fwd_call(nm, w_qkv, vecs, kv0, kv1)
    outs, out5, gm, ga, ga5, *dws, vec, gbu = mid_call(
        nf,
        nt,
        fast,
        me,
        xs,
        cs,
        att,
        att5,
        inputs,
        cotangent,
        w_out,
        vecs,
        w_up,
        w_down,
    )
    pieces = lambda x: x.reshape(nt, nf, -1, width)
    pd = ff // dev
    if fast:
        dff = lax.psum_scatter(
            dws[0].reshape(nt * ng, nf * (pd + nf * per), width),
            ("tm", "grp"),
            scatter_dimension=0,
            tiled=True,
        )
        keep_o, got_o = pieces(dws[1]), pieces(swap_cores(dws[2]))
    got_ga5 = over(both, ga5).reshape(-1, 2 * HD)
    gq, gkv = attn_bwd_call(ga, q, kv0, kv1, o, rr, e)
    g5 = attn5_bwd_call(got5, tie(got_ga5, gq, *([got_o] if fast else [])), o5, r5, e5).reshape(nf * nt, r // 2, 6 * HD)
    *dxs, vec_m = dx_call(tie(gq, g5), gkv, ns, w_qkv)
    dxs = exchange("tm", dxs)
    g5 = over(both, g5)
    *dwqkv, gin5, vec8 = tail5_call(
        nf, nt, fast, me, tie(gq, vec_m), gkv, ns, g5, n5, inputs, gm, w_qkv, vecs, vec_m, vec, gbu
    )
    outs = over("freq", tie(outs, g5))
    gin = tail_call(tie(dxs, vec8), xs, gm, vecs)
    order = gin[0]
    gin = exchange("freq", gin)
    if fast:
        trios = [(dwqkv[i], swap_cores(dwqkv[i + 1])) for i in (0, 2, 4)]
        trios += [(keep_o, got_o)]
        trios[0] = (trios[0][0], tie(trios[0][1], order))
        dxq, d0q, d2q, uyq, u0q, u1q = pair_sum(trios)
        gxq, gyq = relay_start(dxq, uyq)
        sdq, suq = relay_sum(d2q, gxq, u1q, gyq)
        rdq, ruq = along("tm", 2, sdq), along("tm", 1, suq)
        dff = over("freq", tie(dff, dxq).reshape(nf, -1, width))
        sums_q = exchange("freq", tm_sum(nf, me, d0q, gxq, rdq, u0q, gyq, ruq))
        places = [(0, pd, 0, 0)] + [(pd + i * per, per, 1, i * width) for i in range(nf)]
        dwd, dwu = last_sum([dff], places, [(pd, width), (per, ff)])
        places = [(0, per, 0, 0), (per, 8, None, 0), (per + 8, per, 0, width)]
        places += [(2 * per + 8, per, 0, 2 * width), (3 * per + 8, per, 1, 0)]
        shapes = [(per, 3 * width), (per, width)] + [(per,)] * 8 + [(pd,)]
        dwqkv, dwo, *small, gbu = last_sum(sums_q, places, shapes, 2, per)
        piece = lambda i: small[i]
    else:
        dwd, dwu, dwo, dwqkv = (
            lax.psum_scatter(x, ALL, scatter_dimension=0, tiled=True).astype(F32)
            for x in dws + dwqkv
        )
        small = vec8.reshape(8, dev, per).transpose(1, 0, 2).reshape(dev, -1)
        small = jnp.concatenate([small, gbu.reshape(dev, pd)], axis=1)
        small = jnp.sum(over(ALL, small), axis=0)
        piece = lambda i: small[i * per : (i + 1) * per]
        gbu = small[8 * per :]
    block_out = jnp.concatenate([outs.astype(F32), out5[None]], axis=0)
    grad_in = assemble_call(nf, me, gin, gin5)
    return (
        block_out,
        grad_in,
        piece(0),
        piece(1),
        dwqkv,
        piece(6),
        piece(7),
        dwo,
        piece(2),
        piece(3),
        piece(4),
        dwu,
        gbu,
        dwd,
        piece(5),
    )


def solution(mesh):
    tokens = P("grp", ("freq", "tm"), None)
    vec = P(ALL)
    mat = P(ALL, None)
    return jax.shard_map(
        functools.partial(local, mesh.shape["freq"], mesh.shape["tm"], mesh.shape["grp"]),
        mesh=mesh,
        in_specs=(tokens,) + (P(),) * 13 + (tokens,),
        out_specs=(
            tokens,
            tokens,
            vec,
            vec,
            mat,
            vec,
            vec,
            mat,
            vec,
            vec,
            vec,
            mat,
            vec,
            mat,
            vec,
        ),
        check_vma=False,
    )
```

```python
import functools

import jax
import jax.numpy as jnp
from jax import lax
from jax.experimental import pallas as pl
from jax.experimental.pallas import tpu as pltpu
from jax.sharding import PartitionSpec as P

HD = 64
NORM_EPS = 1e-06
BF = jnp.bfloat16
F32 = jnp.float32
ALL = ("freq", "tm", "grp")
VMEM_LIMIT = 60 * 1024 * 1024
SAFE = 50.0
GAIN1, SHIFT1, BIAS_Q, BIAS_V, BIAS_OUT, GAIN2, SHIFT2, BIAS_DOWN, BIAS_UP = range(9)


def row_of(ref, i):
    return ref[i : i + 1, :]


def nn(a, b):
    return lax.dot_general(a, b, (((1,), (0,)), ((), ())), preferred_element_type=F32)


def nt_dot(a, b):
    return lax.dot_general(a, b, (((1,), (1,)), ((), ())), preferred_element_type=F32)


def tn_dot(a, b):
    return lax.dot_general(a, b, (((0,), (0,)), ((), ())), preferred_element_type=F32)


def normalize(x):
    mean = jnp.mean(x, axis=-1, keepdims=True)
    centered = x - mean
    var = jnp.mean(centered * centered, axis=-1, keepdims=True)
    rstd = lax.rsqrt(var + NORM_EPS)
    return centered * rstd, rstd


def norm_back(e, n, rstd, gain):
    eg = e * gain
    return rstd * (
        eg - jnp.mean(eg, axis=-1, keepdims=True) - n * jnp.mean(eg * n, axis=-1, keepdims=True)
    )


def colsum(x):
    return jnp.sum(x, axis=0, keepdims=True)


def low_lanes(rows):
    return lax.broadcasted_iota(jnp.int32, (rows, 2 * HD), 1) < HD


def swap_halves(x):
    return pltpu.roll(x, HD, 1)


def slot_of(head, nf, nt):
    per = -(-(12) // nf)
    return (head // per) * nt + head % per


def params(count=1):
    return pltpu.CompilerParams(
        dimension_semantics=("arbitrary",) * count, vmem_limit_bytes=VMEM_LIMIT
    )


def full(shape):
    return pl.BlockSpec(shape, lambda *_: (0,) * len(shape))


def clip_at(x, i):
    return pl.BlockSpec((None,) + x.shape[1:], lambda *_: (i, 0, 0))


def cost(flops, nbytes, weight=1):
    return pl.CostEstimate(
        flops=int(weight * flops), bytes_accessed=int(weight * nbytes), transcendentals=0
    )


def pick_kernel(nf, count, me_ref, x_ref, c_ref, *refs):
    vecs, outs, cots = refs[:count], refs[count : -nf], refs[-nf:]
    for k in range(nf):
        outs[k][...] = x_ref[me_ref[0] ^ k]
        cots[k][...] = c_ref[me_ref[0] ^ k]
    if count:
        width = x_ref.shape[2]
        for i in range(count - 1):
            outs[nf][i : i + 1, :] = vecs[i][...].reshape(1, width)
        last = vecs[count - 1]
        for i in range(last.shape[0] // width):
            at = count - 1 + i
            outs[nf][at : at + 1, :] = last[i * width : (i + 1) * width].reshape(1, width)


def pick_call(nf, me, x, c, vecs):
    _, rows, width = x.shape
    count = 8 + -(-sum(v.shape[0] for v in vecs) // width) // 8 * 8
    more = [(count, width)] if vecs else []
    return pl.pallas_call(
        functools.partial(pick_kernel, nf, len(vecs)),
        grid_spec=pltpu.PrefetchScalarGridSpec(
            num_scalar_prefetch=1,
            grid=(1,),
            in_specs=[full(x.shape)] * 2 + [full(v.shape) for v in vecs],
            out_specs=[full((rows, width))] * nf
            + [full(y) for y in more]
            + [full((rows, width))] * nf,
        ),
        out_shape=[jax.ShapeDtypeStruct((rows, width), BF)] * nf
        + [jax.ShapeDtypeStruct(y, F32) for y in more]
        + [jax.ShapeDtypeStruct((rows, width), BF)] * nf,
        compiler_params=params(),
        cost_estimate=cost(0, 8 * x.size),
        name="pick",
    )(me, x, c, *vecs)


def assemble_kernel(nf, me_ref, *refs):
    for k in range(nf):
        refs[-1][me_ref[0] ^ k] = refs[k][...].astype(F32)
    refs[-1][nf] = refs[nf][...]


def assemble_call(nf, me, parts, five):
    rows, width = five.shape
    return pl.pallas_call(
        functools.partial(assemble_kernel, nf),
        grid_spec=pltpu.PrefetchScalarGridSpec(
            num_scalar_prefetch=1,
            grid=(1,),
            in_specs=[full((rows, width))] * (nf + 1),
            out_specs=full((nf + 1, rows, width)),
        ),
        out_shape=jax.ShapeDtypeStruct((nf + 1, rows, width), F32),
        compiler_params=params(),
        cost_estimate=cost(0, 8 * (nf + 1) * five.size),
        name="assemble",
    )(me, *parts, five)


def ln_kernel(nf, *refs):
    vec_ref, n_ref = refs[nf:]
    for k in range(nf):
        rows = refs[k].shape[0]
        n, _ = normalize(refs[k][...].astype(F32))
        n = n * row_of(vec_ref, GAIN1) + row_of(vec_ref, SHIFT1)
        n_ref[k * rows : (k + 1) * rows, :] = n.astype(BF)


def ln_call(xs, vecs):
    rows, width = xs[0].shape
    return pl.pallas_call(
        functools.partial(ln_kernel, len(xs)),
        grid=(1,),
        in_specs=[full((rows, width))] * len(xs) + [full(vecs.shape)],
        out_specs=full((len(xs) * rows, width)),
        out_shape=jax.ShapeDtypeStruct((len(xs) * rows, width), BF),
        compiler_params=pltpu.CompilerParams(vmem_limit_bytes=VMEM_LIMIT),
        cost_estimate=cost(len(xs) * rows * width * 10, len(xs) * rows * width * 4, 10000),
        name="ln_one",
    )(*xs, vecs)


def q5_kernel(nf, nt, x_ref, vec_ref, w_ref, n_ref, pack_ref):
    rows, width = x_ref.shape
    half = rows // 2
    hat, _ = normalize(x_ref[...].astype(F32))
    n = (hat * row_of(vec_ref, GAIN1) + row_of(vec_ref, SHIFT1)).astype(BF)
    n_ref[...] = n
    low = low_lanes(half)
    pack_ref[...] = jnp.zeros_like(pack_ref)
    for part in range(3):
        proj = nn(n, w_ref[:, part * width : (part + 1) * width])
        if part == 0:
            proj = (proj + row_of(vec_ref, BIAS_Q)) * (HD**-0.5)
        if part == 2:
            proj = proj + row_of(vec_ref, BIAS_V)
        for pair in range(width // (2 * HD)):
            blk = proj[:, pair * 2 * HD : (pair + 1) * 2 * HD]
            top, bot = blk[:half], blk[half:]
            even = jnp.where(low, top, swap_halves(bot))
            odd = jnp.where(low, swap_halves(top), bot)
            lanes = slice(part * 2 * HD, (part + 1) * 2 * HD)
            pack_ref[slot_of(2 * pair, nf, nt), :, lanes] = even.astype(BF)
            pack_ref[slot_of(2 * pair + 1, nf, nt), :, lanes] = odd.astype(BF)


def q5_call(nf, nt, x, vecs, w):
    _, rows, width = x.shape
    return pl.pallas_call(
        functools.partial(q5_kernel, nf, nt),
        grid=(1,),
        in_specs=[clip_at(x, nf), full(vecs.shape), full(w.shape)],
        out_specs=[full((rows, width)), full((nf * nt, rows // 2, 6 * HD))],
        out_shape=(
            jax.ShapeDtypeStruct((rows, width), BF),
            jax.ShapeDtypeStruct((nf * nt, rows // 2, 6 * HD), BF),
        ),
        compiler_params=pltpu.CompilerParams(vmem_limit_bytes=VMEM_LIMIT),
        cost_estimate=cost(2 * rows * w.size, w.size * 2),
        name="q_shared",
    )(x, vecs, w)


def spread(x):
    rows = x.shape[0]
    low = low_lanes(rows)
    zero = jnp.zeros_like(x)
    return jnp.concatenate([jnp.where(low, x, zero), jnp.where(low, swap_halves(x), zero)], axis=0)


def unspread(x):
    half = x.shape[0] // 2
    return x[:half] + swap_halves(x[half:])


def stack_heads(x):
    low = low_lanes(x.shape[0])
    zero = jnp.zeros_like(x)
    return jnp.concatenate([jnp.where(low, x, zero), jnp.where(low, zero, x)], axis=0)


def plain_block(q, k, v):
    e = jnp.exp(nt_dot(q, k))
    rinv = 1.0 / jnp.sum(e, axis=-1, keepdims=True)
    e = e.astype(BF)
    return e, nn(e, v) * rinv, rinv


def softmax_block(q, k, v):
    s = nt_dot(q, k)
    m = jnp.max(s, axis=-1, keepdims=True)
    e = jnp.exp(s - m)
    total = jnp.sum(e, axis=-1, keepdims=True)
    e = e.astype(BF)
    rinv = 1.0 / total
    return e, nn(e, v) * rinv, rinv


def attn5_fwd_kernel(x_ref, o_ref, r_ref, ob_ref, e_ref, qf, kf, vf, of, rf):
    step = pl.program_id(0)

    @pl.when(step == 0)
    def _():
        for part, dst in enumerate((qf, kf, vf)):
            blk = x_ref[:, part * 2 * HD : (part + 1) * 2 * HD].astype(F32)
            dst[...] = spread(blk).astype(BF)

    rows = e_ref.shape[0]
    at = pl.ds(pl.multiple_of(step * rows, rows), rows)
    e, o, rinv = softmax_block(qf[at, :], kf[...], vf[...])
    e_ref[...] = e
    of[at, :] = o
    rf[at, :] = jnp.where(low_lanes(rows), jnp.broadcast_to(rinv, (rows, 2 * HD)), 0.0)

    @pl.when(step == pl.num_programs(0) - 1)
    def _():
        packed = unspread(of[...])
        o_ref[...] = packed
        ob_ref[...] = packed.astype(BF)
        r_ref[...] = unspread(rf[...])


def attn5_fwd_call(x):
    rows = x.shape[0]
    toks = 2 * rows
    shape = jax.ShapeDtypeStruct
    return pl.pallas_call(
        attn5_fwd_kernel,
        grid=(2,),
        in_specs=[full(x.shape)],
        out_specs=[full((rows, 2 * HD))] * 3 + [pl.BlockSpec((toks // 2, toks), lambda j: (j, 0))],
        out_shape=(
            shape((rows, 2 * HD), F32),
            shape((rows, 2 * HD), F32),
            shape((rows, 2 * HD), BF),
            shape((toks, toks), BF),
        ),
        scratch_shapes=[pltpu.VMEM((toks, 2 * HD), BF)] * 3 + [pltpu.VMEM((toks, 2 * HD), F32)] * 2,
        compiler_params=params(),
        cost_estimate=cost(4 * 4 * toks * toks * 2 * HD, toks * toks * 2),
        name="attn_shared_fwd",
    )(x)


def attn5_bwd_kernel(x_ref, ga_ref, o_ref, r_ref, e_ref, out_ref, qf, kf, vf, gf, inn, dq, dk, dv):
    step = pl.program_id(0)

    @pl.when(step == 0)
    def _():
        for part, dst in enumerate((qf, kf, vf)):
            blk = x_ref[:, part * 2 * HD : (part + 1) * 2 * HD].astype(F32)
            dst[...] = spread(blk).astype(BF)
        g = ga_ref[...].astype(F32) * r_ref[...]
        gs = spread(g)
        gf[...] = gs.astype(BF)
        inn[...] = jnp.sum(gs * spread(o_ref[...]), axis=-1, keepdims=True)
        dk[...] = jnp.zeros_like(dk)
        dv[...] = jnp.zeros_like(dv)

    rows = e_ref.shape[0]
    at = pl.ds(pl.multiple_of(step * rows, rows), rows)
    e = e_ref[...]
    gb = gf[at, :]
    dp = nt_dot(gb, vf[...])
    ds = (e.astype(F32) * (dp - inn[at, :])).astype(BF)
    dq[at, :] = nn(ds, kf[...]) * (HD**-0.5)
    dk[...] += tn_dot(ds, qf[at, :])
    dv[...] += tn_dot(e, gb)

    @pl.when(step == pl.num_programs(0) - 1)
    def _():
        for part, src in enumerate((dq, dk, dv)):
            out_ref[:, part * 2 * HD : (part + 1) * 2 * HD] = unspread(src[...]).astype(BF)


def attn5_bwd_call(x, ga, o, r, e):
    rows = x.shape[0]
    toks = 2 * rows
    return pl.pallas_call(
        attn5_bwd_kernel,
        grid=(4,),
        in_specs=[full(y.shape) for y in (x, ga, o, r)]
        + [pl.BlockSpec((toks // 4, toks), lambda j: (j, 0))],
        out_specs=full((rows, 6 * HD)),
        out_shape=jax.ShapeDtypeStruct((rows, 6 * HD), BF),
        scratch_shapes=[pltpu.VMEM((toks, 2 * HD), BF)] * 4
        + [pltpu.VMEM((toks, 1), F32)]
        + [pltpu.VMEM((toks, 2 * HD), F32)] * 3,
        compiler_params=params(),
        cost_estimate=cost(8 * 4 * toks * toks * 2 * HD, toks * toks * 2),
        name="attn_shared_bwd",
    )(x, ga, o, r, e)


def attn_fwd_kernel(nt, *refs):
    ns, (wq, wk, wv, vec_ref, att_ref, o_ref, r_ref, q_ref, kv_ref, e_ref, x_all, w_kv, qs, os, rs) = refs[:nt], refs[nt:]
    rows = ns[0].shape[0]

    @pl.when(pl.program_id(0) == 0)
    def _():
        for c in range(nt):
            x_all[c * rows : (c + 1) * rows, :] = ns[c][...]

    lanes = 2 * HD
    w_kv[:, 0:lanes] = wk[...]
    w_kv[:, lanes:] = wv[...]
    kv = nn(x_all[...], w_kv[...])
    kv_ref[0] = kv[:, 0:lanes].astype(BF)
    kv_ref[1] = (kv[:, lanes:] + row_of(vec_ref, BIAS_V)).astype(BF)
    q = ((nn(x_all[0:rows, :], wq[...]) + row_of(vec_ref, BIAS_Q)) * (HD**-0.5)).astype(BF)
    q_ref[...] = q
    low = low_lanes(rows)
    weight = jnp.abs(q.astype(F32)) * jnp.max(jnp.abs(kv_ref[0].astype(F32)), axis=0, keepdims=True)
    left = jnp.sum(jnp.where(low, weight, 0.0), axis=-1, keepdims=True)
    right = jnp.sum(jnp.where(low, 0.0, weight), axis=-1, keepdims=True)
    small = jnp.max(jnp.maximum(left, right)) < SAFE

    def put(o, r0, r1):
        o_ref[...] = o
        att_ref[...] = o.astype(BF)
        r_ref[...] = jnp.where(
            low, jnp.broadcast_to(r0, (rows, lanes)), jnp.broadcast_to(r1, (rows, lanes))
        )

    @pl.when(small)
    def _():
        zero = jnp.zeros_like(q)
        k, v = kv_ref[0], kv_ref[1]
        e0, o0, r0 = plain_block(jnp.where(low, q, zero), k, v)
        e_ref[0] = e0
        e1, o1, r1 = plain_block(jnp.where(low, zero, q), k, v)
        e_ref[1] = e1
        put(jnp.where(low, o0, o1), r0, r1)

    @pl.when(jnp.logical_not(small))
    def _():
        qs[...] = stack_heads(q)
        part = 32

        def body(i, carry):
            at = pl.ds(pl.multiple_of(i * part, part), part)
            e, o, rinv = softmax_block(qs[at, :], kv_ref[0], kv_ref[1])
            side = i // (rows // part)
            e_ref[side, pl.ds(pl.multiple_of((i - side * (rows // part)) * part, part), part), :] = e
            os[at, :] = o
            rs[at, :] = rinv
            return carry

        lax.fori_loop(0, 2 * rows // part, body, 0)
        put(jnp.where(low, os[0:rows, :], os[rows:, :]), rs[0:rows, :], rs[rows:, :])


def attn_fwd_call(ns, w, vecs):
    rows, width = ns[0].shape
    nt = len(ns)
    toks = nt * rows
    blk = 2 * HD
    pairs = width // blk
    row = pl.BlockSpec((rows, blk), lambda j: (0, j))
    shape = jax.ShapeDtypeStruct
    return pl.pallas_call(
        functools.partial(attn_fwd_kernel, nt),
        grid=(pairs,),
        in_specs=[full((rows, width))] * nt
        + [pl.BlockSpec((width, blk), lambda j, p=p: (0, p * pairs + j)) for p in range(3)]
        + [pl.BlockSpec((8, blk), lambda j: (0, j))],
        out_specs=[row] * 4
        + [pl.BlockSpec((2, toks, blk), lambda j: (0, 0, j))]
        + [pl.BlockSpec((2, rows, toks), lambda j: (j, 0, 0))],
        out_shape=(
            shape((rows, width), BF),
            shape((rows, width), F32),
            shape((rows, width), F32),
            shape((rows, width), BF),
            shape((2, toks, width), BF),
            shape((width // HD, rows, toks), BF),
        ),
        scratch_shapes=[
            pltpu.VMEM((toks, width), BF),
            pltpu.VMEM((width, 2 * blk), BF),
            pltpu.VMEM((2 * rows, blk), BF),
            pltpu.VMEM((2 * rows, blk), F32),
            pltpu.VMEM((2 * rows, 1), F32),
        ],
        compiler_params=params(),
        cost_estimate=cost(16 * rows * toks * width, 20 << 20, 0.01),
        name="attn_fwd",
    )(*ns, w, w, w, vecs)


def attn_bwd_kernel(ga_ref, q_ref, kv_ref, o_ref, r_ref, e_ref, gq_ref, gkv_ref):
    rows = q_ref.shape[0]
    low = low_lanes(rows)
    stack = stack_heads
    g = ga_ref[...].astype(F32) * r_ref[...]
    inner = jnp.sum(stack(g * o_ref[...]), axis=-1, keepdims=True)
    gs, qs = stack(g.astype(BF)), stack(q_ref[...])
    e = e_ref[...].reshape(2 * rows, e_ref.shape[2])
    dp = nt_dot(gs, kv_ref[1])
    ds = (e.astype(F32) * (dp - inner)).astype(BF)
    dq = nn(ds, kv_ref[0])
    gq_ref[...] = (jnp.where(low, dq[:rows], dq[rows:]) * (HD**-0.5)).astype(BF)
    gkv_ref[0] = tn_dot(ds, qs).astype(BF)
    gkv_ref[1] = tn_dot(e, gs).astype(BF)


def attn_bwd_call(ga, q, kv, o, r, e):
    rows, width = q.shape
    toks = e.shape[2]
    blk = 2 * HD
    row = pl.BlockSpec((rows, blk), lambda j: (0, j))
    both = pl.BlockSpec((2, toks, blk), lambda j: (0, 0, j))
    return pl.pallas_call(
        attn_bwd_kernel,
        grid=(width // blk,),
        in_specs=[row, row, both, row, row, pl.BlockSpec((2, rows, toks), lambda j: (j, 0, 0))],
        out_specs=[row, both],
        out_shape=[
            jax.ShapeDtypeStruct((rows, width), BF),
            jax.ShapeDtypeStruct((2, toks, width), BF),
        ],
        compiler_params=params(),
        cost_estimate=cost(32 * rows * toks * width, 24 << 20),
        name="attn_bwd",
    )(ga, q, kv, o, r, e)


def put_pieces(me_ref, src, keep_ref, send_ref, index):
    nt, nf = keep_ref.shape[0], keep_ref.shape[1]
    for k in range(nt):
        for f in range(nf):
            at = (f * nt + (me_ref[1] ^ k)) * 2
            keep_ref[(k, f) + index] = src[at + me_ref[2]]
            send_ref[(k, f) + index] = src[at + 1 - me_ref[2]]


def spread_over(n, vec, lanes):
    size = vec.shape[1]
    scale = -(-(1 << 21) // n)
    assert all((i * scale) >> 21 == i // n for i in range(size))
    dev = size // n
    col = lax.broadcasted_iota(jnp.int32, (dev, size), 1)
    mine = ((col * scale) >> 21) == lax.broadcasted_iota(jnp.int32, (dev, size), 0)
    left = jnp.where(mine, jnp.broadcast_to(vec, (dev, size)), 0.0).astype(BF)
    row = lax.broadcasted_iota(jnp.int32, (size, lanes), 0)
    place = row - ((row * scale) >> 21) * n
    hit = place == lax.broadcasted_iota(jnp.int32, (size, lanes), 1)
    return nn(left, jnp.where(hit, 1.0, 0.0).astype(BF))


def dx_kernel(gq_ref, gkv_ref, n0, n1, n2, n3, w_ref, own, *refs):
    *others, vec_ref, total, n_all = refs
    width = w_ref.shape[0]
    step = pl.program_id(0)
    e = nt_dot(gkv_ref[0], w_ref[:, width : 2 * width])
    total[...] = e + nt_dot(gkv_ref[1], w_ref[:, 2 * width :])

    @pl.when(step == 0)
    def _():
        total[...] += nt_dot(gq_ref[...], w_ref[:, 0:width])
        own[...] = total[...]
        vec_ref[...] = jnp.zeros_like(vec_ref)

    for c, n in enumerate((n0, n1, n2, n3)):

        @pl.when(step == c)
        def _():
            n_all[...] = n[...]

    vec_ref[0:1, :] += colsum(total[...] * n_all[...].astype(F32))
    vec_ref[1:2, :] += colsum(total[...])
    for c, out in enumerate(others):

        @pl.when(step == c + 1)
        def _():
            out[...] = total[...].astype(BF)


def dx_call(gq, gkv, ns, w):
    rows, width = gq.shape
    shape = jax.ShapeDtypeStruct
    return pl.pallas_call(
        dx_kernel,
        grid=(4,),
        in_specs=[full(gq.shape), pl.BlockSpec((2, rows, width), lambda j: (0, j, 0))]
        + [full((rows, width))] * 4
        + [full(w.shape)],
        out_specs=[full((rows, width))] * 4 + [full((2, width))],
        out_shape=[shape((rows, width), F32)]
        + [shape((rows, width), BF)] * 3
        + [shape((2, width), F32)],
        scratch_shapes=[pltpu.VMEM((rows, width), F32), pltpu.VMEM((rows, width), BF)],
        compiler_params=params(),
        cost_estimate=cost(16 * rows * width * width, 12 << 20),
        name="dx",
    )(gq, gkv, *ns, w)


def mid_kernel(nf, nt, fast, me_ref, *refs):
    refs = list(refs)
    if fast:
        *refs, down, up, side, sems = refs
    xms, cms, refs = refs[:nf], refs[nf : 2 * nf], refs[2 * nf :]
    att_ref, att5_ref, x5_ref, c5_ref, wo_ref, vec_in = refs[:6]
    wu_ref, wd_ref, outs_ref, out5_ref, gm_ref, ga_ref, ga5_ref = refs[6:13]
    *grads, vec_ref, gbu_ref, att, cot, mid, hat, rst, two, acc, gn2 = refs[13:]
    step = pl.program_id(0)
    r5, width = x5_ref.shape
    rm = nf * r5
    half = r5 // 2
    low = low_lanes(half)
    pairs = width // (2 * HD)

    @pl.when(step == 0)
    def _():
        att[0:rm, :] = att_ref[...]
        for pair in range(pairs):
            lanes = slice(pair * 2 * HD, (pair + 1) * 2 * HD)
            even = att5_ref[slot_of(2 * pair, nf, nt)].astype(F32)
            odd = att5_ref[slot_of(2 * pair + 1, nf, nt)].astype(F32)
            top = jnp.where(low, even, swap_halves(odd))
            bot = jnp.where(low, swap_halves(even), odd)
            att[rm : rm + r5, lanes] = jnp.concatenate([top, bot], axis=0).astype(BF)
        for k in range(nf):
            cot[k * r5 : (k + 1) * r5, :] = cms[k][...]
        cot[rm : rm + r5, :] = c5_ref[...]
        mid[...] = nn(att[...], wo_ref[...]) + row_of(vec_in, BIAS_OUT)
        for k in range(nf):
            mid[k * r5 : (k + 1) * r5, :] += xms[k][...].astype(F32)
        mid[rm : rm + r5, :] += x5_ref[...].astype(F32)
        n, rstd = normalize(mid[...])
        hat[...] = n
        rst[...] = rstd
        two[...] = (n * row_of(vec_in, GAIN2) + row_of(vec_in, SHIFT2)).astype(BF)
        acc[...] = mid[...] + row_of(vec_in, BIAS_DOWN)
        gn2[...] = jnp.zeros_like(gn2)

    pre = nn(two[...], wu_ref[...]) + vec_in[pl.ds(BIAS_UP + step, 1), :]
    cdf = 0.5 * (1.0 + lax.erf(pre * (0.5**0.5)))
    slope = cdf + pre * (jnp.exp(-0.5 * pre * pre) * 0.3989422804014327)
    act = (pre * cdf).astype(BF)
    acc[...] += nn(act, wd_ref[...])
    dwd = tn_dot(act, cot[...]).astype(BF)
    if fast:
        pd, pu = down.shape[2], up.shape[2]
        owners = down.shape[1]

        def copies(j):
            to_down = grads[0].at[:, j, pl.ds(0, pd), :]
            return [pltpu.make_async_copy(down.at[j], to_down, sems.at[0, j])] + [
                pltpu.make_async_copy(
                    up.at[j, pl.ds(f * owners, owners)],
                    grads[0].at[:, f, pl.ds(pd + j * pu, pu), :],
                    sems.at[1 + f, j],
                )
                for f in range(nf)
            ]

        down[step] = dwd.reshape(down.shape[1:])
    else:
        grads[0][...] = dwd
    gpre = (nt_dot(cot[...], wd_ref[...]) * slope).astype(BF)
    gbu_ref[...] = colsum(gpre.astype(F32))
    dwu = tn_dot(two[...], gpre)
    if fast:
        up[step] = dwu.reshape(up.shape[1:]).astype(BF)
        for copy in copies(step):
            copy.start()
    else:
        grads[1][...] = dwu.astype(BF)
    gn2[...] += nt_dot(gpre, wu_ref[...])

    @pl.when(step == pl.num_programs(0) - 1)
    def _():
        for k in range(nf):
            outs_ref[me_ref[0] ^ k] = acc[k * r5 : (k + 1) * r5, :].astype(BF)
        out5_ref[...] = acc[rm : rm + r5, :]
        e = gn2[...]
        n = hat[...]
        c = cot[...].astype(F32)
        gmid = c + norm_back(e, n, rst[...], row_of(vec_in, GAIN2))
        gm_ref[...] = gmid
        branch = gmid.astype(BF)
        vec_ref[0:1, :] = colsum(branch.astype(F32))
        vec_ref[1:2, :] = colsum(e * n)
        vec_ref[2:3, :] = colsum(e)
        vec_ref[3:4, :] = colsum(c)
        dwo = tn_dot(att[...], branch)
        if fast:
            side[...] = dwo.reshape(side.shape).astype(BF)
            put_pieces(me_ref, side, grads[1], grads[2], ())
        else:
            grads[2][...] = dwo.astype(BF)
        gatt = nt_dot(branch, wo_ref[...])
        ga_ref[...] = gatt[0:rm].astype(BF)
        ga5_ref[...] = jnp.zeros_like(ga5_ref)
        for pair in range(pairs):
            lanes = slice(pair * 2 * HD, (pair + 1) * 2 * HD)
            top, bot = gatt[rm : rm + half, lanes], gatt[rm + half : rm + r5, lanes]
            even = jnp.where(low, top, swap_halves(bot))
            odd = jnp.where(low, swap_halves(top), bot)
            ga5_ref[slot_of(2 * pair, nf, nt)] = even.astype(BF)
            ga5_ref[slot_of(2 * pair + 1, nf, nt)] = odd.astype(BF)
        if fast:
            for j in range(nf):
                for copy in copies(j):
                    copy.wait()


def mid_call(nf, nt, fast, me, xms, cms, att, att5, x5, c5, wo, vecs, wu, wd):
    _, r5, width = x5.shape
    rm = nf * r5
    rows = rm + r5
    ff = wu.shape[1]
    blk = ff // nf
    shape = jax.ShapeDtypeStruct
    if fast:
        dev = nf * nt * 2
        pd, pu = ff // dev, width // dev
        oshape = (nt, nf, pu, width)
        gspecs = [pl.BlockSpec(memory_space=pl.ANY)] + [full(oshape)] * 2
        gshapes = [shape((nt * 2, nf, pd + nf * pu, width), BF)] + [shape(oshape, BF)] * 2
        extra = [
            pltpu.VMEM((nf, nt * 2, pd, width), BF),
            pltpu.VMEM((nf, dev, pu, width), BF),
            pltpu.VMEM((dev, pu, width), BF),
            pltpu.SemaphoreType.DMA((1 + nf, nf)),
        ]
    else:
        gspecs = [
            pl.BlockSpec((blk, width), lambda j, *_: (j, 0)),
            pl.BlockSpec((width, blk), lambda j, *_: (0, j)),
            full((width, width)),
        ]
        gshapes = [shape((ff, width), BF), shape((width, ff), BF), shape((width, width), BF)]
        extra = []
    ins = [*xms, *cms, att, att5, x5, c5, wo, vecs]
    return pl.pallas_call(
        functools.partial(mid_kernel, nf, nt, fast),
        grid_spec=pltpu.PrefetchScalarGridSpec(
            num_scalar_prefetch=1,
            grid=(nf,),
            in_specs=[clip_at(x, nf) if x.ndim == 3 and x.shape[0] == nf + 1 else full(x.shape) for x in ins]
            + [
                pl.BlockSpec((width, blk), lambda j, *_: (0, j)),
                pl.BlockSpec((blk, width), lambda j, *_: (j, 0)),
            ],
            out_specs=[
                full((nf, r5, width)),
                full((r5, width)),
                full((rows, width)),
                full((rm, width)),
                full(att5.shape),
            ]
            + gspecs
            + [full((4, width)), pl.BlockSpec((1, blk), lambda j, *_: (0, j))],
            scratch_shapes=[
                pltpu.VMEM((rows, width), BF),
                pltpu.VMEM((rows, width), BF),
                pltpu.VMEM((rows, width), F32),
                pltpu.VMEM((rows, width), F32),
                pltpu.VMEM((rows, 1), F32),
                pltpu.VMEM((rows, width), BF),
                pltpu.VMEM((rows, width), F32),
                pltpu.VMEM((rows, width), F32),
            ]
            + extra,
        ),
        out_shape=[
            shape((nf, r5, width), BF),
            shape((r5, width), F32),
            shape((rows, width), F32),
            shape((rm, width), BF),
            shape(att5.shape, BF),
        ]
        + gshapes
        + [shape((4, width), F32), shape((1, ff), F32)],
        compiler_params=params(),
        cost_estimate=cost(12 * rows * width * ff + 6 * rows * width * width, 24 << 20),
        name="mid",
    )(me, *ins, wu, wd)


def tail5_kernel(nf, nt, fast, *refs):
    refs = list(refs)
    if fast:
        me_ref = refs.pop(0)
        *refs, side, small = refs
    (gq_ref, gkv_ref), ns, refs = refs[:2], refs[2 : 2 + nt], refs[2 + nt :]
    g_ref, n5_ref, x5_ref, gm_ref, w_ref, in_ref, vm_ref, v2_ref, gbu_ref = refs[:9]
    (*dwo, gin_ref, vec_ref, dx, x_all, g_all, sums) = refs[9:]
    step = pl.program_id(0)
    r5, width = x5_ref.shape
    half = r5 // 2
    low = low_lanes(half)
    rows = ns[0].shape[0]

    @pl.when(step == 0)
    def _():
        x_all[0:r5, :] = n5_ref[...]
        for c in range(nt):
            x_all[r5 + c * rows : r5 + (c + 1) * rows, :] = ns[c][...]
        dx[...] = jnp.zeros_like(dx)

    for pair in range(width // (2 * HD)):
        lanes = slice(pair * 2 * HD, (pair + 1) * 2 * HD)
        even = g_ref[slot_of(2 * pair, nf, nt)].astype(F32)
        odd = g_ref[slot_of(2 * pair + 1, nf, nt)].astype(F32)
        top = jnp.where(low, even, swap_halves(odd))
        bot = jnp.where(low, swap_halves(even), odd)
        g_all[0:r5, lanes] = jnp.concatenate([top, bot], axis=0).astype(BF)
    dx[...] += nt_dot(g_all[0:r5, :], w_ref[...])

    def finish(end):
        g = g_all[0:end, :]
        sums[pl.ds(step, 1), :] = colsum(g.astype(F32))
        dw = tn_dot(x_all[0:end, :], g)
        if fast:
            side[...] = dw.reshape(side.shape).astype(BF)
        else:
            dwo[0][...] = dw.astype(BF)

    @pl.when(step < 2)
    def _():
        g_all[r5:, :] = gkv_ref[0]
        finish(r5 + nt * rows)

    @pl.when(step == 2)
    def _():
        g_all[r5 : r5 + rows, :] = gq_ref[...]
        finish(r5 + rows)
        n, rstd = normalize(x5_ref[...].astype(F32))
        e = dx[...]
        gin_ref[...] = gm_ref[...] + norm_back(e, n, rstd, row_of(in_ref, GAIN1))
        main = vm_ref[0:1, :] - row_of(in_ref, SHIFT1) * vm_ref[1:2, :]
        vec_ref[0:1, :] = main / row_of(in_ref, GAIN1) + colsum(e * n)
        vec_ref[1:2, :] = vm_ref[1:2, :] + colsum(e)
        vec_ref[2:6, :] = v2_ref[...]
        vec_ref[6:7, :] = sums[2:3, :]
        vec_ref[7:8, :] = sums[1:2, :]
        if fast:
            per = width // small.shape[0]
            lanes = width // 4
            total = 0.0
            for i in range(8):
                part = spread_over(per, vec_ref[i : i + 1, :], 2 * HD)
                part = jnp.concatenate([part, jnp.zeros((part.shape[0], lanes - 2 * HD), F32)], 1)
                total += pltpu.roll(part, i * per, 1) if i else part
            wide = spread_over(gbu_ref.shape[1] // small.shape[0], gbu_ref[...], 2 * HD)
            rest = width - lanes - 2 * HD
            line = jnp.concatenate([total, wide, jnp.zeros((wide.shape[0], rest), F32)], 1)
            small[...] = jnp.broadcast_to(line[:, None, :], small.shape).astype(BF)
            keep, send = (x.at[:, :, side.shape[1] :, :] for x in dwo[0:2])
            put_pieces(me_ref, small, keep, send, ())

    if fast:
        for i in range(3):

            @pl.when(step == (i + 2) % 3)
            def _():
                keep, send = (x.at[:, :, 0 : side.shape[1], :] for x in dwo[2 * i : 2 * i + 2])
                put_pieces(me_ref, side, keep, send, ())


def tail5_call(nf, nt, fast, me, gq, gkv, ns, g, n5, x5, gm, w, vecs, vm, v2, gbu):
    _, r5, width = x5.shape
    at = gm.shape[0] // r5 - 1
    toks = gkv.shape[1]
    part = lambda j: (j + 1) % 3
    bshape = jax.ShapeDtypeStruct
    if fast:
        pu = width // (nf * nt * 2)
        heights = (pu + 8,) * 2 + (pu,) * 4
        wspecs = [full((nt, nf, n, width)) for n in heights]
        wshapes = [bshape((nt, nf, n, width), BF) for n in heights]
        extra = [pltpu.VMEM((nf * nt * 2, n, width), BF) for n in (pu, 8)]
    else:
        wspecs = [pl.BlockSpec((width, width), lambda j, *_: (0, part(j)))]
        wshapes = [bshape((width, 3 * width), BF)]
        extra = []
    return pl.pallas_call(
        functools.partial(tail5_kernel, nf, nt, fast),
        grid_spec=pltpu.PrefetchScalarGridSpec(
            num_scalar_prefetch=int(fast),
            grid=(3,),
            in_specs=[full(gq.shape)]
            + [pl.BlockSpec((1, toks, width), lambda j, *_: (jnp.minimum(j, 1), 0, 0))]
            + [full(x.shape) for x in ns]
            + [
                pl.BlockSpec((g.shape[0], r5 // 2, 2 * HD), lambda j, *_: (0, 0, part(j))),
                full(n5.shape),
                clip_at(x5, nf),
                pl.BlockSpec((r5, width), lambda j, *_: (at, 0)),
                pl.BlockSpec((width, width), lambda j, *_: (0, part(j))),
            ]
            + [full(x.shape) for x in (vecs, vm, v2, gbu)],
            out_specs=wspecs + [full((r5, width)), full((8, width))],
            scratch_shapes=[
                pltpu.VMEM((r5, width), F32),
                pltpu.VMEM((r5 + toks, width), BF),
                pltpu.VMEM((r5 + toks, width), BF),
                pltpu.VMEM((8, width), F32),
            ]
            + extra,
        ),
        out_shape=wshapes + [bshape((r5, width), F32), bshape((8, width), F32)],
        compiler_params=params(),
        cost_estimate=cost(4 * r5 * width * width * 3 + 4 * width * width * toks, 16 << 20),
        name="tail_shared",
    )(*([me] if fast else []), gq, gkv, *ns, g, n5, x5, gm, w, vecs, vm, v2, gbu)


def tail_kernel(nf, nt, *refs):
    dxs, xs, refs = refs[:nt], refs[nt : nt + nf], refs[nt + nf :]
    gm_ref, vec_ref, *gins = refs
    rows = xs[0].shape[0]
    for k in range(nf):
        at = slice(k * rows, (k + 1) * rows)
        e = dxs[0][at, :]
        for c in range(1, nt):
            e = e + dxs[c][at, :].astype(F32)
        n, rstd = normalize(xs[k][...].astype(F32))
        gins[k][...] = (gm_ref[at, :] + norm_back(e, n, rstd, row_of(vec_ref, GAIN1))).astype(BF)


def tail_call(dxs, xs, gm, vecs):
    rows, width = xs[0].shape
    nf, nt = len(xs), len(dxs)
    return pl.pallas_call(
        functools.partial(tail_kernel, nf, nt),
        grid=(1,),
        in_specs=[full((nf * rows, width))] * nt
        + [full((rows, width))] * nf
        + [full((nf * rows, width)), full(vecs.shape)],
        out_specs=[full((rows, width))] * nf,
        out_shape=[jax.ShapeDtypeStruct((rows, width), BF)] * nf,
        compiler_params=params(),
        cost_estimate=cost(30 * nf * rows * width, 6 << 20, 1000),
        name="tail",
    )(*dxs, *xs, gm, vecs)


def pair_sum_kernel(count, *refs):
    ins, (dx, d0, d2, uy, u0, u1) = refs[: 4 * count], refs[4 * count :]
    outs = ((d0, dx.at[0], d2, dx.at[1]), (u0, u1, uy.at[0], uy.at[1]))
    for side in range(2):
        pairs = ins[2 * count * side : 2 * count * (side + 1)]
        at = 0
        for keep, got in zip(pairs[0::2], pairs[1::2]):
            rows = keep.shape[2]
            for k in range(4):
                total = (keep[k, 0].astype(F32) + got[k, 0].astype(F32)).astype(BF)
                outs[side][k][0, at : at + rows, :] = total
            at += rows


def pair_sum(trios):
    _, blocks, _, width = trios[0][0].shape
    steps = blocks // 2
    rows = sum(x[0].shape[2] for x in trios)
    specs, args = [], []
    for first in (0, steps):
        for keep, got in trios:
            spec = pl.BlockSpec((4, 1) + keep.shape[2:], lambda j, f=first: (0, j + f, 0, 0))
            specs += [spec, spec]
            args += [keep, got]
    two = pl.BlockSpec((2, 1, rows, width), lambda j: (0, j, 0, 0))
    one = pl.BlockSpec((1, rows, width), lambda j: (j, 0, 0))
    shape = jax.ShapeDtypeStruct
    return pl.pallas_call(
        functools.partial(pair_sum_kernel, len(trios)),
        grid=(steps,),
        in_specs=specs,
        out_specs=[two, one, one] * 2,
        out_shape=[
            shape((2, steps, rows, width), BF),
            shape((steps, rows, width), BF),
            shape((steps, rows, width), BF),
        ]
        * 2,
        compiler_params=params(),
        cost_estimate=cost(1 << 20, 8 << 20),
        name="pair_sum",
    )(*args)


def relay_sum_kernel(d2, gx, u1, gy, sd, su):
    sd[...] = (d2[...].astype(F32) + gx[0].astype(F32)).astype(BF)
    su[...] = (u1[...].astype(F32) + gy[0].astype(F32)).astype(BF)


def relay_sum(d2, gx, u1, gy):
    second = lambda x: pl.BlockSpec((1,) + x.shape[1:], lambda *_: (1,) + (0,) * (x.ndim - 1))
    return pl.pallas_call(
        relay_sum_kernel,
        grid=(1,),
        in_specs=[full(d2.shape), second(gx), full(u1.shape), second(gy)],
        out_specs=[full(d2.shape), full(u1.shape)],
        out_shape=[jax.ShapeDtypeStruct(d2.shape, BF), jax.ShapeDtypeStruct(u1.shape, BF)],
        compiler_params=params(),
        cost_estimate=cost(d2.size, 6 * d2.size, 1),
        name="relay_sum",
    )(d2, gx, u1, gy)


def along(axis, k, x):
    return lax.ppermute(x, axis, [(i, i ^ k) for i in range(4)])


def relay_start(dx, uy):
    return along("tm", 1, dx), along("tm", 2, uy)


def relay_end(gx, gy, d2, u1):
    sd, su = relay_sum(d2, gx, u1, gy)
    return along("tm", 2, sd), along("tm", 1, su)


def tm_sum_kernel(nf, lead, me_ref, *refs):
    d0, gx, rd, u0, gy, ru = refs[:6]
    outs, total = refs[6 : 6 + nf], refs[-1]
    half = d0.shape[0]
    for first, own, one, two in ((0, d0, gx, rd), (half, u0, gy, ru)):
        for f in range(half):
            part = own[f].astype(F32) + one[0, f, lead:, :].astype(F32) + two[f, lead:, :].astype(F32)
            total[first + f] = part.astype(BF)
    for k in range(nf):
        outs[k][...] = total[me_ref[0] ^ k]


def tm_sum(nf, me, d0, gx, rd, u0, gy, ru):
    _, rows, width = d0.shape
    first = full((1,) + gx.shape[1:])
    return pl.pallas_call(
        functools.partial(tm_sum_kernel, nf, gx.shape[2] - rows),
        grid_spec=pltpu.PrefetchScalarGridSpec(
            num_scalar_prefetch=1,
            grid=(1,),
            in_specs=[full(d0.shape), first, full(rd.shape)] * 2,
            out_specs=[full((rows, width))] * nf,
            scratch_shapes=[pltpu.VMEM((nf, rows, width), BF)],
        ),
        out_shape=[jax.ShapeDtypeStruct((rows, width), BF)] * nf,
        compiler_params=params(),
        cost_estimate=cost(1 << 20, 5 << 20),
        name="tm_sum",
    )(me, d0, gx, rd, u0, gy, ru)


def last_sum_kernel(nf, places, first_vec, per, *refs):
    parts, stacked, outs = refs[:nf], refs[nf], refs[nf + 1 :]
    for at, rows, out, col, source in places:
        if source:
            parts = [stacked.at[i] for i in range(stacked.shape[0])]
        lanes = parts[0].shape[1]
        total = parts[0][at : at + rows, :].astype(F32)
        for part in parts[1:]:
            total = total + part[at : at + rows, :].astype(F32)
        if out is None:
            for i in range(8):
                outs[first_vec + i][...] = (pltpu.roll(total, lanes - i * per, 1) if i else total)[0, 0:per]
            outs[first_vec + 8][...] = total[0, lanes // 4 : lanes // 4 + outs[first_vec + 8].shape[0]]
        else:
            outs[out][:, col : col + lanes] = total


def last_sum(parts, stacked, places, shapes, first_vec, per):
    nf = len(parts)
    return pl.pallas_call(
        functools.partial(last_sum_kernel, nf, places, first_vec, per),
        out_shape=[jax.ShapeDtypeStruct(x, F32) for x in shapes],
        compiler_params=pltpu.CompilerParams(vmem_limit_bytes=VMEM_LIMIT),
        cost_estimate=cost(nf * parts[0].size, 2 * nf * parts[0].size, 1),
        name="last_sum",
    )(*parts, stacked)


def swap_cores(x):
    return lax.ppermute(x, "grp", [(0, 1), (1, 0)])


def exchange(axis, parts):
    pairs = lambda k: [(i, i ^ k) for i in range(len(parts))]
    return [parts[0]] + [lax.ppermute(parts[k], axis, pairs(k)) for k in range(1, len(parts))]


def tie(x, *deps):
    flat, tree = jax.tree.flatten(x)
    tied = lax.optimization_barrier((flat, deps))[0]
    return jax.tree.unflatten(tree, tied)


def over(axes, x):
    return lax.all_to_all(x, axes, 0, 0)


def local(
    nf,
    nt,
    ng,
    inputs,
    gain_one,
    shift_one,
    w_qkv,
    bias_query,
    bias_value,
    w_out,
    bias_out,
    gain_two,
    shift_two,
    w_up,
    bias_up,
    w_down,
    bias_down,
    cotangent,
):
    _, r, width = inputs.shape
    ff = w_up.shape[1]
    dev = nf * nt * ng
    per = width // dev
    fast = ng == 2 and per % 8 == 0 and ff // nf == width
    me = jnp.stack([lax.axis_index(a) for a in ALL]).astype(jnp.int32)
    both = ("freq", "tm")
    got = pick_call(
        nf,
        me,
        inputs,
        cotangent,
        (gain_one, shift_one, bias_query, bias_value, bias_out, gain_two, shift_two, bias_down, bias_up),
    )
    picked, vecs, cs = got[:nf], got[nf], got[nf + 1 :]
    xs = exchange("freq", picked)
    n5, pack5 = q5_call(nf, nt, tie(inputs, picked[0]), vecs, w_qkv)
    got5 = over(both, pack5).reshape(-1, 6 * HD)
    nm = ln_call(tie(xs, pack5), vecs)
    ns = exchange("tm", [nm] * nt)
    o5, r5, ob5, e5 = attn5_fwd_call(got5)
    att5 = over(both, ob5.reshape(nf * nt, r // 2, 2 * HD))
    cs = exchange("freq", tie(cs, ob5))
    att, o, rr, q, kv, e = attn_fwd_call(tie(ns, ob5), w_qkv, vecs)
    outs, out5, gm, ga, ga5, *dws, vec, gbu = mid_call(
        nf,
        nt,
        fast,
        me,
        xs,
        cs,
        att,
        att5,
        inputs,
        cotangent,
        w_out,
        vecs,
        w_up,
        w_down,
    )
    pieces = lambda x: x.reshape(nt, nf, -1, width)
    pd = ff // dev
    if fast:
        dff = lax.psum_scatter(
            dws[0].reshape(nt * ng, nf * (pd + nf * per), width),
            ("tm", "grp"),
            scatter_dimension=0,
            tiled=True,
        )
        keep_o, got_o = pieces(dws[1]), pieces(swap_cores(dws[2]))
    got_ga5 = over(both, ga5).reshape(-1, 2 * HD)
    gq, gkv = attn_bwd_call(ga, q, kv, o, rr, e)
    g5 = attn5_bwd_call(got5, tie(got_ga5, gq, *([got_o] if fast else [])), o5, r5, e5).reshape(nf * nt, r // 2, 6 * HD)
    *dxs, vec_m = dx_call(tie(gq, g5), gkv, ns, w_qkv)
    dxs = exchange("tm", dxs)
    g5 = over(both, g5)
    *dwqkv, gin5, vec8 = tail5_call(
        nf, nt, fast, me, tie(gq, vec_m), gkv, ns, g5, n5, inputs, gm, w_qkv, vecs, vec_m, vec, gbu
    )
    outs = over("freq", tie(outs, g5))
    gin = tail_call(tie(dxs, vec8), xs, gm, vecs)
    order = gin[0]
    gin = exchange("freq", gin)
    if fast:
        trios = [(dwqkv[i], swap_cores(dwqkv[i + 1])) for i in (0, 2, 4)]
        trios += [(keep_o, got_o)]
        trios[0] = (trios[0][0], tie(trios[0][1], order))
        dxq, d0q, d2q, uyq, u0q, u1q = pair_sum(trios)
        gxq, gyq = relay_start(dxq, uyq)
        sdq, suq = relay_sum(d2q, gxq, u1q, gyq)
        rdq, ruq = along("tm", 2, sdq), along("tm", 1, suq)
        dff = over("freq", tie(dff, dxq).reshape(nf, -1, width))
        sums_q = exchange("freq", tm_sum(nf, me, d0q, gxq, rdq, u0q, gyq, ruq))
        places = [(0, per, 0, 0, 0), (per, 8, None, 0, 0), (per + 8, per, 0, width, 0)]
        places += [(2 * per + 8, per, 0, 2 * width, 0), (3 * per + 8, per, 1, 0, 0)]
        places += [(0, pd, 2, 0, 1)] + [(pd + i * per, per, 3, i * width, 1) for i in range(nf)]
        shapes = [(per, 3 * width), (per, width), (pd, width), (per, ff)] + [(per,)] * 8 + [(pd,)]
        dwqkv, dwo, dwd, dwu, *small, gbu = last_sum(sums_q, dff, places, shapes, 4, per)
        piece = lambda i: small[i]
    else:
        dwd, dwu, dwo, dwqkv = (
            lax.psum_scatter(x, ALL, scatter_dimension=0, tiled=True).astype(F32)
            for x in dws + dwqkv
        )
        small = vec8.reshape(8, dev, per).transpose(1, 0, 2).reshape(dev, -1)
        small = jnp.concatenate([small, gbu.reshape(dev, pd)], axis=1)
        small = jnp.sum(over(ALL, small), axis=0)
        piece = lambda i: small[i * per : (i + 1) * per]
        gbu = small[8 * per :]
    block_out = jnp.concatenate([outs.astype(F32), out5[None]], axis=0)
    grad_in = assemble_call(nf, me, gin, gin5)
    return (
        block_out,
        grad_in,
        piece(0),
        piece(1),
        dwqkv,
        piece(6),
        piece(7),
        dwo,
        piece(2),
        piece(3),
        piece(4),
        dwu,
        gbu,
        dwd,
        piece(5),
    )


def solution(mesh):
    tokens = P("grp", ("freq", "tm"), None)
    vec = P(ALL)
    mat = P(ALL, None)
    return jax.shard_map(
        functools.partial(local, mesh.shape["freq"], mesh.shape["tm"], mesh.shape["grp"]),
        mesh=mesh,
        in_specs=(tokens,) + (P(),) * 13 + (tokens,),
        out_specs=(
            tokens,
            tokens,
            vec,
            vec,
            mat,
            vec,
            vec,
            mat,
            vec,
            vec,
            vec,
            mat,
            vec,
            mat,
            vec,
        ),
        check_vma=False,
    )
```

```python
import functools

import jax
import jax.numpy as jnp
from jax import lax
from jax.experimental import pallas as pl
from jax.experimental.pallas import tpu as pltpu
from jax.sharding import PartitionSpec as P

HD = 64
NORM_EPS = 1e-06
BF = jnp.bfloat16
F32 = jnp.float32
ALL = ("freq", "tm", "grp")
VMEM_LIMIT = 60 * 1024 * 1024
SAFE = 50.0
GAIN1, SHIFT1, BIAS_Q, BIAS_V, BIAS_OUT, GAIN2, SHIFT2, BIAS_DOWN, BIAS_UP = range(9)


def row_of(ref, i):
    return ref[i : i + 1, :]


def nn(a, b):
    return lax.dot_general(a, b, (((1,), (0,)), ((), ())), preferred_element_type=F32)


def nt_dot(a, b):
    return lax.dot_general(a, b, (((1,), (1,)), ((), ())), preferred_element_type=F32)


def tn_dot(a, b):
    return lax.dot_general(a, b, (((0,), (0,)), ((), ())), preferred_element_type=F32)


def normalize(x):
    mean = jnp.mean(x, axis=-1, keepdims=True)
    centered = x - mean
    var = jnp.mean(centered * centered, axis=-1, keepdims=True)
    rstd = lax.rsqrt(var + NORM_EPS)
    return centered * rstd, rstd


def norm_back(e, n, rstd, gain):
    eg = e * gain
    return rstd * (
        eg - jnp.mean(eg, axis=-1, keepdims=True) - n * jnp.mean(eg * n, axis=-1, keepdims=True)
    )


def colsum(x):
    return jnp.sum(x, axis=0, keepdims=True)


def low_lanes(rows):
    return lax.broadcasted_iota(jnp.int32, (rows, 2 * HD), 1) < HD


def swap_halves(x):
    return pltpu.roll(x, HD, 1)


def slot_of(head, nf, nt):
    per = -(-(12) // nf)
    return (head // per) * nt + head % per


def params(count=1):
    return pltpu.CompilerParams(
        dimension_semantics=("arbitrary",) * count, vmem_limit_bytes=VMEM_LIMIT
    )


def full(shape):
    return pl.BlockSpec(shape, lambda *_: (0,) * len(shape))


def clip_at(x, i):
    return pl.BlockSpec((None,) + x.shape[1:], lambda *_: (i, 0, 0))


def cost(flops, nbytes, weight=1):
    return pl.CostEstimate(
        flops=int(weight * flops), bytes_accessed=int(weight * nbytes), transcendentals=0
    )


def pick_kernel(nf, count, me_ref, x_ref, c_ref, *refs):
    vecs, outs, cots = refs[:count], refs[count : -nf], refs[-nf:]
    for k in range(nf):
        outs[k][...] = x_ref[me_ref[0] ^ k]
        cots[k][...] = c_ref[me_ref[0] ^ k]
    if count:
        width = x_ref.shape[2]
        for i in range(count - 1):
            outs[nf][i : i + 1, :] = vecs[i][...].reshape(1, width)
        last = vecs[count - 1]
        for i in range(last.shape[0] // width):
            at = count - 1 + i
            outs[nf][at : at + 1, :] = last[i * width : (i + 1) * width].reshape(1, width)


def pick_call(nf, me, x, c, vecs):
    _, rows, width = x.shape
    count = 8 + -(-sum(v.shape[0] for v in vecs) // width) // 8 * 8
    more = [(count, width)] if vecs else []
    return pl.pallas_call(
        functools.partial(pick_kernel, nf, len(vecs)),
        grid_spec=pltpu.PrefetchScalarGridSpec(
            num_scalar_prefetch=1,
            grid=(1,),
            in_specs=[full(x.shape)] * 2 + [full(v.shape) for v in vecs],
            out_specs=[full((rows, width))] * nf
            + [full(y) for y in more]
            + [full((rows, width))] * nf,
        ),
        out_shape=[jax.ShapeDtypeStruct((rows, width), BF)] * nf
        + [jax.ShapeDtypeStruct(y, F32) for y in more]
        + [jax.ShapeDtypeStruct((rows, width), BF)] * nf,
        compiler_params=params(),
        cost_estimate=cost(0, 8 * x.size),
        name="pick",
    )(me, x, c, *vecs)


def assemble_kernel(nf, me_ref, *refs):
    for k in range(nf):
        refs[-1][me_ref[0] ^ k] = refs[k][...].astype(F32)
    refs[-1][nf] = refs[nf][...]


def assemble_call(nf, me, parts, five):
    rows, width = five.shape
    return pl.pallas_call(
        functools.partial(assemble_kernel, nf),
        grid_spec=pltpu.PrefetchScalarGridSpec(
            num_scalar_prefetch=1,
            grid=(1,),
            in_specs=[full((rows, width))] * (nf + 1),
            out_specs=full((nf + 1, rows, width)),
        ),
        out_shape=jax.ShapeDtypeStruct((nf + 1, rows, width), F32),
        compiler_params=params(),
        cost_estimate=cost(0, 8 * (nf + 1) * five.size),
        name="assemble",
    )(me, *parts, five)


def ln_kernel(nf, *refs):
    vec_ref, n_ref = refs[nf:]
    for k in range(nf):
        rows = refs[k].shape[0]
        n, _ = normalize(refs[k][...].astype(F32))
        n = n * row_of(vec_ref, GAIN1) + row_of(vec_ref, SHIFT1)
        n_ref[k * rows : (k + 1) * rows, :] = n.astype(BF)


def ln_call(xs, vecs):
    rows, width = xs[0].shape
    return pl.pallas_call(
        functools.partial(ln_kernel, len(xs)),
        grid=(1,),
        in_specs=[full((rows, width))] * len(xs) + [full(vecs.shape)],
        out_specs=full((len(xs) * rows, width)),
        out_shape=jax.ShapeDtypeStruct((len(xs) * rows, width), BF),
        compiler_params=pltpu.CompilerParams(vmem_limit_bytes=VMEM_LIMIT),
        cost_estimate=cost(len(xs) * rows * width * 10, len(xs) * rows * width * 4, 10000),
        name="ln_one",
    )(*xs, vecs)


def q5_kernel(nf, nt, x_ref, vec_ref, w_ref, n_ref, pack_ref):
    rows, width = x_ref.shape
    half = rows // 2
    hat, _ = normalize(x_ref[...].astype(F32))
    n = (hat * row_of(vec_ref, GAIN1) + row_of(vec_ref, SHIFT1)).astype(BF)
    n_ref[...] = n
    low = low_lanes(half)
    pack_ref[...] = jnp.zeros_like(pack_ref)
    for part in range(3):
        proj = nn(n, w_ref[:, part * width : (part + 1) * width])
        if part == 0:
            proj = (proj + row_of(vec_ref, BIAS_Q)) * (HD**-0.5)
        if part == 2:
            proj = proj + row_of(vec_ref, BIAS_V)
        for pair in range(width // (2 * HD)):
            blk = proj[:, pair * 2 * HD : (pair + 1) * 2 * HD]
            top, bot = blk[:half], blk[half:]
            even = jnp.where(low, top, swap_halves(bot))
            odd = jnp.where(low, swap_halves(top), bot)
            lanes = slice(part * 2 * HD, (part + 1) * 2 * HD)
            pack_ref[slot_of(2 * pair, nf, nt), :, lanes] = even.astype(BF)
            pack_ref[slot_of(2 * pair + 1, nf, nt), :, lanes] = odd.astype(BF)


def q5_call(nf, nt, x, vecs, w):
    _, rows, width = x.shape
    return pl.pallas_call(
        functools.partial(q5_kernel, nf, nt),
        grid=(1,),
        in_specs=[clip_at(x, nf), full(vecs.shape), full(w.shape)],
        out_specs=[full((rows, width)), full((nf * nt, rows // 2, 6 * HD))],
        out_shape=(
            jax.ShapeDtypeStruct((rows, width), BF),
            jax.ShapeDtypeStruct((nf * nt, rows // 2, 6 * HD), BF),
        ),
        compiler_params=pltpu.CompilerParams(vmem_limit_bytes=VMEM_LIMIT),
        cost_estimate=cost(2 * rows * w.size, w.size * 2),
        name="q_shared",
    )(x, vecs, w)


def spread(x):
    rows = x.shape[0]
    low = low_lanes(rows)
    zero = jnp.zeros_like(x)
    return jnp.concatenate([jnp.where(low, x, zero), jnp.where(low, swap_halves(x), zero)], axis=0)


def unspread(x):
    half = x.shape[0] // 2
    return x[:half] + swap_halves(x[half:])


def stack_heads(x):
    low = low_lanes(x.shape[0])
    zero = jnp.zeros_like(x)
    return jnp.concatenate([jnp.where(low, x, zero), jnp.where(low, zero, x)], axis=0)


def plain_block(q, k, v):
    e = jnp.exp(nt_dot(q, k))
    rinv = 1.0 / jnp.sum(e, axis=-1, keepdims=True)
    e = e.astype(BF)
    return e, nn(e, v) * rinv, rinv


def softmax_block(q, k, v):
    s = nt_dot(q, k)
    m = jnp.max(s, axis=-1, keepdims=True)
    e = jnp.exp(s - m)
    total = jnp.sum(e, axis=-1, keepdims=True)
    e = e.astype(BF)
    rinv = 1.0 / total
    return e, nn(e, v) * rinv, rinv


def attn5_fwd_kernel(x_ref, o_ref, r_ref, ob_ref, e_ref, qf, kf, vf, of, rf):
    step = pl.program_id(0)

    @pl.when(step == 0)
    def _():
        for part, dst in enumerate((qf, kf, vf)):
            blk = x_ref[:, part * 2 * HD : (part + 1) * 2 * HD].astype(F32)
            dst[...] = spread(blk).astype(BF)

    rows = e_ref.shape[0]
    at = pl.ds(pl.multiple_of(step * rows, rows), rows)
    peak = jnp.max(jnp.abs(kf[...].astype(F32)), axis=0, keepdims=True)
    bound = jnp.sum(jnp.abs(qf[at, :].astype(F32)) * peak, axis=-1, keepdims=True)
    small = jnp.max(bound) < SAFE

    @pl.when(small)
    def _():
        e, o, rinv = plain_block(qf[at, :], kf[...], vf[...])
        e_ref[...] = e
        of[at, :] = o
        rf[at, :] = jnp.where(low_lanes(rows), jnp.broadcast_to(rinv, (rows, 2 * HD)), 0.0)

    @pl.when(jnp.logical_not(small))
    def _():
        part = 32

        def body(i, carry):
            here = pl.ds(pl.multiple_of(i * part, part), part)
            there = pl.ds(pl.multiple_of(step * rows + i * part, part), part)
            e, o, rinv = softmax_block(qf[there, :], kf[...], vf[...])
            e_ref[here, :] = e
            of[there, :] = o
            rf[there, :] = jnp.where(low_lanes(part), jnp.broadcast_to(rinv, (part, 2 * HD)), 0.0)
            return carry

        lax.fori_loop(0, rows // part, body, 0)

    @pl.when(step == pl.num_programs(0) - 1)
    def _():
        packed = unspread(of[...])
        o_ref[...] = packed
        ob_ref[...] = packed.astype(BF)
        r_ref[...] = unspread(rf[...])


def attn5_fwd_call(x):
    rows = x.shape[0]
    toks = 2 * rows
    shape = jax.ShapeDtypeStruct
    return pl.pallas_call(
        attn5_fwd_kernel,
        grid=(2,),
        in_specs=[full(x.shape)],
        out_specs=[full((rows, 2 * HD))] * 3 + [pl.BlockSpec((toks // 2, toks), lambda j: (j, 0))],
        out_shape=(
            shape((rows, 2 * HD), F32),
            shape((rows, 2 * HD), F32),
            shape((rows, 2 * HD), BF),
            shape((toks, toks), BF),
        ),
        scratch_shapes=[pltpu.VMEM((toks, 2 * HD), BF)] * 3 + [pltpu.VMEM((toks, 2 * HD), F32)] * 2,
        compiler_params=params(),
        cost_estimate=cost(4 * 4 * toks * toks * 2 * HD, toks * toks * 2),
        name="attn_shared_fwd",
    )(x)


def attn5_bwd_kernel(x_ref, ga_ref, o_ref, r_ref, e_ref, out_ref, qf, kf, vf, gf, inn, dq, dk, dv):
    step = pl.program_id(0)

    @pl.when(step == 0)
    def _():
        for part, dst in enumerate((qf, kf, vf)):
            blk = x_ref[:, part * 2 * HD : (part + 1) * 2 * HD].astype(F32)
            dst[...] = spread(blk).astype(BF)
        g = ga_ref[...].astype(F32) * r_ref[...]
        gs = spread(g)
        gf[...] = gs.astype(BF)
        inn[...] = jnp.sum(gs * spread(o_ref[...]), axis=-1, keepdims=True)
        dk[...] = jnp.zeros_like(dk)
        dv[...] = jnp.zeros_like(dv)

    rows = e_ref.shape[0]
    at = pl.ds(pl.multiple_of(step * rows, rows), rows)
    e = e_ref[...]
    gb = gf[at, :]
    dp = nt_dot(gb, vf[...])
    ds = (e.astype(F32) * (dp - inn[at, :])).astype(BF)
    dq[at, :] = nn(ds, kf[...]) * (HD**-0.5)
    dk[...] += tn_dot(ds, qf[at, :])
    dv[...] += tn_dot(e, gb)

    @pl.when(step == pl.num_programs(0) - 1)
    def _():
        for part, src in enumerate((dq, dk, dv)):
            out_ref[:, part * 2 * HD : (part + 1) * 2 * HD] = unspread(src[...]).astype(BF)


def attn5_bwd_call(x, ga, o, r, e):
    rows = x.shape[0]
    toks = 2 * rows
    return pl.pallas_call(
        attn5_bwd_kernel,
        grid=(4,),
        in_specs=[full(y.shape) for y in (x, ga, o, r)]
        + [pl.BlockSpec((toks // 4, toks), lambda j: (j, 0))],
        out_specs=full((rows, 6 * HD)),
        out_shape=jax.ShapeDtypeStruct((rows, 6 * HD), BF),
        scratch_shapes=[pltpu.VMEM((toks, 2 * HD), BF)] * 4
        + [pltpu.VMEM((toks, 1), F32)]
        + [pltpu.VMEM((toks, 2 * HD), F32)] * 3,
        compiler_params=params(),
        cost_estimate=cost(8 * 4 * toks * toks * 2 * HD, toks * toks * 2),
        name="attn_shared_bwd",
    )(x, ga, o, r, e)


def attn_fwd_kernel(nt, *refs):
    ns, (wq, wk, wv, vec_ref, att_ref, o_ref, r_ref, q_ref, kv_ref, e_ref, x_all, w_kv, qs, os, rs) = refs[:nt], refs[nt:]
    rows = ns[0].shape[0]

    @pl.when(pl.program_id(0) == 0)
    def _():
        for c in range(nt):
            x_all[c * rows : (c + 1) * rows, :] = ns[c][...]

    lanes = 2 * HD
    w_kv[:, 0:lanes] = wk[...]
    w_kv[:, lanes:] = wv[...]
    kv = nn(x_all[...], w_kv[...])
    kv_ref[0] = kv[:, 0:lanes].astype(BF)
    kv_ref[1] = (kv[:, lanes:] + row_of(vec_ref, BIAS_V)).astype(BF)
    q = ((nn(x_all[0:rows, :], wq[...]) + row_of(vec_ref, BIAS_Q)) * (HD**-0.5)).astype(BF)
    q_ref[...] = q
    low = low_lanes(rows)
    weight = jnp.abs(q.astype(F32)) * jnp.max(jnp.abs(kv_ref[0].astype(F32)), axis=0, keepdims=True)
    left = jnp.sum(jnp.where(low, weight, 0.0), axis=-1, keepdims=True)
    right = jnp.sum(jnp.where(low, 0.0, weight), axis=-1, keepdims=True)
    small = jnp.max(jnp.maximum(left, right)) < SAFE

    def put(o, r0, r1):
        o_ref[...] = o
        att_ref[...] = o.astype(BF)
        r_ref[...] = jnp.where(
            low, jnp.broadcast_to(r0, (rows, lanes)), jnp.broadcast_to(r1, (rows, lanes))
        )

    @pl.when(small)
    def _():
        zero = jnp.zeros_like(q)
        k, v = kv_ref[0], kv_ref[1]
        e0, o0, r0 = plain_block(jnp.where(low, q, zero), k, v)
        e_ref[0] = e0
        e1, o1, r1 = plain_block(jnp.where(low, zero, q), k, v)
        e_ref[1] = e1
        put(jnp.where(low, o0, o1), r0, r1)

    @pl.when(jnp.logical_not(small))
    def _():
        qs[...] = stack_heads(q)
        part = 32

        def body(i, carry):
            at = pl.ds(pl.multiple_of(i * part, part), part)
            e, o, rinv = softmax_block(qs[at, :], kv_ref[0], kv_ref[1])
            side = i // (rows // part)
            e_ref[side, pl.ds(pl.multiple_of((i - side * (rows // part)) * part, part), part), :] = e
            os[at, :] = o
            rs[at, :] = rinv
            return carry

        lax.fori_loop(0, 2 * rows // part, body, 0)
        put(jnp.where(low, os[0:rows, :], os[rows:, :]), rs[0:rows, :], rs[rows:, :])


def attn_fwd_call(ns, w, vecs):
    rows, width = ns[0].shape
    nt = len(ns)
    toks = nt * rows
    blk = 2 * HD
    pairs = width // blk
    row = pl.BlockSpec((rows, blk), lambda j: (0, j))
    shape = jax.ShapeDtypeStruct
    return pl.pallas_call(
        functools.partial(attn_fwd_kernel, nt),
        grid=(pairs,),
        in_specs=[full((rows, width))] * nt
        + [pl.BlockSpec((width, blk), lambda j, p=p: (0, p * pairs + j)) for p in range(3)]
        + [pl.BlockSpec((8, blk), lambda j: (0, j))],
        out_specs=[row] * 4
        + [pl.BlockSpec((2, toks, blk), lambda j: (0, 0, j))]
        + [pl.BlockSpec((2, rows, toks), lambda j: (j, 0, 0))],
        out_shape=(
            shape((rows, width), BF),
            shape((rows, width), F32),
            shape((rows, width), F32),
            shape((rows, width), BF),
            shape((2, toks, width), BF),
            shape((width // HD, rows, toks), BF),
        ),
        scratch_shapes=[
            pltpu.VMEM((toks, width), BF),
            pltpu.VMEM((width, 2 * blk), BF),
            pltpu.VMEM((2 * rows, blk), BF),
            pltpu.VMEM((2 * rows, blk), F32),
            pltpu.VMEM((2 * rows, 1), F32),
        ],
        compiler_params=params(),
        cost_estimate=cost(16 * rows * toks * width, 20 << 20, 0.01),
        name="attn_fwd",
    )(*ns, w, w, w, vecs)


def attn_bwd_kernel(ga_ref, q_ref, kv_ref, o_ref, r_ref, e_ref, gq_ref, gkv_ref):
    rows = q_ref.shape[0]
    low = low_lanes(rows)
    stack = stack_heads
    g = ga_ref[...].astype(F32) * r_ref[...]
    inner = jnp.sum(stack(g * o_ref[...]), axis=-1, keepdims=True)
    gs, qs = stack(g.astype(BF)), stack(q_ref[...])
    e = e_ref[...].reshape(2 * rows, e_ref.shape[2])
    dp = nt_dot(gs, kv_ref[1])
    ds = (e.astype(F32) * (dp - inner)).astype(BF)
    dq = nn(ds, kv_ref[0])
    gq_ref[...] = (jnp.where(low, dq[:rows], dq[rows:]) * (HD**-0.5)).astype(BF)
    gkv_ref[0] = tn_dot(ds, qs).astype(BF)
    gkv_ref[1] = tn_dot(e, gs).astype(BF)


def attn_bwd_call(ga, q, kv, o, r, e):
    rows, width = q.shape
    toks = e.shape[2]
    blk = 2 * HD
    row = pl.BlockSpec((rows, blk), lambda j: (0, j))
    both = pl.BlockSpec((2, toks, blk), lambda j: (0, 0, j))
    return pl.pallas_call(
        attn_bwd_kernel,
        grid=(width // blk,),
        in_specs=[row, row, both, row, row, pl.BlockSpec((2, rows, toks), lambda j: (j, 0, 0))],
        out_specs=[row, both],
        out_shape=[
            jax.ShapeDtypeStruct((rows, width), BF),
            jax.ShapeDtypeStruct((2, toks, width), BF),
        ],
        compiler_params=params(),
        cost_estimate=cost(32 * rows * toks * width, 24 << 20),
        name="attn_bwd",
    )(ga, q, kv, o, r, e)


def put_pieces(me_ref, src, keep_ref, send_ref, index):
    nt, nf = keep_ref.shape[0], keep_ref.shape[1]
    for k in range(nt):
        for f in range(nf):
            at = (f * nt + (me_ref[1] ^ k)) * 2
            keep_ref[(k, f) + index] = src[at + me_ref[2]]
            send_ref[(k, f) + index] = src[at + 1 - me_ref[2]]


def spread_over(n, vec, lanes):
    size = vec.shape[1]
    scale = -(-(1 << 21) // n)
    assert all((i * scale) >> 21 == i // n for i in range(size))
    dev = size // n
    col = lax.broadcasted_iota(jnp.int32, (dev, size), 1)
    mine = ((col * scale) >> 21) == lax.broadcasted_iota(jnp.int32, (dev, size), 0)
    left = jnp.where(mine, jnp.broadcast_to(vec, (dev, size)), 0.0).astype(BF)
    row = lax.broadcasted_iota(jnp.int32, (size, lanes), 0)
    place = row - ((row * scale) >> 21) * n
    hit = place == lax.broadcasted_iota(jnp.int32, (size, lanes), 1)
    return nn(left, jnp.where(hit, 1.0, 0.0).astype(BF))


def dx_kernel(gq_ref, gkv_ref, n0, n1, n2, n3, w_ref, own, *refs):
    *others, vec_ref, total, n_all = refs
    width = w_ref.shape[0]
    step = pl.program_id(0)
    e = nt_dot(gkv_ref[0], w_ref[:, width : 2 * width])
    total[...] = e + nt_dot(gkv_ref[1], w_ref[:, 2 * width :])

    @pl.when(step == 0)
    def _():
        total[...] += nt_dot(gq_ref[...], w_ref[:, 0:width])
        own[...] = total[...]
        vec_ref[...] = jnp.zeros_like(vec_ref)

    for c, n in enumerate((n0, n1, n2, n3)):

        @pl.when(step == c)
        def _():
            n_all[...] = n[...]

    vec_ref[0:1, :] += colsum(total[...] * n_all[...].astype(F32))
    vec_ref[1:2, :] += colsum(total[...])
    for c, out in enumerate(others):

        @pl.when(step == c + 1)
        def _():
            out[...] = total[...].astype(BF)


def dx_call(gq, gkv, ns, w):
    rows, width = gq.shape
    shape = jax.ShapeDtypeStruct
    return pl.pallas_call(
        dx_kernel,
        grid=(4,),
        in_specs=[full(gq.shape), pl.BlockSpec((2, rows, width), lambda j: (0, j, 0))]
        + [full((rows, width))] * 4
        + [full(w.shape)],
        out_specs=[full((rows, width))] * 4 + [full((2, width))],
        out_shape=[shape((rows, width), F32)]
        + [shape((rows, width), BF)] * 3
        + [shape((2, width), F32)],
        scratch_shapes=[pltpu.VMEM((rows, width), F32), pltpu.VMEM((rows, width), BF)],
        compiler_params=params(),
        cost_estimate=cost(16 * rows * width * width, 12 << 20),
        name="dx",
    )(gq, gkv, *ns, w)


def mid_kernel(nf, nt, fast, me_ref, *refs):
    refs = list(refs)
    if fast:
        *refs, down, up, side, sems = refs
    xms, cms, refs = refs[:nf], refs[nf : 2 * nf], refs[2 * nf :]
    att_ref, att5_ref, x5_ref, c5_ref, wo_ref, vec_in = refs[:6]
    wu_ref, wd_ref, outs_ref, out5_ref, gm_ref, ga_ref, ga5_ref = refs[6:13]
    *grads, vec_ref, gbu_ref, att, cot, mid, hat, rst, two, acc, gn2 = refs[13:]
    step = pl.program_id(0)
    r5, width = x5_ref.shape
    rm = nf * r5
    half = r5 // 2
    low = low_lanes(half)
    pairs = width // (2 * HD)

    @pl.when(step == 0)
    def _():
        att[0:rm, :] = att_ref[...]
        for pair in range(pairs):
            lanes = slice(pair * 2 * HD, (pair + 1) * 2 * HD)
            even = att5_ref[slot_of(2 * pair, nf, nt)].astype(F32)
            odd = att5_ref[slot_of(2 * pair + 1, nf, nt)].astype(F32)
            top = jnp.where(low, even, swap_halves(odd))
            bot = jnp.where(low, swap_halves(even), odd)
            att[rm : rm + r5, lanes] = jnp.concatenate([top, bot], axis=0).astype(BF)
        for k in range(nf):
            cot[k * r5 : (k + 1) * r5, :] = cms[k][...]
        cot[rm : rm + r5, :] = c5_ref[...]
        mid[...] = nn(att[...], wo_ref[...]) + row_of(vec_in, BIAS_OUT)
        for k in range(nf):
            mid[k * r5 : (k + 1) * r5, :] += xms[k][...].astype(F32)
        mid[rm : rm + r5, :] += x5_ref[...].astype(F32)
        n, rstd = normalize(mid[...])
        hat[...] = n
        rst[...] = rstd
        two[...] = (n * row_of(vec_in, GAIN2) + row_of(vec_in, SHIFT2)).astype(BF)
        acc[...] = mid[...] + row_of(vec_in, BIAS_DOWN)
        gn2[...] = jnp.zeros_like(gn2)

    pre = nn(two[...], wu_ref[...]) + vec_in[pl.ds(BIAS_UP + step, 1), :]
    cdf = 0.5 * (1.0 + lax.erf(pre * (0.5**0.5)))
    slope = cdf + pre * (jnp.exp(-0.5 * pre * pre) * 0.3989422804014327)
    act = (pre * cdf).astype(BF)
    acc[...] += nn(act, wd_ref[...])
    dwd = tn_dot(act, cot[...]).astype(BF)
    if fast:
        pd, pu = down.shape[2], up.shape[2]
        owners = down.shape[1]

        def copies(j):
            to_down = grads[0].at[:, j, pl.ds(0, pd), :]
            return [pltpu.make_async_copy(down.at[j], to_down, sems.at[0, j])] + [
                pltpu.make_async_copy(
                    up.at[j, pl.ds(f * owners, owners)],
                    grads[0].at[:, f, pl.ds(pd + j * pu, pu), :],
                    sems.at[1 + f, j],
                )
                for f in range(nf)
            ]

        down[step] = dwd.reshape(down.shape[1:])
    else:
        grads[0][...] = dwd
    gpre = (nt_dot(cot[...], wd_ref[...]) * slope).astype(BF)
    gbu_ref[...] = colsum(gpre.astype(F32))
    dwu = tn_dot(two[...], gpre)
    if fast:
        up[step] = dwu.reshape(up.shape[1:]).astype(BF)
        for copy in copies(step):
            copy.start()
    else:
        grads[1][...] = dwu.astype(BF)
    gn2[...] += nt_dot(gpre, wu_ref[...])

    @pl.when(step == pl.num_programs(0) - 1)
    def _():
        for k in range(nf):
            outs_ref[me_ref[0] ^ k] = acc[k * r5 : (k + 1) * r5, :].astype(BF)
        out5_ref[...] = acc[rm : rm + r5, :]
        e = gn2[...]
        n = hat[...]
        c = cot[...].astype(F32)
        gmid = c + norm_back(e, n, rst[...], row_of(vec_in, GAIN2))
        gm_ref[...] = gmid
        branch = gmid.astype(BF)
        vec_ref[0:1, :] = colsum(branch.astype(F32))
        vec_ref[1:2, :] = colsum(e * n)
        vec_ref[2:3, :] = colsum(e)
        vec_ref[3:4, :] = colsum(c)
        dwo = tn_dot(att[...], branch)
        if fast:
            side[...] = dwo.reshape(side.shape).astype(BF)
            put_pieces(me_ref, side, grads[1], grads[2], ())
        else:
            grads[2][...] = dwo.astype(BF)
        gatt = nt_dot(branch, wo_ref[...])
        ga_ref[...] = gatt[0:rm].astype(BF)
        ga5_ref[...] = jnp.zeros_like(ga5_ref)
        for pair in range(pairs):
            lanes = slice(pair * 2 * HD, (pair + 1) * 2 * HD)
            top, bot = gatt[rm : rm + half, lanes], gatt[rm + half : rm + r5, lanes]
            even = jnp.where(low, top, swap_halves(bot))
            odd = jnp.where(low, swap_halves(top), bot)
            ga5_ref[slot_of(2 * pair, nf, nt)] = even.astype(BF)
            ga5_ref[slot_of(2 * pair + 1, nf, nt)] = odd.astype(BF)
        if fast:
            for j in range(nf):
                for copy in copies(j):
                    copy.wait()


def mid_call(nf, nt, fast, me, xms, cms, att, att5, x5, c5, wo, vecs, wu, wd):
    _, r5, width = x5.shape
    rm = nf * r5
    rows = rm + r5
    ff = wu.shape[1]
    blk = ff // nf
    shape = jax.ShapeDtypeStruct
    if fast:
        dev = nf * nt * 2
        pd, pu = ff // dev, width // dev
        oshape = (nt, nf, pu, width)
        gspecs = [pl.BlockSpec(memory_space=pl.ANY)] + [full(oshape)] * 2
        gshapes = [shape((nt * 2, nf, pd + nf * pu, width), BF)] + [shape(oshape, BF)] * 2
        extra = [
            pltpu.VMEM((nf, nt * 2, pd, width), BF),
            pltpu.VMEM((nf, dev, pu, width), BF),
            pltpu.VMEM((dev, pu, width), BF),
            pltpu.SemaphoreType.DMA((1 + nf, nf)),
        ]
    else:
        gspecs = [
            pl.BlockSpec((blk, width), lambda j, *_: (j, 0)),
            pl.BlockSpec((width, blk), lambda j, *_: (0, j)),
            full((width, width)),
        ]
        gshapes = [shape((ff, width), BF), shape((width, ff), BF), shape((width, width), BF)]
        extra = []
    ins = [*xms, *cms, att, att5, x5, c5, wo, vecs]
    return pl.pallas_call(
        functools.partial(mid_kernel, nf, nt, fast),
        grid_spec=pltpu.PrefetchScalarGridSpec(
            num_scalar_prefetch=1,
            grid=(nf,),
            in_specs=[clip_at(x, nf) if x.ndim == 3 and x.shape[0] == nf + 1 else full(x.shape) for x in ins]
            + [
                pl.BlockSpec((width, blk), lambda j, *_: (0, j)),
                pl.BlockSpec((blk, width), lambda j, *_: (j, 0)),
            ],
            out_specs=[
                full((nf, r5, width)),
                full((r5, width)),
                full((rows, width)),
                full((rm, width)),
                full(att5.shape),
            ]
            + gspecs
            + [full((4, width)), pl.BlockSpec((1, blk), lambda j, *_: (0, j))],
            scratch_shapes=[
                pltpu.VMEM((rows, width), BF),
                pltpu.VMEM((rows, width), BF),
                pltpu.VMEM((rows, width), F32),
                pltpu.VMEM((rows, width), F32),
                pltpu.VMEM((rows, 1), F32),
                pltpu.VMEM((rows, width), BF),
                pltpu.VMEM((rows, width), F32),
                pltpu.VMEM((rows, width), F32),
            ]
            + extra,
        ),
        out_shape=[
            shape((nf, r5, width), BF),
            shape((r5, width), F32),
            shape((rows, width), F32),
            shape((rm, width), BF),
            shape(att5.shape, BF),
        ]
        + gshapes
        + [shape((4, width), F32), shape((1, ff), F32)],
        compiler_params=params(),
        cost_estimate=cost(12 * rows * width * ff + 6 * rows * width * width, 24 << 20),
        name="mid",
    )(me, *ins, wu, wd)


def tail5_kernel(nf, nt, fast, *refs):
    refs = list(refs)
    if fast:
        me_ref = refs.pop(0)
        *refs, side, small = refs
    (gq_ref, gkv_ref), ns, refs = refs[:2], refs[2 : 2 + nt], refs[2 + nt :]
    g_ref, n5_ref, x5_ref, gm_ref, w_ref, in_ref, vm_ref, v2_ref, gbu_ref = refs[:9]
    (*dwo, gin_ref, vec_ref, dx, x_all, g_all, sums) = refs[9:]
    step = pl.program_id(0)
    r5, width = x5_ref.shape
    half = r5 // 2
    low = low_lanes(half)
    rows = ns[0].shape[0]

    @pl.when(step == 0)
    def _():
        x_all[0:r5, :] = n5_ref[...]
        for c in range(nt):
            x_all[r5 + c * rows : r5 + (c + 1) * rows, :] = ns[c][...]
        dx[...] = jnp.zeros_like(dx)

    for pair in range(width // (2 * HD)):
        lanes = slice(pair * 2 * HD, (pair + 1) * 2 * HD)
        even = g_ref[slot_of(2 * pair, nf, nt)].astype(F32)
        odd = g_ref[slot_of(2 * pair + 1, nf, nt)].astype(F32)
        top = jnp.where(low, even, swap_halves(odd))
        bot = jnp.where(low, swap_halves(even), odd)
        g_all[0:r5, lanes] = jnp.concatenate([top, bot], axis=0).astype(BF)
    dx[...] += nt_dot(g_all[0:r5, :], w_ref[...])

    def finish(end):
        g = g_all[0:end, :]
        sums[pl.ds(step, 1), :] = colsum(g.astype(F32))
        dw = tn_dot(x_all[0:end, :], g)
        if fast:
            side[...] = dw.reshape(side.shape).astype(BF)
        else:
            dwo[0][...] = dw.astype(BF)

    @pl.when(step < 2)
    def _():
        g_all[r5:, :] = gkv_ref[0]
        finish(r5 + nt * rows)

    @pl.when(step == 2)
    def _():
        g_all[r5 : r5 + rows, :] = gq_ref[...]
        finish(r5 + rows)
        n, rstd = normalize(x5_ref[...].astype(F32))
        e = dx[...]
        gin_ref[...] = gm_ref[...] + norm_back(e, n, rstd, row_of(in_ref, GAIN1))
        main = vm_ref[0:1, :] - row_of(in_ref, SHIFT1) * vm_ref[1:2, :]
        vec_ref[0:1, :] = main / row_of(in_ref, GAIN1) + colsum(e * n)
        vec_ref[1:2, :] = vm_ref[1:2, :] + colsum(e)
        vec_ref[2:6, :] = v2_ref[...]
        vec_ref[6:7, :] = sums[2:3, :]
        vec_ref[7:8, :] = sums[1:2, :]
        if fast:
            per = width // small.shape[0]
            lanes = width // 4
            total = 0.0
            for i in range(8):
                part = spread_over(per, vec_ref[i : i + 1, :], 2 * HD)
                part = jnp.concatenate([part, jnp.zeros((part.shape[0], lanes - 2 * HD), F32)], 1)
                total += pltpu.roll(part, i * per, 1) if i else part
            wide = spread_over(gbu_ref.shape[1] // small.shape[0], gbu_ref[...], 2 * HD)
            rest = width - lanes - 2 * HD
            line = jnp.concatenate([total, wide, jnp.zeros((wide.shape[0], rest), F32)], 1)
            small[...] = jnp.broadcast_to(line[:, None, :], small.shape).astype(BF)
            keep, send = (x.at[:, :, side.shape[1] :, :] for x in dwo[0:2])
            put_pieces(me_ref, small, keep, send, ())

    if fast:
        for i in range(3):

            @pl.when(step == (i + 2) % 3)
            def _():
                keep, send = (x.at[:, :, 0 : side.shape[1], :] for x in dwo[2 * i : 2 * i + 2])
                put_pieces(me_ref, side, keep, send, ())


def tail5_call(nf, nt, fast, me, gq, gkv, ns, g, n5, x5, gm, w, vecs, vm, v2, gbu):
    _, r5, width = x5.shape
    at = gm.shape[0] // r5 - 1
    toks = gkv.shape[1]
    part = lambda j: (j + 1) % 3
    bshape = jax.ShapeDtypeStruct
    if fast:
        pu = width // (nf * nt * 2)
        heights = (pu + 8,) * 2 + (pu,) * 4
        wspecs = [full((nt, nf, n, width)) for n in heights]
        wshapes = [bshape((nt, nf, n, width), BF) for n in heights]
        extra = [pltpu.VMEM((nf * nt * 2, n, width), BF) for n in (pu, 8)]
    else:
        wspecs = [pl.BlockSpec((width, width), lambda j, *_: (0, part(j)))]
        wshapes = [bshape((width, 3 * width), BF)]
        extra = []
    return pl.pallas_call(
        functools.partial(tail5_kernel, nf, nt, fast),
        grid_spec=pltpu.PrefetchScalarGridSpec(
            num_scalar_prefetch=int(fast),
            grid=(3,),
            in_specs=[full(gq.shape)]
            + [pl.BlockSpec((1, toks, width), lambda j, *_: (jnp.minimum(j, 1), 0, 0))]
            + [full(x.shape) for x in ns]
            + [
                pl.BlockSpec((g.shape[0], r5 // 2, 2 * HD), lambda j, *_: (0, 0, part(j))),
                full(n5.shape),
                clip_at(x5, nf),
                pl.BlockSpec((r5, width), lambda j, *_: (at, 0)),
                pl.BlockSpec((width, width), lambda j, *_: (0, part(j))),
            ]
            + [full(x.shape) for x in (vecs, vm, v2, gbu)],
            out_specs=wspecs + [full((r5, width)), full((8, width))],
            scratch_shapes=[
                pltpu.VMEM((r5, width), F32),
                pltpu.VMEM((r5 + toks, width), BF),
                pltpu.VMEM((r5 + toks, width), BF),
                pltpu.VMEM((8, width), F32),
            ]
            + extra,
        ),
        out_shape=wshapes + [bshape((r5, width), F32), bshape((8, width), F32)],
        compiler_params=params(),
        cost_estimate=cost(4 * r5 * width * width * 3 + 4 * width * width * toks, 16 << 20),
        name="tail_shared",
    )(*([me] if fast else []), gq, gkv, *ns, g, n5, x5, gm, w, vecs, vm, v2, gbu)


def tail_kernel(nf, nt, *refs):
    dxs, xs, refs = refs[:nt], refs[nt : nt + nf], refs[nt + nf :]
    gm_ref, vec_ref, *gins = refs
    rows = xs[0].shape[0]
    for k in range(nf):
        at = slice(k * rows, (k + 1) * rows)
        e = dxs[0][at, :]
        for c in range(1, nt):
            e = e + dxs[c][at, :].astype(F32)
        n, rstd = normalize(xs[k][...].astype(F32))
        gins[k][...] = (gm_ref[at, :] + norm_back(e, n, rstd, row_of(vec_ref, GAIN1))).astype(BF)


def tail_call(dxs, xs, gm, vecs):
    rows, width = xs[0].shape
    nf, nt = len(xs), len(dxs)
    return pl.pallas_call(
        functools.partial(tail_kernel, nf, nt),
        grid=(1,),
        in_specs=[full((nf * rows, width))] * nt
        + [full((rows, width))] * nf
        + [full((nf * rows, width)), full(vecs.shape)],
        out_specs=[full((rows, width))] * nf,
        out_shape=[jax.ShapeDtypeStruct((rows, width), BF)] * nf,
        compiler_params=params(),
        cost_estimate=cost(30 * nf * rows * width, 6 << 20, 1000),
        name="tail",
    )(*dxs, *xs, gm, vecs)


def pair_sum_kernel(count, *refs):
    ins, (dx, d0, d2, uy, u0, u1) = refs[: 4 * count], refs[4 * count :]
    outs = ((d0, dx.at[0], d2, dx.at[1]), (u0, u1, uy.at[0], uy.at[1]))
    for side in range(2):
        pairs = ins[2 * count * side : 2 * count * (side + 1)]
        at = 0
        for keep, got in zip(pairs[0::2], pairs[1::2]):
            rows = keep.shape[2]
            for k in range(4):
                total = (keep[k, 0].astype(F32) + got[k, 0].astype(F32)).astype(BF)
                outs[side][k][0, at : at + rows, :] = total
            at += rows


def pair_sum(trios):
    _, blocks, _, width = trios[0][0].shape
    steps = blocks // 2
    rows = sum(x[0].shape[2] for x in trios)
    specs, args = [], []
    for first in (0, steps):
        for keep, got in trios:
            spec = pl.BlockSpec((4, 1) + keep.shape[2:], lambda j, f=first: (0, j + f, 0, 0))
            specs += [spec, spec]
            args += [keep, got]
    two = pl.BlockSpec((2, 1, rows, width), lambda j: (0, j, 0, 0))
    one = pl.BlockSpec((1, rows, width), lambda j: (j, 0, 0))
    shape = jax.ShapeDtypeStruct
    return pl.pallas_call(
        functools.partial(pair_sum_kernel, len(trios)),
        grid=(steps,),
        in_specs=specs,
        out_specs=[two, one, one] * 2,
        out_shape=[
            shape((2, steps, rows, width), BF),
            shape((steps, rows, width), BF),
            shape((steps, rows, width), BF),
        ]
        * 2,
        compiler_params=params(),
        cost_estimate=cost(1 << 20, 8 << 20),
        name="pair_sum",
    )(*args)


def relay_sum_kernel(d2, gx, u1, gy, sd, su):
    sd[...] = (d2[...].astype(F32) + gx[0].astype(F32)).astype(BF)
    su[...] = (u1[...].astype(F32) + gy[0].astype(F32)).astype(BF)


def relay_sum(d2, gx, u1, gy):
    second = lambda x: pl.BlockSpec((1,) + x.shape[1:], lambda *_: (1,) + (0,) * (x.ndim - 1))
    return pl.pallas_call(
        relay_sum_kernel,
        grid=(1,),
        in_specs=[full(d2.shape), second(gx), full(u1.shape), second(gy)],
        out_specs=[full(d2.shape), full(u1.shape)],
        out_shape=[jax.ShapeDtypeStruct(d2.shape, BF), jax.ShapeDtypeStruct(u1.shape, BF)],
        compiler_params=params(),
        cost_estimate=cost(d2.size, 6 * d2.size, 1),
        name="relay_sum",
    )(d2, gx, u1, gy)


def along(axis, k, x):
    return lax.ppermute(x, axis, [(i, i ^ k) for i in range(4)])


def relay_start(dx, uy):
    return along("tm", 1, dx), along("tm", 2, uy)


def relay_end(gx, gy, d2, u1):
    sd, su = relay_sum(d2, gx, u1, gy)
    return along("tm", 2, sd), along("tm", 1, su)


def tm_sum_kernel(nf, lead, me_ref, *refs):
    d0, gx, rd, u0, gy, ru = refs[:6]
    outs, total = refs[6 : 6 + nf], refs[-1]
    half = d0.shape[0]
    for first, own, one, two in ((0, d0, gx, rd), (half, u0, gy, ru)):
        for f in range(half):
            part = own[f].astype(F32) + one[0, f, lead:, :].astype(F32) + two[f, lead:, :].astype(F32)
            total[first + f] = part.astype(BF)
    for k in range(nf):
        outs[k][...] = total[me_ref[0] ^ k]


def tm_sum(nf, me, d0, gx, rd, u0, gy, ru):
    _, rows, width = d0.shape
    first = full((1,) + gx.shape[1:])
    return pl.pallas_call(
        functools.partial(tm_sum_kernel, nf, gx.shape[2] - rows),
        grid_spec=pltpu.PrefetchScalarGridSpec(
            num_scalar_prefetch=1,
            grid=(1,),
            in_specs=[full(d0.shape), first, full(rd.shape)] * 2,
            out_specs=[full((rows, width))] * nf,
            scratch_shapes=[pltpu.VMEM((nf, rows, width), BF)],
        ),
        out_shape=[jax.ShapeDtypeStruct((rows, width), BF)] * nf,
        compiler_params=params(),
        cost_estimate=cost(1 << 20, 5 << 20),
        name="tm_sum",
    )(me, d0, gx, rd, u0, gy, ru)


def last_sum_kernel(nf, places, first_vec, per, *refs):
    parts, stacked, outs = refs[:nf], refs[nf], refs[nf + 1 :]
    for at, rows, out, col, source in places:
        if source:
            parts = [stacked.at[i] for i in range(stacked.shape[0])]
        lanes = parts[0].shape[1]
        total = parts[0][at : at + rows, :].astype(F32)
        for part in parts[1:]:
            total = total + part[at : at + rows, :].astype(F32)
        if out is None:
            for i in range(8):
                outs[first_vec + i][...] = (pltpu.roll(total, lanes - i * per, 1) if i else total)[0, 0:per]
            outs[first_vec + 8][...] = total[0, lanes // 4 : lanes // 4 + outs[first_vec + 8].shape[0]]
        else:
            outs[out][:, col : col + lanes] = total


def last_sum(parts, stacked, places, shapes, first_vec, per):
    nf = len(parts)
    return pl.pallas_call(
        functools.partial(last_sum_kernel, nf, places, first_vec, per),
        out_shape=[jax.ShapeDtypeStruct(x, F32) for x in shapes],
        compiler_params=pltpu.CompilerParams(vmem_limit_bytes=VMEM_LIMIT),
        cost_estimate=cost(nf * parts[0].size, 2 * nf * parts[0].size, 1),
        name="last_sum",
    )(*parts, stacked)


def swap_cores(x):
    return lax.ppermute(x, "grp", [(0, 1), (1, 0)])


def exchange(axis, parts):
    pairs = lambda k: [(i, i ^ k) for i in range(len(parts))]
    return [parts[0]] + [lax.ppermute(parts[k], axis, pairs(k)) for k in range(1, len(parts))]


def tie(x, *deps):
    flat, tree = jax.tree.flatten(x)
    tied = lax.optimization_barrier((flat, deps))[0]
    return jax.tree.unflatten(tree, tied)


def over(axes, x):
    return lax.all_to_all(x, axes, 0, 0)


def local(
    nf,
    nt,
    ng,
    inputs,
    gain_one,
    shift_one,
    w_qkv,
    bias_query,
    bias_value,
    w_out,
    bias_out,
    gain_two,
    shift_two,
    w_up,
    bias_up,
    w_down,
    bias_down,
    cotangent,
):
    _, r, width = inputs.shape
    ff = w_up.shape[1]
    dev = nf * nt * ng
    per = width // dev
    fast = ng == 2 and per % 8 == 0 and ff // nf == width
    me = jnp.stack([lax.axis_index(a) for a in ALL]).astype(jnp.int32)
    both = ("freq", "tm")
    got = pick_call(
        nf,
        me,
        inputs,
        cotangent,
        (gain_one, shift_one, bias_query, bias_value, bias_out, gain_two, shift_two, bias_down, bias_up),
    )
    picked, vecs, cs = got[:nf], got[nf], got[nf + 1 :]
    xs = exchange("freq", picked)
    n5, pack5 = q5_call(nf, nt, tie(inputs, picked[0]), vecs, w_qkv)
    got5 = over(both, pack5).reshape(-1, 6 * HD)
    nm = ln_call(tie(xs, pack5), vecs)
    ns = exchange("tm", [nm] * nt)
    o5, r5, ob5, e5 = attn5_fwd_call(got5)
    att5 = over(both, ob5.reshape(nf * nt, r // 2, 2 * HD))
    cs = exchange("freq", tie(cs, ob5))
    att, o, rr, q, kv, e = attn_fwd_call(tie(ns, ob5), w_qkv, vecs)
    outs, out5, gm, ga, ga5, *dws, vec, gbu = mid_call(
        nf,
        nt,
        fast,
        me,
        xs,
        cs,
        att,
        att5,
        inputs,
        cotangent,
        w_out,
        vecs,
        w_up,
        w_down,
    )
    pieces = lambda x: x.reshape(nt, nf, -1, width)
    pd = ff // dev
    if fast:
        dff = lax.psum_scatter(
            dws[0].reshape(nt * ng, nf * (pd + nf * per), width),
            ("tm", "grp"),
            scatter_dimension=0,
            tiled=True,
        )
        keep_o, got_o = pieces(dws[1]), pieces(swap_cores(dws[2]))
    got_ga5 = over(both, ga5).reshape(-1, 2 * HD)
    gq, gkv = attn_bwd_call(ga, q, kv, o, rr, e)
    g5 = attn5_bwd_call(got5, tie(got_ga5, gq, *([got_o] if fast else [])), o5, r5, e5).reshape(nf * nt, r // 2, 6 * HD)
    *dxs, vec_m = dx_call(tie(gq, g5), gkv, ns, w_qkv)
    dxs = exchange("tm", dxs)
    g5 = over(both, g5)
    *dwqkv, gin5, vec8 = tail5_call(
        nf, nt, fast, me, tie(gq, vec_m), gkv, ns, g5, n5, inputs, gm, w_qkv, vecs, vec_m, vec, gbu
    )
    outs = over("freq", tie(outs, g5))
    gin = tail_call(tie(dxs, vec8), xs, gm, vecs)
    order = gin[0]
    gin = exchange("freq", gin)
    if fast:
        trios = [(dwqkv[i], swap_cores(dwqkv[i + 1])) for i in (0, 2, 4)]
        trios += [(keep_o, got_o)]
        trios[0] = (trios[0][0], tie(trios[0][1], order))
        dxq, d0q, d2q, uyq, u0q, u1q = pair_sum(trios)
        gxq, gyq = relay_start(dxq, uyq)
        sdq, suq = relay_sum(d2q, gxq, u1q, gyq)
        rdq, ruq = along("tm", 2, sdq), along("tm", 1, suq)
        dff = over("freq", tie(dff, dxq).reshape(nf, -1, width))
        sums_q = exchange("freq", tm_sum(nf, me, d0q, gxq, rdq, u0q, gyq, ruq))
        places = [(0, per, 0, 0, 0), (per, 8, None, 0, 0), (per + 8, per, 0, width, 0)]
        places += [(2 * per + 8, per, 0, 2 * width, 0), (3 * per + 8, per, 1, 0, 0)]
        places += [(0, pd, 2, 0, 1)] + [(pd + i * per, per, 3, i * width, 1) for i in range(nf)]
        shapes = [(per, 3 * width), (per, width), (pd, width), (per, ff)] + [(per,)] * 8 + [(pd,)]
        dwqkv, dwo, dwd, dwu, *small, gbu = last_sum(sums_q, dff, places, shapes, 4, per)
        piece = lambda i: small[i]
    else:
        dwd, dwu, dwo, dwqkv = (
            lax.psum_scatter(x, ALL, scatter_dimension=0, tiled=True).astype(F32)
            for x in dws + dwqkv
        )
        small = vec8.reshape(8, dev, per).transpose(1, 0, 2).reshape(dev, -1)
        small = jnp.concatenate([small, gbu.reshape(dev, pd)], axis=1)
        small = jnp.sum(over(ALL, small), axis=0)
        piece = lambda i: small[i * per : (i + 1) * per]
        gbu = small[8 * per :]
    block_out = jnp.concatenate([outs.astype(F32), out5[None]], axis=0)
    grad_in = assemble_call(nf, me, gin, gin5)
    return (
        block_out,
        grad_in,
        piece(0),
        piece(1),
        dwqkv,
        piece(6),
        piece(7),
        dwo,
        piece(2),
        piece(3),
        piece(4),
        dwu,
        gbu,
        dwd,
        piece(5),
    )


def solution(mesh):
    tokens = P("grp", ("freq", "tm"), None)
    vec = P(ALL)
    mat = P(ALL, None)
    return jax.shard_map(
        functools.partial(local, mesh.shape["freq"], mesh.shape["tm"], mesh.shape["grp"]),
        mesh=mesh,
        in_specs=(tokens,) + (P(),) * 13 + (tokens,),
        out_specs=(
            tokens,
            tokens,
            vec,
            vec,
            mat,
            vec,
            vec,
            mat,
            vec,
            vec,
            vec,
            mat,
            vec,
            mat,
            vec,
        ),
        check_vma=False,
    )
```
